256 devices in a mesh: blk: 16 (over x_lo, y, core), rows: 16 (over x_hi, z).
Axes of the slice: x: 4 (x_hi: 2, x_lo: 2; x = x_hi * 2 + x_lo), y: 4, z: 8, core: 2. Of those that a mesh axis runs over, the one named last changes fastest.
Arguments:
- excitations: float32 [64, 131072], P(None, ('blk', 'rows')), may hold values from -6 to 6
- adjoint_loads: float32 [64, 131072], P(None, ('blk', 'rows')), may hold values from -6 to 6
- near_tiles: bfloat16 [8192, 256, 256], P(('blk', 'rows')), may hold values from -0.125 to 0.125
- tile_rows: int32 [8192], P(('blk', 'rows')), may hold values from 0 to 1
- tile_cols: int32 [8192], P(('blk', 'rows')), may hold values from 0 to 31
- tile_count: int32 [256], P(('blk', 'rows')), may hold values from 4 to 32, as said below
- skeleton_in: bfloat16 [1024, 131072], P(None, ('blk', 'rows')), may hold values from -0.0625 to 0.0625
- skeleton_out: bfloat16 [1024, 131072], P(None, ('blk', 'rows')), may hold values from -0.1875 to 0.1875
- translation: float32 [16, 15, 1024, 1024], P('blk', None, 'rows'), may hold values from -0.046875 to 0.046875
Outputs:
- response: float32 [64, 131072], P(None, ('blk', 'rows'))
- sensitivity: float32 [64, 131072], P(None, ('blk', 'rows'))
The draws below stay inside these ranges and needn't reach their ends.
Inputs may be any that keep to these rules, and one draw needn't show every extreme that they name: `tile_count`: slots of a device are used from slot 0 on; later slots are no part of the operator.
All inputs are finite; a program needn't handle non-finite values.
Results may differ from the reference program's by a relative error of at most 0.0036.
Values may be sent and summed in bfloat16 or wider, within the bound.
No kernel may reach another device: no remote copies, remote signals or barrier semaphores. Data moves between devices by JAX's collectives and lax.ppermute only.
A program may use at most 128 MiB of HBM per device.

```python
import jax
import jax.numpy as jnp
from jax import lax

E = 64
S = 1024
TB = 256
TPB = 16
P_DEV = 512
CLUSTER = 8192
CLUSTERS = 16
PANELS = 131072
RB = 2
CBLK = 32
CAP = 32
N_BLK = 16
N_ROWS = 16
DEVICES = 256


def draw_tile_count(key, part):
    first_draw = jax.random.randint(jax.random.fold_in(key, 11), (DEVICES,), CAP // 8, CAP + 1)
    second_draw = jax.random.randint(jax.random.fold_in(key, 12), (DEVICES,), CAP // 8, CAP + 1)
    counts = jnp.minimum(first_draw, second_draw)
    busiest = jax.random.randint(jax.random.fold_in(key, 13), (), 0, DEVICES)
    return counts.at[busiest].set(CAP).astype(jnp.int32)


def plant(entries, key, least, top_value):
    extent = entries.shape
    place = [jax.random.randint(jax.random.fold_in(key, axis), (), 0, extent[axis]) for axis in range(len(extent))]
    entries = entries.at[tuple(place)].set(least)
    longest = extent.index(max(extent))
    place[longest] = (place[longest] + 1) % extent[longest]
    return entries.at[tuple(place)].set(top_value)


def shard_levels(key, shape, split, smallest, high):
    factor_of, own = 1.0, jax.random.fold_in(key, 6)
    for position, parts in split:
        heights = jnp.exp(jax.random.uniform(jax.random.fold_in(own, position), (parts,), jnp.float32, smallest / len(split), high / len(split)))
        factor_of = factor_of * jnp.repeat(heights, shape[position] // parts).reshape([-1 if axis == position else 1 for axis in range(len(shape))])
    return factor_of


def normal_values(stream_key, dims, deviation, bound, pieces=(), kind=jnp.bfloat16):
    level = shard_levels(stream_key, dims, pieces, -0.22, 0.18) if pieces else 1.0
    entries = jax.random.normal(stream_key, dims, jnp.float32) * deviation * level
    return jnp.minimum(jnp.maximum(entries, -bound), bound).astype(kind)


def setup_inputs(seed: int = 0) -> dict:
    key_of = jax.random.split(jax.random.key(seed), 10)
    return {
        "excitations": normal_values(key_of[0], (E, PANELS), 1.0, 6.0, ((1, 256),), jnp.float32),
        "adjoint_loads": normal_values(key_of[1], (E, PANELS), 1.0, 6.0, ((1, 256),), jnp.float32),
        "near_tiles": normal_values(key_of[2], (N_BLK * N_ROWS * CAP, TB, TB), (TB * TPB // 2) ** -0.5, 0.125, ((0, 256),)),
        "tile_rows": plant(jax.random.randint(key_of[3], (N_BLK * N_ROWS * CAP,), 0, RB), jax.random.fold_in(key_of[3], 1), 0, RB - 1).astype(jnp.int32),
        "tile_cols": plant(jax.random.randint(key_of[4], (N_BLK * N_ROWS * CAP,), 0, CBLK), jax.random.fold_in(key_of[4], 1), 0, CBLK - 1).astype(jnp.int32),
        "tile_count": draw_tile_count(jax.random.fold_in(key_of[9], 71), 0),
        "skeleton_in": normal_values(key_of[6], (S, PANELS), CLUSTER ** -0.5, 0.0625, ((1, 256),)),
        "skeleton_out": normal_values(key_of[7], (S, PANELS), S ** -0.5, 0.1875, ((1, 256),)),
        "translation": normal_values(key_of[8], (N_BLK, N_BLK - 1, S, S), (S * (N_BLK - 1)) ** -0.5, 0.046875, ((0, 16), (2, 16)), jnp.float32),
    }


highest = lax.Precision.HIGHEST


def reference(excitations, adjoint_loads, near_tiles, tile_rows, tile_cols, tile_count, skeleton_in, skeleton_out, translation):
    drive_low = excitations.astype(jnp.bfloat16)
    loads_low = adjoint_loads.astype(jnp.bfloat16)
    per_cluster = CLUSTER // P_DEV

    def near_slot(slot_raw, carry):
        ahead, behind = carry
        slot = jnp.asarray(slot_raw).astype(jnp.int32)
        device = slot // CAP
        live_mask = (slot % CAP < tile_count[device]).astype(jnp.float32)
        row_start = (device * P_DEV + tile_rows[slot] * TB).astype(jnp.int32)
        col_start = ((device // per_cluster) * CLUSTER + tile_cols[slot] * TB).astype(jnp.int32)
        tile_block = near_tiles[slot]
        source = lax.dynamic_slice_in_dim(drive_low, col_start, TB, 1)
        target = lax.dynamic_slice_in_dim(loads_low, row_start, TB, 1)
        forward = lax.dot_general(source, tile_block, (((1,), (1,)), ((), ())), preferred_element_type=jnp.float32) * live_mask
        backward = jnp.dot(target, tile_block, preferred_element_type=jnp.float32) * live_mask
        ahead = lax.dynamic_update_slice_in_dim(ahead, lax.dynamic_slice_in_dim(ahead, row_start, TB, 1) + forward, row_start, 1)
        behind = lax.dynamic_update_slice_in_dim(behind, lax.dynamic_slice_in_dim(behind, col_start, TB, 1) + backward, col_start, 1)
        return ahead, behind

    blank = jnp.zeros((E, PANELS), jnp.float32)
    near_ahead, near_behind = lax.fori_loop(0, N_BLK * N_ROWS * CAP, near_slot, (blank, blank))

    cluster_ids = jnp.arange(CLUSTERS, dtype=jnp.int32)
    lag = jnp.arange(1, CLUSTERS, dtype=jnp.int32)

    def cluster_part(values, matrix, index):
        start = (index * CLUSTER).astype(jnp.int32)
        left = lax.dynamic_slice_in_dim(values, start, CLUSTER, 1)
        right = lax.dynamic_slice_in_dim(matrix, start, CLUSTER, 1)
        return lax.dot_general(left, right, (((1,), (1,)), ((), ())), preferred_element_type=jnp.float32)

    charges = lax.map(lambda index: cluster_part(drive_low, skeleton_in, index), cluster_ids)
    gradient = lax.map(lambda index: cluster_part(loads_low, skeleton_out, index), cluster_ids)

    def forward_far(index):
        sources = jnp.remainder(index - lag, CLUSTERS).astype(jnp.int32)
        potential = jnp.einsum("dej,dkj->ek", charges[sources], translation[index], precision=highest)
        potential_low = potential.astype(jnp.bfloat16)
        start = (index * CLUSTER).astype(jnp.int32)
        return jnp.dot(potential_low, lax.dynamic_slice_in_dim(skeleton_out, start, CLUSTER, 1), preferred_element_type=jnp.float32)

    def backward_far(index):
        senders = jnp.remainder(index + lag, CLUSTERS).astype(jnp.int32)
        potential = jnp.einsum("dek,dkj->ej", gradient[senders], translation[senders, lag - 1], precision=highest)
        adjoint_low = potential.astype(jnp.bfloat16)
        start = (index * CLUSTER).astype(jnp.int32)
        return jnp.dot(adjoint_low, lax.dynamic_slice_in_dim(skeleton_in, start, CLUSTER, 1), preferred_element_type=jnp.float32)

    far_ahead = jnp.transpose(lax.map(forward_far, cluster_ids), (1, 0, 2)).reshape(E, PANELS)
    far_behind = jnp.transpose(lax.map(backward_far, cluster_ids), (1, 0, 2)).reshape(E, PANELS)
    return near_ahead + far_ahead, near_behind + far_behind
```

```python
import jax
import jax.numpy as jnp
from jax import lax
from jax.experimental import pallas as pl
from jax.experimental.pallas import tpu as pltpu
from jax.sharding import Mesh
from jax.sharding import PartitionSpec as P

BLK = ("xlo", "y", "core")
ROWS = ("xhi", "z")
FACE = ("xlo", "y")
bf16 = jnp.bfloat16
f32 = jnp.float32
LAST = (((1,), (1,)), ((), ()))


def vmem():
    return pl.BlockSpec(memory_space=pltpu.VMEM)


def smem():
    return pl.BlockSpec(memory_space=pltpu.SMEM)


def call(kernel, outs, args, specs=None, scratch=(), flops=10**7, name=None):
    moved = sum(a.size * a.dtype.itemsize for a in args)
    return pl.pallas_call(
        kernel,
        out_shape=[jax.ShapeDtypeStruct(s, d) for s, d in outs],
        in_specs=specs or [vmem()] * len(args),
        out_specs=[vmem()] * len(outs),
        scratch_shapes=list(scratch),
        compiler_params=pltpu.CompilerParams(vmem_limit_bytes=40 * 2**20),
        cost_estimate=pl.CostEstimate(flops=flops, bytes_accessed=moved, transcendentals=0),
        name=name,
    )(*args)


def split(value):
    high = value.astype(bf16)
    return high, (value - high.astype(f32)).astype(bf16)


def dot(a, b):
    return jnp.dot(a, b, preferred_element_type=f32)


def dot_last(a, b):
    return lax.dot_general(a, b, LAST, preferred_element_type=f32)


def put_pieces(ref, value, lead=()):
    for piece in range(16):
        for part in range(4):
            row = piece // 2 * 8
            col = piece % 2 * 512 + part * 128
            ref[(*lead, piece, pl.ds(part * 8, 8), slice(None))] = value[row : row + 8, col : col + 128]


def join_pieces(ref, first):
    rows = []
    for band in range(8):
        blocks = [
            ref[band * 2 + half, first + part * 8 : first + part * 8 + 8, :]
            for half in range(2)
            for part in range(4)
        ]
        rows.append(jnp.concatenate(blocks, axis=1))
    return jnp.concatenate(rows, axis=0)


def prepare(exc_ref, loads_ref, skin_ref, skout_ref, drive_ref, low_ref, msg_ref):
    drive = exc_ref[...].astype(bf16)
    loads = loads_ref[...].astype(bf16)
    for part in range(2):
        drive_ref[part] = drive[:, part * 256 : part * 256 + 256]
        low_ref[part] = loads[:, part * 256 : part * 256 + 256]
    charges = dot_last(drive, skin_ref[...]).astype(bf16).astype(f32)
    twice = jnp.concatenate([loads, loads], axis=0)
    gradient = dot_last(skout_ref[...], twice)
    left = lax.broadcasted_iota(jnp.int32, (32, 128), 1) < 64
    for piece in range(16):
        row = piece // 2 * 8
        for part in range(4):
            col = piece % 2 * 512 + part * 128
            msg_ref[piece, part * 8 : part * 8 + 8, :] = charges[row : row + 8, col : col + 128].astype(bf16)
        k = piece * 64
        msg_ref[piece, 32:64, :] = jnp.where(
            left, gradient[k : k + 32], gradient[k + 32 : k + 64]
        ).astype(bf16)


def cross_core(msg_ref, trans_ref, copies_ref, grad_ref, send_ref):
    total = jnp.sum(msg_ref[...].astype(f32), axis=0)
    share = total[:32].astype(bf16)
    for piece in range(16):
        copies_ref[piece] = share
    packed = total[32:]
    gradient = jnp.concatenate([packed, pltpu.roll(packed, 64, 1)], axis=0)
    gradient = gradient.T[:64]
    grad_ref[...] = gradient
    high, low = split(gradient)
    both = jnp.concatenate([high, low], axis=0)
    cluster = lax.axis_index(BLK)
    other = 1 - lax.axis_index("core")
    for q in range(8):
        lag = lax.rem(cluster - (2 * q + other) + 16, 16)
        t_high, t_low = split(trans_ref[0, lag - 1])
        pair = dot(both, t_high)
        send_ref[q] = (pair[:64] + pair[64:] + dot(high, t_low)).astype(bf16)


def own_core(grad_ref, came_ref, trans_ref, send_ref):
    high, low = split(grad_ref[...])
    both = jnp.concatenate([high, low], axis=0)
    cluster = lax.axis_index(BLK)
    core = lax.axis_index("core")
    for q in range(8):
        lag = lax.rem(cluster - (2 * q + core) + 16, 16)
        t_high, t_low = split(trans_ref[0, jnp.maximum(lag - 1, 0)])
        pair = dot(both, t_high)
        value = pair[:64] + pair[64:] + dot(high, t_low)
        send_ref[q] = (jnp.where(lag == 0, 0.0, value) + came_ref[q].astype(f32)).astype(bf16)


def spread(pieces_ref, out_ref):
    value = join_pieces(pieces_ref, 0)
    for q in range(8):
        out_ref[q] = value


def forward(own_ref, other_ref, adj_ref, trans_ref, pot_ref, msg_ref):
    cluster = lax.axis_index(BLK)
    core = lax.axis_index("core")
    total = jnp.zeros((64, 64), f32)
    for q in range(8):
        for ref, parity in ((own_ref, core), (other_ref, 1 - core)):
            lag = lax.rem(cluster - (2 * q + parity) + 16, 16)
            t_high, t_low = split(trans_ref[0, jnp.maximum(lag - 1, 0)])
            both = jnp.concatenate([t_high, t_low], axis=0)
            pair = dot_last(both, ref[q])
            total = total + jnp.where(lag == 0, 0.0, pair[:64] + pair[64:])
    pot_ref[...] = jnp.concatenate([total[:32], total[32:]], axis=1).astype(bf16)
    put_pieces(msg_ref, jnp.sum(adj_ref[...].astype(f32), axis=0).astype(bf16))


def near(count_ref, rows_ref, cols_ref, tiles_ref, drive_ref, low_ref, adj_ref, ahead_ref, msg_ref, acc, behind):
    acc[...] = jnp.zeros_like(acc)
    behind[...] = jnp.zeros_like(behind)
    count = count_ref[0]
    group = 4

    def step(index, carry):
        results = []
        for part in range(group):
            slot = index * group + part
            live = slot < count
            slot = jnp.minimum(slot, 31)
            row = rows_ref[slot]
            col = cols_ref[slot]
            tile = tiles_ref[slot]
            fwd = dot_last(drive_ref[col], tile)
            bwd = dot(low_ref[row], tile)
            results.append((live, row, col, fwd, bwd))
        for live, row, col, fwd, bwd in results:
            acc[row] += jnp.where(live, fwd, 0.0)
            behind[col] += jnp.where(live, bwd, 0.0)
        return carry

    lax.fori_loop(0, (count + group - 1) // group, step, 0)
    for part in range(2):
        ahead_ref[:, part * 256 : part * 256 + 256] = acc[part]
    for col in range(32):
        for half in range(2):
            msg_ref[col // 2, pl.ds(col % 2 * 128 + half * 64, 64), :] = behind[
                col, :, half * 128 : half * 128 + 128
            ].astype(bf16)
    msg_ref[:, 256:288, :] = adj_ref[...]


def low_shares(near_ref, pot_ref, out_ref):
    adjoint = jnp.sum(near_ref[:, 256:288, :].astype(f32), axis=0).astype(bf16)
    for piece in range(16):
        out_ref[piece, 0:32, :] = adjoint
        out_ref[piece, 32:64, :] = pot_ref[...]


def finish(low_ref, near_ref, ahead_ref, skin_ref, skout_ref, resp_ref, sens_ref):
    adjoint = join_pieces(low_ref, 0)
    packed = jnp.concatenate([low_ref[r, 32:64, :] for r in range(16)], axis=0)
    packed = packed.astype(f32).T.astype(bf16)
    upper = jnp.concatenate([skout_ref[r * 64 : r * 64 + 32, :] for r in range(16)], axis=0)
    lower = jnp.concatenate([skout_ref[r * 64 + 32 : r * 64 + 64, :] for r in range(16)], axis=0)
    resp_ref[...] = ahead_ref[...] + dot(packed[:64], upper) + dot(packed[64:], lower)
    far = dot(adjoint, skin_ref[...])
    for part in range(4):
        value = near_ref[0, part * 64 : part * 64 + 64, :].astype(f32)
        for source in range(1, 16):
            value = value + near_ref[source, part * 64 : part * 64 + 64, :].astype(f32)
        sens_ref[:, part * 128 : part * 128 + 128] = far[:, part * 128 : part * 128 + 128] + value


def swap(value):
    return lax.ppermute(value, "core", [(0, 1), (1, 0)])


def exchange(value, axes):
    return lax.all_to_all(value, axes, 0, 0, tiled=True)


def on_device(exc, loads, tiles, tile_rows, tile_cols, tile_count, skin, skout, trans):
    drive, low, msg = call(
        prepare,
        [((2, 64, 256), bf16), ((2, 64, 256), bf16), ((16, 64, 128), bf16)],
        [exc, loads, skin, skout],
        name="prepare",
    )
    drives = lax.all_gather(drive, ROWS, axis=0, tiled=True)
    msg = exchange(msg, ROWS)
    copies, gradient, send = call(
        cross_core,
        [((16, 32, 128), bf16), ((64, 64), f32), ((8, 64, 1024), bf16)],
        [msg, trans],
        name="cross_core",
    )
    came = swap(send)
    (charges,) = call(spread, [((8, 64, 1024), bf16)], [exchange(copies, ROWS)], name="spread")
    charges = exchange(charges, FACE)
    others = swap(charges)
    (send,) = call(own_core, [((8, 64, 1024), bf16)], [gradient, came, trans], name="own_core")
    adjoint = exchange(send, FACE)
    potential, adjoint = call(
        forward,
        [((32, 128), bf16), ((16, 32, 128), bf16)],
        [charges, others, adjoint, trans],
        name="forward",
    )
    ahead, behind = call(
        near,
        [((64, 512), f32), ((16, 288, 128), bf16)],
        [tile_count, tile_rows, tile_cols, tiles, drives, low, adjoint],
        specs=[smem(), smem(), smem()] + [vmem()] * 4,
        scratch=[pltpu.VMEM((2, 64, 256), f32), pltpu.VMEM((32, 64, 256), f32)],
        name="near",
    )
    behind = exchange(behind, ROWS)
    (shares,) = call(low_shares, [((16, 64, 128), bf16)], [behind, potential], name="low_shares")
    shares = exchange(shares, ROWS)
    return tuple(
        call(
            finish,
            [((64, 512), f32), ((64, 512), f32)],
            [shares, behind, ahead, skin, skout],
            name="finish",
        )
    )


def solution(mesh):
    fine = Mesh(mesh.devices.reshape(2, 4, 2, 2, 8), BLK + ROWS)
    every = BLK + ROWS
    return jax.shard_map(
        on_device,
        mesh=fine,
        in_specs=(
            P(None, every),
            P(None, every),
            P(every, None, None),
            P(every),
            P(every),
            P(every),
            P(None, every),
            P(None, every),
            P(BLK, None, ROWS, None),
        ),
        out_specs=(P(None, every), P(None, every)),
        check_vma=False,
    )
```

```python
import jax
import jax.numpy as jnp
from jax import lax
from jax.experimental import pallas as pl
from jax.experimental.pallas import tpu as pltpu
from jax.sharding import Mesh
from jax.sharding import PartitionSpec as P

BLK = ("xlo", "y", "core")
ROWS = ("xhi", "z")
FACE = ("xlo", "y")
bf16 = jnp.bfloat16
f32 = jnp.float32
LAST = (((1,), (1,)), ((), ()))


def vmem():
    return pl.BlockSpec(memory_space=pltpu.VMEM)


def smem():
    return pl.BlockSpec(memory_space=pltpu.SMEM)


def hbm():
    return pl.BlockSpec(memory_space=pltpu.HBM)


def call(kernel, outs, args, specs=None, scratch=(), flops=10**7, name=None, room=8, alias=None):
    moved = sum(a.size * a.dtype.itemsize for a in args)
    return pl.pallas_call(
        kernel,
        out_shape=[jax.ShapeDtypeStruct(s, d) for s, d in outs],
        in_specs=specs or [vmem()] * len(args),
        out_specs=[vmem()] * len(outs),
        scratch_shapes=list(scratch),
        compiler_params=pltpu.CompilerParams(vmem_limit_bytes=room * 2**20),
        cost_estimate=pl.CostEstimate(flops=flops, bytes_accessed=moved, transcendentals=0),
        name=name,
        input_output_aliases=alias or {},
    )(*args)


def split(value):
    high = value.astype(bf16)
    return high, (value - high.astype(f32)).astype(bf16)


def dot(a, b):
    return jnp.dot(a, b, preferred_element_type=f32)


def dot_last(a, b):
    return lax.dot_general(a, b, LAST, preferred_element_type=f32)


def join_pieces(ref, first):
    rows = []
    for band in range(8):
        blocks = [
            ref[band * 2 + half, first + part * 8 : first + part * 8 + 8, :]
            for half in range(2)
            for part in range(4)
        ]
        rows.append(jnp.concatenate(blocks, axis=1))
    return jnp.concatenate(rows, axis=0)


def round_panels(exc_ref, loads_ref, drive_ref, low_ref):
    drive = exc_ref[...].astype(bf16)
    loads = loads_ref[...].astype(bf16)
    for part in range(2):
        drive_ref[part] = drive[:, part * 256 : part * 256 + 256]
        low_ref[part] = loads[:, part * 256 : part * 256 + 256]


def prepare(drive_ref, low_ref, skin_hbm, skout_hbm, msg_ref, skin, skout, sems):
    first = pltpu.make_async_copy(skin_hbm, skin, sems.at[0])
    second = pltpu.make_async_copy(skout_hbm, skout, sems.at[1])
    first.start()
    second.start()
    drive = jnp.concatenate([drive_ref[0], drive_ref[1]], axis=1)
    loads = jnp.concatenate([low_ref[0], low_ref[1]], axis=1)
    first.wait()
    charges = dot_last(drive, skin[...])
    for piece in range(16):
        row = piece // 2 * 8
        for part in range(4):
            col = piece % 2 * 512 + part * 128
            msg_ref[piece, part * 8 : part * 8 + 8, :] = charges[row : row + 8, col : col + 128].astype(bf16)
    second.wait()
    gradient = dot_last(skout[...], jnp.concatenate([loads, loads], axis=0))
    left = lax.broadcasted_iota(jnp.int32, (32, 128), 1) < 64
    for piece in range(16):
        k = piece * 64
        msg_ref[piece, 32:64, :] = jnp.where(
            left, gradient[k : k + 32], gradient[k + 32 : k + 64]
        ).astype(bf16)


def lags():
    cluster = lax.axis_index(BLK)
    core = lax.axis_index("core")
    return [
        lax.rem(cluster - (2 * q + parity) + 16, 16) for parity in (1 - core, core) for q in range(8)
    ]


def fetch(trans_hbm, blocks, sems, lag):
    copies = []
    for index in range(16):
        copies.append(
            pltpu.make_async_copy(
                trans_hbm.at[0, jnp.maximum(lag[index] - 1, 0)], blocks.at[index], sems.at[index]
            )
        )
        copies[index].start()
    return copies


def adjoint_terms(msg_ref, trans_hbm, copies_ref, send_ref, keep_ref, blocks, sems):
    lag = lags()
    fetched = fetch(trans_hbm, blocks, sems, lag)
    total = jnp.sum(msg_ref[...].astype(f32), axis=0)
    share = total[:32].astype(bf16)
    for piece in range(16):
        copies_ref[piece] = share
    packed = total[32:]
    gradient = jnp.concatenate([packed, pltpu.roll(packed, 64, 1)], axis=0)
    high, low = split(gradient.T[:64])
    both = jnp.concatenate([high, low], axis=0)
    for index in range(16):
        fetched[index].wait()
        t_high, t_low = split(blocks[index])
        pair = dot(both, t_high)
        value = pair[:64] + pair[64:] + dot(high, t_low)
        if index < 8:
            send_ref[index] = value.astype(bf16)
        else:
            keep_ref[index - 8] = jnp.where(lag[index] == 0, 0.0, value)


def pack(keep_ref, came_ref, pieces_ref, out_ref):
    charges = join_pieces(pieces_ref, 0)
    for q in range(8):
        out_ref[q, 0] = (keep_ref[q] + came_ref[q].astype(f32)).astype(bf16)
        out_ref[q, 1] = charges


def unpack(came_ref, near_ref, msg_ref, charges_ref):
    del near_ref
    total = came_ref[0, 0].astype(f32)
    charges_ref[0] = came_ref[0, 1]
    for q in range(1, 8):
        total = total + came_ref[q, 0].astype(f32)
        charges_ref[q] = came_ref[q, 1]
    for piece in range(16):
        row = piece // 2 * 8
        for part in range(4):
            col = piece % 2 * 512 + part * 128
            msg_ref[piece, 256 + part * 8 : 264 + part * 8, :] = total[row : row + 8, col : col + 128].astype(bf16)


def forward(other_ref, came_ref, trans_hbm, pot_ref, blocks, sems):
    lag = lags()
    fetched = fetch(trans_hbm, blocks, sems, lag)
    total = jnp.zeros((64, 64), f32)
    for index in range(16):
        fetched[index].wait()
        t_high, t_low = split(blocks[index])
        both = jnp.concatenate([t_high, t_low], axis=0)
        charges = other_ref[index] if index < 8 else came_ref[index - 8, 1]
        pair = dot_last(both, charges)
        total = total + jnp.where(lag[index] == 0, 0.0, pair[:64] + pair[64:])
    pot_ref[...] = jnp.concatenate([total[:32], total[32:]], axis=1).astype(bf16)


def near(count_ref, rows_ref, cols_ref, low_ref, tiles_hbm, *refs):
    pieces, (ahead_ref, msg_ref, acc, behind, drives, tiles_ref, piece_sems, tile_sems) = refs[:8], refs[8:]

    def tile_copy(index):
        span = pl.ds(index * 4, 4)
        return pltpu.make_async_copy(tiles_hbm.at[span], tiles_ref.at[span], tile_sems.at[index])

    arriving = [
        pltpu.make_async_copy(pieces[index], drives.at[index], piece_sems.at[index]) for index in range(8)
    ]
    for copy in arriving:
        copy.start()
    for index in range(8):
        tile_copy(index).start()
    acc[...] = jnp.zeros_like(acc)
    behind[...] = jnp.zeros_like(behind)
    count = count_ref[0]
    my_z = lax.axis_index("z")
    my_half = lax.axis_index("xhi")
    group = 4
    for copy in arriving:
        copy.wait()

    def step(index, carry):
        tile_copy(index).wait()
        results = []
        for part in range(group):
            slot = index * group + part
            live = slot < count
            row = rows_ref[slot]
            col = cols_ref[slot]
            owner = col // 2
            hops = lax.rem(my_z - lax.rem(owner, 8) + 8, 8)
            side = lax.rem(owner // 8 + my_half, 2)
            tile = tiles_ref[slot]
            fwd = dot_last(drives[hops, side, lax.rem(col, 2)], tile)
            bwd = dot(low_ref[row], tile)
            results.append((live, row, col, fwd, bwd))
        for live, row, col, fwd, bwd in results:
            acc[row] += jnp.where(live, fwd, 0.0)
            behind[col] += jnp.where(live, bwd, 0.0)
        return carry

    groups = (count + group - 1) // group
    lax.fori_loop(0, groups, step, 0)

    def drain(index, carry):
        tile_copy(index).wait()
        return carry

    lax.fori_loop(groups, 8, drain, 0)
    for part in range(2):
        ahead_ref[:, part * 256 : part * 256 + 256] = acc[part]
    for col in range(32):
        for half in range(2):
            msg_ref[col // 2, pl.ds(col % 2 * 128 + half * 64, 64), :] = behind[
                col, :, half * 128 : half * 128 + 128
            ].astype(bf16)
    msg_ref[:, 256:288, :] = jnp.zeros((16, 32, 128), bf16)


def low_shares(near_ref, pot_ref, out_ref):
    adjoint = jnp.sum(near_ref[:, 256:288, :].astype(f32), axis=0).astype(bf16)
    for piece in range(16):
        out_ref[piece, 0:32, :] = adjoint
        out_ref[piece, 32:64, :] = pot_ref[...]


def finish(low_ref, near_ref, ahead_ref, skin_hbm, skout_hbm, resp_ref, sens_ref, skin_ref, skout_ref, sems):
    first = pltpu.make_async_copy(skout_hbm, skout_ref, sems.at[0])
    second = pltpu.make_async_copy(skin_hbm, skin_ref, sems.at[1])
    first.start()
    second.start()
    adjoint = join_pieces(low_ref, 0)
    packed = jnp.concatenate([low_ref[r, 32:64, :] for r in range(16)], axis=0)
    packed = packed.astype(f32).T.astype(bf16)
    first.wait()
    upper = jnp.concatenate([skout_ref[r * 64 : r * 64 + 32, :] for r in range(16)], axis=0)
    lower = jnp.concatenate([skout_ref[r * 64 + 32 : r * 64 + 64, :] for r in range(16)], axis=0)
    resp_ref[...] = ahead_ref[...] + dot(packed[:64], upper) + dot(packed[64:], lower)
    second.wait()
    far = dot(adjoint, skin_ref[...])
    for part in range(4):
        value = near_ref[0, part * 64 : part * 64 + 64, :].astype(f32)
        for source in range(1, 16):
            value = value + near_ref[source, part * 64 : part * 64 + 64, :].astype(f32)
        sens_ref[:, part * 128 : part * 128 + 128] = far[:, part * 128 : part * 128 + 128] + value


def swap(value):
    return lax.ppermute(value, "core", [(0, 1), (1, 0)])


def exchange(value, axes):
    return lax.all_to_all(value, axes, 0, 0, tiled=True)


def in_hbm(value):
    return pltpu.with_memory_space_constraint(value, pltpu.HBM)


def shift(value, step):
    return lax.ppermute(value, "z", [(i, (i + step) % 8) for i in range(8)])


def tie(*values):
    return lax.optimization_barrier(values)


def on_device(exc, loads, tiles, tile_rows, tile_cols, tile_count, skin, skout, trans):
    tiles, skin, skout, trans = (in_hbm(value) for value in (tiles, skin, skout, trans))
    blocks = [pltpu.VMEM((16, 64, 1024), f32), pltpu.SemaphoreType.DMA((16,))]
    drive, low = call(
        round_panels, [((2, 64, 256), bf16), ((2, 64, 256), bf16)], [exc, loads], name="round_panels"
    )
    mate = lax.ppermute(drive, "xhi", [(0, 1), (1, 0)])
    (msg,) = call(
        prepare,
        [((16, 64, 128), bf16)],
        [drive, low, skin, skout],
        specs=[vmem()] * 2 + [hbm()] * 2,
        scratch=[pltpu.VMEM((1024, 512), bf16)] * 2 + [pltpu.SemaphoreType.DMA((2,))],
        name="prepare",
    )
    here = jnp.stack([drive, mate])
    here, msg = tie(here, msg)
    up1, down1 = shift(here, 1), shift(here, -1)
    msg = exchange(msg, ROWS)
    msg, up1, down1 = tie(msg, up1, down1)
    copies, send, keep = call(
        adjoint_terms,
        [((16, 32, 128), bf16), ((8, 64, 1024), bf16), ((8, 64, 1024), f32)],
        [msg, trans],
        specs=[vmem(), hbm()],
        scratch=blocks,
        name="adjoint_terms",
        room=12,
    )
    came = swap(send)
    up2, down2 = shift(up1, 1), shift(down1, -1)
    copies = exchange(copies, ROWS)
    copies, up2, down2 = tie(copies, up2, down2)
    (both,) = call(pack, [((8, 2, 64, 1024), bf16)], [keep, came, copies], name="pack")
    up3, down3 = shift(up2, 1), shift(down2, -1)
    up4 = shift(up3, 1)
    both = exchange(both, FACE)
    ahead, behind = call(
        near,
        [((64, 512), f32), ((16, 288, 128), bf16)],
        [tile_count, tile_rows, tile_cols, low, tiles, here, up1, up2, up3, up4, down3, down2, down1],
        specs=[smem(), smem(), smem(), vmem()] + [hbm()] * 9,
        scratch=[
            pltpu.VMEM((2, 64, 256), f32),
            pltpu.VMEM((32, 64, 256), f32),
            pltpu.VMEM((8, 2, 2, 64, 256), bf16),
            pltpu.VMEM((32, 256, 256), bf16),
            pltpu.SemaphoreType.DMA((8,)),
            pltpu.SemaphoreType.DMA((8,)),
        ],
        name="near",
        room=16,
    )
    behind, charges = call(
        unpack,
        [((16, 288, 128), bf16), ((8, 64, 1024), bf16)],
        [both, behind],
        alias={1: 0},
        name="unpack",
    )
    others = swap(charges)
    behind = exchange(behind, ROWS)
    (potential,) = call(
        forward,
        [((32, 128), bf16)],
        [others, both, trans],
        specs=[vmem(), vmem(), hbm()],
        scratch=blocks,
        name="forward",
        room=12,
    )
    (shares,) = call(low_shares, [((16, 64, 128), bf16)], [behind, potential], name="low_shares")
    shares = exchange(shares, ROWS)
    return tuple(
        call(
            finish,
            [((64, 512), f32), ((64, 512), f32)],
            [shares, behind, ahead, skin, skout],
            specs=[vmem()] * 3 + [hbm()] * 2,
            scratch=[pltpu.VMEM((1024, 512), bf16)] * 2 + [pltpu.SemaphoreType.DMA((2,))],
            name="finish",
        )
    )


def solution(mesh):
    fine = Mesh(mesh.devices.reshape(2, 4, 2, 2, 8), BLK + ROWS)
    every = BLK + ROWS
    return jax.shard_map(
        on_device,
        mesh=fine,
        in_specs=(
            P(None, every),
            P(None, every),
            P(every, None, None),
            P(every),
            P(every),
            P(every),
            P(None, every),
            P(None, every),
            P(BLK, None, ROWS, None),
        ),
        out_specs=(P(None, every), P(None, every)),
        check_vma=False,
    )
```

```python
import jax
import jax.numpy as jnp
from jax import lax
from jax.experimental import pallas as pl
from jax.experimental.pallas import tpu as pltpu
from jax.sharding import Mesh
from jax.sharding import PartitionSpec as P

BLK = ("xlo", "y", "core")
ROWS = ("xhi", "z")
FACE = ("xlo", "y")
bf16 = jnp.bfloat16
f32 = jnp.float32
LAST = (((1,), (1,)), ((), ()))


def vmem():
    return pl.BlockSpec(memory_space=pltpu.VMEM)


def smem():
    return pl.BlockSpec(memory_space=pltpu.SMEM)


def hbm():
    return pl.BlockSpec(memory_space=pltpu.HBM)


def call(kernel, outs, args, specs=None, scratch=(), flops=10**7, name=None, room=8, alias=None):
    moved = sum(a.size * a.dtype.itemsize for a in args)
    return pl.pallas_call(
        kernel,
        out_shape=[jax.ShapeDtypeStruct(s, d) for s, d in outs],
        in_specs=specs or [vmem()] * len(args),
        out_specs=[vmem()] * len(outs),
        scratch_shapes=list(scratch),
        compiler_params=pltpu.CompilerParams(vmem_limit_bytes=room * 2**20),
        cost_estimate=pl.CostEstimate(flops=flops, bytes_accessed=moved, transcendentals=0),
        name=name,
        input_output_aliases=alias or {},
    )(*args)


def split(value):
    high = value.astype(bf16)
    return high, (value - high.astype(f32)).astype(bf16)


def dot(a, b):
    return jnp.dot(a, b, preferred_element_type=f32)


def dot_last(a, b):
    return lax.dot_general(a, b, LAST, preferred_element_type=f32)


def join_pieces(ref, first):
    rows = []
    for band in range(8):
        blocks = [
            ref[band * 2 + half, first + part * 8 : first + part * 8 + 8, :]
            for half in range(2)
            for part in range(4)
        ]
        rows.append(jnp.concatenate(blocks, axis=1))
    return jnp.concatenate(rows, axis=0)


def prepare(exc_hbm, loads_hbm, skin_hbm, skout_hbm, drive_ref, low_ref, msg_ref, exc, loads, skin, skout, sems):
    pairs = ((exc_hbm, exc), (skin_hbm, skin), (loads_hbm, loads), (skout_hbm, skout))
    copies = [pltpu.make_async_copy(src, dst, sems.at[i]) for i, (src, dst) in enumerate(pairs)]
    for copy in copies:
        copy.start()
    copies[0].wait()
    drive = exc[...].astype(bf16)
    for part in range(2):
        drive_ref[part] = drive[:, part * 256 : part * 256 + 256]
    copies[1].wait()
    charges = dot_last(drive, skin[...])
    for piece in range(16):
        row = piece // 2 * 8
        for part in range(4):
            col = piece % 2 * 512 + part * 128
            msg_ref[piece, part * 8 : part * 8 + 8, :] = charges[row : row + 8, col : col + 128].astype(bf16)
    copies[2].wait()
    low = loads[...].astype(bf16)
    for part in range(2):
        low_ref[part] = low[:, part * 256 : part * 256 + 256]
    twice = jnp.concatenate([low, low], axis=0)
    copies[3].wait()
    gradient = dot_last(skout[...], twice)
    left = lax.broadcasted_iota(jnp.int32, (32, 128), 1) < 64
    for piece in range(16):
        k = piece * 64
        high, rest = split(jnp.where(left, gradient[k : k + 32], gradient[k + 32 : k + 64]))
        msg_ref[piece, 32:64, :] = high
        msg_ref[piece, 64:96, :] = rest


def split_translation(trans_hbm, high_ref, low_ref, blocks, sems):
    copies = [pltpu.make_async_copy(trans_hbm.at[0, d], blocks.at[d], sems.at[d]) for d in range(15)]
    for copy in copies:
        copy.start()
    for d in range(15):
        copies[d].wait()
        high, low = split(blocks[d])
        high_ref[d] = high
        low_ref[d] = low


def lags():
    cluster = lax.axis_index(BLK)
    core = lax.axis_index("core")
    return [
        lax.rem(cluster - (2 * q + parity) + 16, 16) for parity in (1 - core, core) for q in range(8)
    ]


def adjoint_terms(msg_ref, high_ref, low_ref, copies_ref, send_ref, keep_ref):
    lag = lags()
    total = jnp.sum(msg_ref[:, 0:32, :].astype(f32), axis=0)
    share = total.astype(bf16)
    for piece in range(16):
        copies_ref[piece] = share
    packed = jnp.sum(msg_ref[:, 32:64, :].astype(f32) + msg_ref[:, 64:96, :].astype(f32), axis=0)
    gradient = jnp.concatenate([packed, pltpu.roll(packed, 64, 1)], axis=0)
    high, low = split(gradient.T[:64])
    both = jnp.concatenate([high, low], axis=0)
    for index in range(16):
        block = jnp.maximum(lag[index] - 1, 0)
        pair = dot(both, high_ref[block])
        value = pair[:64] + pair[64:] + dot(high, low_ref[block])
        if index < 8:
            send_ref[index] = value
        else:
            keep_ref[index - 8] = jnp.where(lag[index] == 0, 0.0, value)


def pack(keep_ref, came_ref, pieces_ref, out_ref):
    charges = join_pieces(pieces_ref, 0)
    for q in range(8):
        out_ref[q, 0] = (keep_ref[q] + came_ref[q]).astype(bf16)
        out_ref[q, 1] = charges


def unpack(came_ref, keep_ref, mate_ref, msg_ref, charges_ref):
    total = came_ref[0, 0].astype(f32)
    charges_ref[0] = came_ref[0, 1]
    for q in range(1, 8):
        total = total + came_ref[q, 0].astype(f32)
        charges_ref[q] = came_ref[q, 1]
    for piece in range(8):
        msg_ref[piece, 0:256, :] = (keep_ref[piece] + mate_ref[piece].astype(f32)).astype(bf16)
        for part in range(8):
            msg_ref[piece, 256 + part * 8 : 264 + part * 8, :] = total[
                piece * 8 : piece * 8 + 8, part * 128 : part * 128 + 128
            ].astype(bf16)


def forward(other_ref, came_ref, high_ref, low_ref, pot_ref):
    lag = lags()
    total = jnp.zeros((64, 64), f32)
    for index in range(16):
        block = jnp.maximum(lag[index] - 1, 0)
        both = jnp.concatenate([high_ref[block], low_ref[block]], axis=0)
        charges = other_ref[index] if index < 8 else came_ref[index - 8, 1]
        pair = dot_last(both, charges)
        total = total + jnp.where(lag[index] == 0, 0.0, pair[:64] + pair[64:])
    pot_ref[...] = jnp.concatenate([total[:32], total[32:]], axis=1).astype(bf16)


def near(count_ref, rows_ref, cols_ref, low_ref, tiles_hbm, *refs):
    pieces, refs = refs[:8], refs[8:]
    ahead_ref, send_ref, keep_ref, acc, behind, drives, tiles_ref, tile_sems, piece_sems = refs

    def tile_copy(index):
        span = pl.ds(index * 4, 4)
        return pltpu.make_async_copy(tiles_hbm.at[span], tiles_ref.at[span], tile_sems.at[index])

    arriving = [
        pltpu.make_async_copy(pieces[index], drives.at[index], piece_sems.at[index]) for index in range(8)
    ]
    for copy in arriving:
        copy.start()
    for index in range(8):
        tile_copy(index).start()
    acc[...] = jnp.zeros_like(acc)
    behind[...] = jnp.zeros_like(behind)
    for copy in arriving:
        copy.wait()
    count = count_ref[0]
    my_z = lax.axis_index("z")
    my_half = lax.axis_index("xhi")
    group = 4

    def step(index, carry):
        tile_copy(index).wait()
        results = []
        for part in range(group):
            slot = index * group + part
            row = rows_ref[slot]
            col = cols_ref[slot]
            owner = col // 2
            hops = lax.rem(my_z - lax.rem(owner, 8) + 8, 8)
            side = lax.rem(owner // 8 + my_half, 2)
            tile = tiles_ref[slot]
            fwd = dot_last(drives[hops, side, lax.rem(col, 2)], tile)
            bwd = dot(low_ref[row], tile)
            results.append((slot < count, row, col, fwd, bwd))
        for live, row, col, fwd, bwd in results:
            acc[row] += jnp.where(live, fwd, 0.0)
            behind[col] += jnp.where(live, bwd, 0.0)
        return carry

    groups = (count + group - 1) // group
    lax.fori_loop(0, groups, step, 0)

    def drain(index, carry):
        tile_copy(index).wait()
        return carry

    lax.fori_loop(groups, 8, drain, 0)
    for part in range(2):
        ahead_ref[:, part * 256 : part * 256 + 256] = acc[part]
    for z in range(8):
        for part in range(4):
            rows = pl.ds(part * 64, 64)
            cols = pl.ds(part % 2 * 128, 128)
            send_ref[z, rows, :] = behind[(1 - my_half) * 16 + 2 * z + part // 2, :, cols].astype(bf16)
            keep_ref[z, rows, :] = behind[my_half * 16 + 2 * z + part // 2, :, cols]


def fold(msg_ref, out_ref):
    out_ref[...] = jnp.sum(msg_ref[:, 256:320, :].astype(f32), axis=0)


def low_shares(mine_ref, mate_ref, pot_ref, mate_pot_ref, out_ref):
    adjoint = (mine_ref[...] + mate_ref[...]).astype(bf16)
    upper = lax.axis_index("xhi") == 1
    pot = pot_ref[...].astype(f32)
    mate_pot = mate_pot_ref[...].astype(f32)
    first = jnp.where(upper, mate_pot, pot).astype(bf16)
    second = jnp.where(upper, pot, mate_pot).astype(bf16)
    for piece in range(8):
        out_ref[piece, 0:64, :] = adjoint
        out_ref[piece, 64:96, :] = first
        out_ref[piece, 96:128, :] = second


def finish(low_ref, near_ref, ahead_ref, skin_ref, skout_ref, resp_ref, sens_ref):
    adjoint = jnp.concatenate(
        [
            jnp.concatenate([low_ref[z, part * 8 : part * 8 + 8, :] for part in range(8)], axis=1)
            for z in range(8)
        ],
        axis=0,
    )
    packed = jnp.concatenate([low_ref[r % 8, 64 + r // 8 * 32 : 96 + r // 8 * 32, :] for r in range(16)], axis=0)
    packed = packed.astype(f32).T.astype(bf16)
    upper = jnp.concatenate([skout_ref[r * 64 : r * 64 + 32, :] for r in range(16)], axis=0)
    lower = jnp.concatenate([skout_ref[r * 64 + 32 : r * 64 + 64, :] for r in range(16)], axis=0)
    resp_ref[...] = ahead_ref[...] + dot(packed[:64], upper) + dot(packed[64:], lower)
    far = dot(adjoint, skin_ref[...])
    for part in range(4):
        value = near_ref[0, part * 64 : part * 64 + 64, :].astype(f32)
        for source in range(1, 8):
            value = value + near_ref[source, part * 64 : part * 64 + 64, :].astype(f32)
        sens_ref[:, part * 128 : part * 128 + 128] = far[:, part * 128 : part * 128 + 128] + value


def swap(value, axis):
    return lax.ppermute(value, axis, [(0, 1), (1, 0)])


def exchange(value, axes):
    return lax.all_to_all(value, axes, 0, 0, tiled=True)


def in_hbm(value):
    return pltpu.with_memory_space_constraint(value, pltpu.HBM)


def shift(value, step):
    return lax.ppermute(value, "z", [(i, (i + step) % 8) for i in range(8)])


def tie(*values):
    return lax.optimization_barrier(values)


def on_device(exc, loads, tiles, tile_rows, tile_cols, tile_count, skin, skout, trans):
    drive, low, msg = call(
        prepare,
        [((2, 64, 256), bf16), ((2, 64, 256), bf16), ((16, 96, 128), bf16)],
        [in_hbm(exc), in_hbm(loads), in_hbm(skin), in_hbm(skout)],
        specs=[hbm()] * 4,
        scratch=[pltpu.VMEM((64, 512), f32)] * 2
        + [pltpu.VMEM((1024, 512), bf16)] * 2
        + [pltpu.SemaphoreType.DMA((4,))],
        name="prepare",
    )
    here = jnp.stack([drive, swap(drive, "xhi")])
    up1, down1 = shift(here, 1), shift(here, -1)
    up2, down2 = shift(up1, 1), shift(down1, -1)
    high, rest = call(
        split_translation,
        [((15, 64, 1024), bf16)] * 2,
        [in_hbm(trans)],
        specs=[hbm()],
        scratch=[pltpu.VMEM((15, 64, 1024), f32), pltpu.SemaphoreType.DMA((15,))],
        name="split_translation",
        room=16,
    )
    msg, up2, down2, high, rest = tie(exchange(msg, ROWS), up2, down2, high, rest)
    copies, send, keep = call(
        adjoint_terms,
        [((16, 32, 128), bf16), ((8, 64, 1024), f32), ((8, 64, 1024), f32)],
        [msg, high, rest],
        name="adjoint_terms",
        room=12,
    )
    came = swap(send, "core")
    up3, down3 = shift(up2, 1), shift(down2, -1)
    up4 = shift(up3, 1)
    copies, up4, down3 = tie(exchange(copies, ROWS), up4, down3)
    (both,) = call(pack, [((8, 2, 64, 1024), bf16)], [keep, came, copies], name="pack")
    both = exchange(both, FACE)
    ahead, send, keep = call(
        near,
        [((64, 512), f32), ((8, 256, 128), bf16), ((8, 256, 128), f32)],
        [tile_count, tile_rows, tile_cols, low, in_hbm(tiles)]
        + [in_hbm(piece) for piece in (here, up1, up2, up3, up4, down3, down2, down1)],
        specs=[smem(), smem(), smem(), vmem()] + [hbm()] * 9,
        scratch=[
            pltpu.VMEM((2, 64, 256), f32),
            pltpu.VMEM((32, 64, 256), f32),
            pltpu.VMEM((8, 2, 2, 64, 256), bf16),
            pltpu.VMEM((32, 256, 256), bf16),
            pltpu.SemaphoreType.DMA((8,)),
            pltpu.SemaphoreType.DMA((8,)),
        ],
        name="near",
        room=16,
    )
    mate = swap(send, "xhi")
    behind, charges = call(
        unpack,
        [((8, 320, 128), bf16), ((8, 64, 1024), bf16)],
        [both, keep, mate],
        name="unpack",
    )
    others = swap(charges, "core")
    behind = exchange(behind, "z")
    (potential,) = call(
        forward,
        [((32, 128), bf16)],
        [others, both, high, rest],
        name="forward",
        room=12,
    )
    mate_pot = swap(potential, "xhi")
    behind, mate_pot = tie(behind, mate_pot)
    (mine,) = call(fold, [((64, 128), f32)], [behind], name="fold")
    (shares,) = call(
        low_shares,
        [((8, 128, 128), bf16)],
        [mine, swap(mine, "xhi"), potential, mate_pot],
        name="low_shares",
    )
    shares = exchange(shares, "z")
    return tuple(
        call(
            finish,
            [((64, 512), f32), ((64, 512), f32)],
            [shares, behind, ahead, skin, skout],
            name="finish",
        )
    )


def solution(mesh):
    fine = Mesh(mesh.devices.reshape(2, 4, 2, 2, 8), BLK + ROWS)
    every = BLK + ROWS
    return jax.shard_map(
        on_device,
        mesh=fine,
        in_specs=(
            P(None, every),
            P(None, every),
            P(every, None, None),
            P(every),
            P(every),
            P(every),
            P(None, every),
            P(None, every),
            P(BLK, None, ROWS, None),
        ),
        out_specs=(P(None, every), P(None, every)),
        check_vma=False,
    )
```

```python
import jax
import jax.numpy as jnp
from jax import lax
from jax.experimental import pallas as pl
from jax.experimental.pallas import tpu as pltpu
from jax.sharding import Mesh
from jax.sharding import PartitionSpec as P

BLK = ("xlo", "y", "core")
ROWS = ("xhi", "z")
FACE = ("xlo", "y")
bf16 = jnp.bfloat16
f32 = jnp.float32
LAST = (((1,), (1,)), ((), ()))


def vmem():
    return pl.BlockSpec(memory_space=pltpu.VMEM)


def smem():
    return pl.BlockSpec(memory_space=pltpu.SMEM)


def hbm():
    return pl.BlockSpec(memory_space=pltpu.HBM)


def call(kernel, outs, args, specs=None, scratch=(), flops=10**7, name=None):
    moved = sum(a.size * a.dtype.itemsize for a in args)
    return pl.pallas_call(
        kernel,
        out_shape=[jax.ShapeDtypeStruct(s, d) for s, d in outs],
        in_specs=specs or [vmem()] * len(args),
        out_specs=[vmem()] * len(outs),
        scratch_shapes=list(scratch),
        compiler_params=pltpu.CompilerParams(vmem_limit_bytes=20 * 2**20),
        cost_estimate=pl.CostEstimate(flops=flops, bytes_accessed=moved, transcendentals=0),
        name=name,
    )(*args)


def split(value):
    high = value.astype(bf16)
    return high, (value - high.astype(f32)).astype(bf16)


def dot(a, b):
    return jnp.dot(a, b, preferred_element_type=f32)


def dot_last(a, b):
    return lax.dot_general(a, b, LAST, preferred_element_type=f32)


def join_pieces(ref, first):
    rows = []
    for band in range(8):
        blocks = [
            ref[band * 2 + half, first + part * 8 : first + part * 8 + 8, :]
            for half in range(2)
            for part in range(4)
        ]
        rows.append(jnp.concatenate(blocks, axis=1))
    return jnp.concatenate(rows, axis=0)


def prepare(exc_hbm, loads_hbm, skin_hbm, skout_hbm, drive_ref, low_ref, msg_ref, exc, loads, skin, skout, sems):
    pairs = ((exc_hbm, exc), (skin_hbm, skin), (loads_hbm, loads), (skout_hbm, skout))
    copies = [pltpu.make_async_copy(src, dst, sems.at[i]) for i, (src, dst) in enumerate(pairs)]
    for copy in copies:
        copy.start()
    copies[0].wait()
    drive = exc[...].astype(bf16)
    for part in range(2):
        drive_ref[part] = drive[:, part * 256 : part * 256 + 256]
    copies[1].wait()
    charges = dot_last(drive, skin[...])
    for piece in range(16):
        row = piece // 2 * 8
        for part in range(4):
            col = piece % 2 * 512 + part * 128
            msg_ref[piece, part * 8 : part * 8 + 8, :] = charges[row : row + 8, col : col + 128].astype(bf16)
    copies[2].wait()
    low = loads[...].astype(bf16)
    for part in range(2):
        low_ref[part] = low[:, part * 256 : part * 256 + 256]
    twice = jnp.concatenate([low, low], axis=0)
    copies[3].wait()
    gradient = dot_last(skout[...], twice)
    left = lax.broadcasted_iota(jnp.int32, (32, 128), 1) < 64
    for piece in range(16):
        k = piece * 64
        high, rest = split(jnp.where(left, gradient[k : k + 32], gradient[k + 32 : k + 64]))
        msg_ref[piece, 32:64, :] = high
        msg_ref[piece, 64:96, :] = rest


def split_translation(trans_hbm, out_ref, blocks, sems):
    copies = [pltpu.make_async_copy(trans_hbm.at[0, d], blocks.at[d], sems.at[d]) for d in range(15)]
    for copy in copies:
        copy.start()
    for d in range(15):
        copies[d].wait()
        high, low = split(blocks[d])
        out_ref[d, :64] = high
        out_ref[d, 64:] = low


def lags(parity):
    cluster = lax.axis_index(BLK)
    return [lax.rem(cluster - (2 * q + parity) + 16, 16) for q in range(8)]


def fetch(parts_hbm, blocks, sems, lag):
    copies = []
    for index, behind in enumerate(lag):
        source = parts_hbm.at[jnp.maximum(behind - 1, 0)]
        copies.append(pltpu.make_async_copy(source, blocks.at[index], sems.at[index]))
        copies[index].start()
    return copies


def term(both, block):
    pair = dot(both, block[:64])
    return pair[:64] + pair[64:] + dot(both[:64], block[64:])


def other_terms(msg_ref, parts_hbm, copies_ref, grad_ref, send_ref, blocks, sems):
    fetched = fetch(parts_hbm, blocks, sems, lags(1 - lax.axis_index("core")))
    share = jnp.sum(msg_ref[:, 0:32, :].astype(f32), axis=0).astype(bf16)
    for piece in range(16):
        copies_ref[piece] = share
    packed = jnp.sum(msg_ref[:, 32:64, :].astype(f32) + msg_ref[:, 64:96, :].astype(f32), axis=0)
    gradient = jnp.concatenate([packed, pltpu.roll(packed, 64, 1)], axis=0)
    high, low = split(gradient.T[:64])
    both = jnp.concatenate([high, low], axis=0)
    grad_ref[...] = both
    for index in range(8):
        fetched[index].wait()
        send_ref[index] = term(both, blocks[index])


def own_terms(grad_ref, came_ref, parts_hbm, out_ref, blocks, sems):
    lag = lags(lax.axis_index("core"))
    fetched = fetch(parts_hbm, blocks, sems, lag)
    both = grad_ref[...]
    for index in range(8):
        fetched[index].wait()
        value = jnp.where(lag[index] == 0, 0.0, term(both, blocks[index]))
        out_ref[index] = (value + came_ref[index]).astype(bf16)


def pack(own_ref, pieces_ref, out_ref):
    charges = join_pieces(pieces_ref, 0)
    for q in range(8):
        out_ref[q, 0] = own_ref[q]
        out_ref[q, 1] = charges


def unpack(came_ref, msg_ref, charges_ref):
    total = came_ref[0, 0].astype(f32)
    charges_ref[0] = came_ref[0, 1]
    for q in range(1, 8):
        total = total + came_ref[q, 0].astype(f32)
        charges_ref[q] = came_ref[q, 1]
    for piece in range(8):
        for part in range(8):
            msg_ref[piece, part * 8 : part * 8 + 8, :] = total[
                piece * 8 : piece * 8 + 8, part * 128 : part * 128 + 128
            ].astype(bf16)


def forward(other_ref, came_ref, parts_hbm, pot_ref, blocks, sems):
    core = lax.axis_index("core")
    lag = lags(1 - core) + lags(core)
    fetched = fetch(parts_hbm, blocks, sems, lag)
    total = jnp.zeros((64, 64), f32)
    for index in range(16):
        charges = other_ref[index] if index < 8 else came_ref[index - 8, 1]
        fetched[index].wait()
        pair = dot_last(blocks[index], charges)
        total = total + jnp.where(lag[index] == 0, 0.0, pair[:64] + pair[64:])
    pot_ref[...] = jnp.concatenate([total[:32], total[32:]], axis=1).astype(bf16)


def near(count_ref, rows_ref, cols_ref, low_ref, tiles_hbm, *refs):
    pieces, refs = refs[:8], refs[8:]
    ahead_ref, send_ref, keep_ref, acc, behind, drives, tiles_ref, tile_sems, piece_sems = refs

    def tile_copy(index):
        span = pl.ds(index * 4, 4)
        return pltpu.make_async_copy(tiles_hbm.at[span], tiles_ref.at[span], tile_sems.at[index])

    arriving = [
        pltpu.make_async_copy(pieces[index], drives.at[index], piece_sems.at[index]) for index in range(8)
    ]
    for copy in arriving:
        copy.start()
    for index in range(8):
        tile_copy(index).start()
    acc[...] = jnp.zeros_like(acc)
    behind[...] = jnp.zeros_like(behind)
    for copy in arriving:
        copy.wait()
    count = count_ref[0]
    my_z = lax.axis_index("z")
    my_half = lax.axis_index("xhi")
    group = 4

    def step(index, carry):
        tile_copy(index).wait()
        results = []
        for part in range(group):
            slot = index * group + part
            row = rows_ref[slot]
            col = cols_ref[slot]
            owner = col // 2
            hops = lax.rem(my_z - lax.rem(owner, 8) + 8, 8)
            side = lax.rem(owner // 8 + my_half, 2)
            tile = tiles_ref[slot]
            fwd = dot_last(drives[hops, side, lax.rem(col, 2)], tile)
            bwd = dot(low_ref[row], tile)
            results.append((slot < count, row, col, fwd, bwd))
        for live, row, col, fwd, bwd in results:
            acc[row] += jnp.where(live, fwd, 0.0)
            behind[col] += jnp.where(live, bwd, 0.0)
        return carry

    groups = (count + group - 1) // group
    lax.fori_loop(0, groups, step, 0)

    def drain(index, carry):
        tile_copy(index).wait()
        return carry

    lax.fori_loop(groups, 8, drain, 0)
    for part in range(2):
        ahead_ref[:, part * 256 : part * 256 + 256] = acc[part]
    for z in range(8):
        for part in range(4):
            rows = pl.ds(part * 64, 64)
            cols = pl.ds(part % 2 * 128, 128)
            send_ref[z, rows, :] = behind[(1 - my_half) * 16 + 2 * z + part // 2, :, cols].astype(bf16)
            keep_ref[z, rows, :] = behind[my_half * 16 + 2 * z + part // 2, :, cols]


def fold(msg_ref, out_ref):
    out_ref[...] = jnp.sum(msg_ref[...].astype(f32), axis=0)


def last_message(mine_ref, mate_ref, pot_ref, mate_pot_ref, keep_ref, mate_near_ref, out_ref):
    adjoint = (mine_ref[...] + mate_ref[...]).astype(bf16)
    upper = lax.axis_index("xhi") == 1
    pot = pot_ref[...].astype(f32)
    mate_pot = mate_pot_ref[...].astype(f32)
    first = jnp.where(upper, mate_pot, pot).astype(bf16)
    second = jnp.where(upper, pot, mate_pot).astype(bf16)
    for piece in range(8):
        out_ref[piece, 0:64, :] = adjoint
        out_ref[piece, 64:96, :] = first
        out_ref[piece, 96:128, :] = second
        out_ref[piece, 128:384, :] = (keep_ref[piece] + mate_near_ref[piece].astype(f32)).astype(bf16)


def finish(msg_ref, ahead_ref, skin_hbm, skout_hbm, resp_ref, sens_ref, skin_ref, skout_ref, sems):
    first = pltpu.make_async_copy(skin_hbm, skin_ref, sems.at[0])
    second = pltpu.make_async_copy(skout_hbm, skout_ref, sems.at[1])
    first.start()
    second.start()
    adjoint = jnp.concatenate(
        [
            jnp.concatenate([msg_ref[z, part * 8 : part * 8 + 8, :] for part in range(8)], axis=1)
            for z in range(8)
        ],
        axis=0,
    )
    packed = jnp.concatenate([msg_ref[r % 8, 64 + r // 8 * 32 : 96 + r // 8 * 32, :] for r in range(16)], axis=0)
    packed = packed.astype(f32).T.astype(bf16)
    near_sums = []
    for part in range(4):
        rows = slice(128 + part * 64, 192 + part * 64)
        value = msg_ref[0, rows, :].astype(f32)
        for source in range(1, 8):
            value = value + msg_ref[source, rows, :].astype(f32)
        near_sums.append(value)
    first.wait()
    sens_ref[...] = dot(adjoint, skin_ref[...]) + jnp.concatenate(near_sums, axis=1)
    second.wait()
    upper = jnp.concatenate([skout_ref[r * 64 : r * 64 + 32, :] for r in range(16)], axis=0)
    lower = jnp.concatenate([skout_ref[r * 64 + 32 : r * 64 + 64, :] for r in range(16)], axis=0)
    resp_ref[...] = ahead_ref[...] + dot(packed[:64], upper) + dot(packed[64:], lower)


def swap(value, axis):
    return lax.ppermute(value, axis, [(0, 1), (1, 0)])


def exchange(value, axes):
    return lax.all_to_all(value, axes, 0, 0, tiled=True)


def in_hbm(value):
    return pltpu.with_memory_space_constraint(value, pltpu.HBM)


def shift(value, step):
    return lax.ppermute(value, "z", [(i, (i + step) % 8) for i in range(8)])


def tie(*values):
    return lax.optimization_barrier(values)


def on_device(exc, loads, tiles, tile_rows, tile_cols, tile_count, skin, skout, trans):
    drive, low, msg = call(
        prepare,
        [((2, 64, 256), bf16), ((2, 64, 256), bf16), ((16, 96, 128), bf16)],
        [in_hbm(exc), in_hbm(loads), in_hbm(skin), in_hbm(skout)],
        specs=[hbm()] * 4,
        scratch=[pltpu.VMEM((64, 512), f32)] * 2
        + [pltpu.VMEM((1024, 512), bf16)] * 2
        + [pltpu.SemaphoreType.DMA((4,))],
        name="prepare",
    )
    mate = swap(drive, "xhi")
    (parts,) = call(
        split_translation,
        [((15, 128, 1024), bf16)],
        [in_hbm(trans)],
        specs=[hbm()],
        scratch=[pltpu.VMEM((15, 64, 1024), f32), pltpu.SemaphoreType.DMA((15,))],
        name="split_translation",
    )
    parts = in_hbm(parts)
    msg, mate, parts = tie(exchange(msg, ROWS), mate, parts)
    blocks = [pltpu.VMEM((8, 128, 1024), bf16), pltpu.SemaphoreType.DMA((8,))]
    copies, gradient, send = call(
        other_terms,
        [((16, 32, 128), bf16), ((128, 64), bf16), ((8, 64, 1024), f32)],
        [msg, parts],
        specs=[vmem(), hbm()],
        scratch=blocks,
        name="other_terms",
    )
    here = jnp.stack([drive, mate])
    up1, down1 = shift(here, 1), shift(here, -1)
    (own,) = call(
        own_terms,
        [((8, 64, 1024), bf16)],
        [gradient, swap(send, "core"), parts],
        specs=[vmem(), vmem(), hbm()],
        scratch=blocks,
        name="own_terms",
    )
    copies, up1, down1, own = tie(exchange(copies, ROWS), up1, down1, own)
    (both,) = call(pack, [((8, 2, 64, 1024), bf16)], [own, copies], name="pack")
    up2, down2 = shift(up1, 1), shift(down1, -1)
    up3, down3 = shift(up2, 1), shift(down2, -1)
    up4 = shift(up3, 1)
    ahead, send, keep = call(
        near,
        [((64, 512), f32), ((8, 256, 128), bf16), ((8, 256, 128), f32)],
        [tile_count, tile_rows, tile_cols, low, in_hbm(tiles)]
        + [in_hbm(piece) for piece in (here, up1, up2, up3, up4, down3, down2, down1)],
        specs=[smem(), smem(), smem(), vmem()] + [hbm()] * 9,
        scratch=[
            pltpu.VMEM((2, 64, 256), f32),
            pltpu.VMEM((32, 64, 256), f32),
            pltpu.VMEM((8, 2, 2, 64, 256), bf16),
            pltpu.VMEM((32, 256, 256), bf16),
            pltpu.SemaphoreType.DMA((8,)),
            pltpu.SemaphoreType.DMA((8,)),
        ],
        name="near",
    )
    both, ahead, send, keep = tie(exchange(both, FACE), ahead, send, keep)
    mate_near = swap(send, "xhi")
    adjoint, charges = call(
        unpack,
        [((8, 64, 128), bf16), ((8, 64, 1024), bf16)],
        [both],
        name="unpack",
    )
    others = swap(charges, "core")
    (potential,) = call(
        forward,
        [((32, 128), bf16)],
        [others, both, parts],
        specs=[vmem(), vmem(), hbm()],
        scratch=[pltpu.VMEM((16, 128, 1024), bf16), pltpu.SemaphoreType.DMA((16,))],
        name="forward",
    )
    mate_pot = swap(potential, "xhi")
    adjoint, mate_pot = tie(exchange(adjoint, "z"), mate_pot)
    (mine,) = call(fold, [((64, 128), f32)], [adjoint], name="fold")
    (last,) = call(
        last_message,
        [((8, 384, 128), bf16)],
        [mine, swap(mine, "xhi"), potential, mate_pot, keep, mate_near],
        name="last_message",
    )
    return tuple(
        call(
            finish,
            [((64, 512), f32), ((64, 512), f32)],
            [exchange(last, "z"), ahead, in_hbm(skin), in_hbm(skout)],
            specs=[vmem()] * 2 + [hbm()] * 2,
            scratch=[pltpu.VMEM((1024, 512), bf16)] * 2 + [pltpu.SemaphoreType.DMA((2,))],
            name="finish",
        )
    )


def solution(mesh):
    fine = Mesh(mesh.devices.reshape(2, 4, 2, 2, 8), BLK + ROWS)
    every = BLK + ROWS
    return jax.shard_map(
        on_device,
        mesh=fine,
        in_specs=(
            P(None, every),
            P(None, every),
            P(every, None, None),
            P(every),
            P(every),
            P(every),
            P(None, every),
            P(None, every),
            P(BLK, None, ROWS, None),
        ),
        out_specs=(P(None, every), P(None, every)),
        check_vma=False,
    )
```

```python
import jax
import jax.numpy as jnp
from jax import lax
from jax.experimental import pallas as pl
from jax.experimental.pallas import tpu as pltpu
from jax.sharding import Mesh
from jax.sharding import PartitionSpec as P

BLK = ("xlo", "y", "core")
ROWS = ("xhi", "z")
FACE = ("xlo", "y")
bf16 = jnp.bfloat16
f32 = jnp.float32
LAST = (((1,), (1,)), ((), ()))


def vmem():
    return pl.BlockSpec(memory_space=pltpu.VMEM)


def smem():
    return pl.BlockSpec(memory_space=pltpu.SMEM)


def hbm():
    return pl.BlockSpec(memory_space=pltpu.HBM)


def call(kernel, outs, args, specs=None, scratch=(), name=None):
    return pl.pallas_call(
        kernel,
        out_shape=[jax.ShapeDtypeStruct(s, d) for s, d in outs],
        in_specs=specs or [vmem()] * len(args),
        out_specs=[vmem()] * len(outs),
        scratch_shapes=list(scratch),
        compiler_params=pltpu.CompilerParams(vmem_limit_bytes=20 * 2**20),
        cost_estimate=pl.CostEstimate(flops=1000, bytes_accessed=1000, transcendentals=0),
        name=name,
    )(*args)


def split(value):
    high = value.astype(bf16)
    return high, (value - high.astype(f32)).astype(bf16)


def dot(a, b):
    return jnp.dot(a, b, preferred_element_type=f32)


def dot_last(a, b):
    return lax.dot_general(a, b, LAST, preferred_element_type=f32)


def join_pieces(ref, first):
    rows = []
    for band in range(8):
        blocks = [
            ref[band * 2 + half, first + part * 8 : first + part * 8 + 8, :]
            for half in range(2)
            for part in range(4)
        ]
        rows.append(jnp.concatenate(blocks, axis=1))
    return jnp.concatenate(rows, axis=0)


def prepare(exc_hbm, loads_hbm, skin_hbm, skout_hbm, drive_ref, low_ref, msg_ref, exc, loads, skin, skout, sems):
    pairs = ((exc_hbm, exc), (skin_hbm, skin), (loads_hbm, loads), (skout_hbm, skout))
    copies = [pltpu.make_async_copy(src, dst, sems.at[i]) for i, (src, dst) in enumerate(pairs)]
    for copy in copies:
        copy.start()
    copies[0].wait()
    drive = exc[...].astype(bf16)
    for part in range(2):
        drive_ref[part] = drive[:, part * 256 : part * 256 + 256]
    copies[1].wait()
    charges = dot_last(drive, skin[...])
    for piece in range(16):
        row = piece // 2 * 8
        for part in range(4):
            col = piece % 2 * 512 + part * 128
            msg_ref[piece, part * 8 : part * 8 + 8, :] = charges[row : row + 8, col : col + 128].astype(bf16)
    copies[2].wait()
    low = loads[...].astype(bf16)
    for part in range(2):
        low_ref[part] = low[:, part * 256 : part * 256 + 256]
    twice = jnp.concatenate([low, low], axis=0)
    copies[3].wait()
    gradient = dot_last(skout[...], twice)
    left = lax.broadcasted_iota(jnp.int32, (32, 128), 1) < 64
    for piece in range(16):
        k = piece * 64
        high, rest = split(jnp.where(left, gradient[k : k + 32], gradient[k + 32 : k + 64]))
        msg_ref[piece, 32:64, :] = high
        msg_ref[piece, 64:96, :] = rest


def split_translation(trans_hbm, out_ref, blocks, sems):
    copies = [pltpu.make_async_copy(trans_hbm.at[0, d], blocks.at[d], sems.at[d]) for d in range(15)]
    for copy in copies:
        copy.start()
    for d in range(15):
        copies[d].wait()
        high, low = split(blocks[d])
        out_ref[d, :64] = high
        out_ref[d, 64:] = low


def lags(parity):
    cluster = lax.axis_index(BLK)
    return [lax.rem(cluster - (2 * q + parity) + 16, 16) for q in range(8)]


def fetch(parts_hbm, blocks, sems, lag):
    copies = []
    for index, behind in enumerate(lag):
        source = parts_hbm.at[jnp.maximum(behind - 1, 0)]
        copies.append(pltpu.make_async_copy(source, blocks.at[index], sems.at[index]))
        copies[index].start()
    return copies


def term(both, block):
    pair = dot(both, block[:64])
    return pair[:64] + pair[64:] + dot(both[:64], block[64:])


def shares(msg_ref, copies_ref, grad_ref):
    share = jnp.sum(msg_ref[:, 0:32, :].astype(f32), axis=0).astype(bf16)
    for piece in range(16):
        copies_ref[piece] = share
    packed = jnp.sum(msg_ref[:, 32:64, :].astype(f32) + msg_ref[:, 64:96, :].astype(f32), axis=0)
    gradient = jnp.concatenate([packed, pltpu.roll(packed, 64, 1)], axis=0)
    high, low = split(gradient.T[:64])
    grad_ref[:64] = high
    grad_ref[64:] = low


def other_terms(grad_ref, parts_hbm, send_ref, blocks, sems):
    fetched = fetch(parts_hbm, blocks, sems, lags(1 - lax.axis_index("core")))
    both = grad_ref[...]
    for index in range(8):
        fetched[index].wait()
        send_ref[index] = term(both, blocks[index])


def own_terms(grad_ref, came_ref, parts_hbm, out_ref, blocks, sems):
    lag = lags(lax.axis_index("core"))
    fetched = fetch(parts_hbm, blocks, sems, lag)
    both = grad_ref[...]
    for index in range(8):
        fetched[index].wait()
        value = jnp.where(lag[index] == 0, 0.0, term(both, blocks[index]))
        out_ref[index] = (value + came_ref[index]).astype(bf16)


def pack(own_ref, pieces_ref, out_ref):
    charges = join_pieces(pieces_ref, 0)
    for q in range(8):
        out_ref[q, 0] = own_ref[q]
        out_ref[q, 1] = charges


def unpack(came_ref, msg_ref, charges_ref):
    total = came_ref[0, 0].astype(f32)
    charges_ref[0] = came_ref[0, 1]
    for q in range(1, 8):
        total = total + came_ref[q, 0].astype(f32)
        charges_ref[q] = came_ref[q, 1]
    for piece in range(8):
        for part in range(8):
            msg_ref[piece, part * 8 : part * 8 + 8, :] = total[
                piece * 8 : piece * 8 + 8, part * 128 : part * 128 + 128
            ].astype(bf16)


def forward(other_ref, came_ref, parts_hbm, pot_ref, blocks, sems):
    core = lax.axis_index("core")
    lag = lags(1 - core) + lags(core)
    fetched = fetch(parts_hbm, blocks, sems, lag)
    total = jnp.zeros((64, 64), f32)
    for index in range(16):
        charges = other_ref[index] if index < 8 else came_ref[index - 8, 1]
        fetched[index].wait()
        pair = dot_last(blocks[index], charges)
        total = total + jnp.where(lag[index] == 0, 0.0, pair[:64] + pair[64:])
    pot_ref[...] = jnp.concatenate([total[:32], total[32:]], axis=1).astype(bf16)


def near(count_ref, rows_ref, cols_ref, low_ref, tiles_hbm, *refs):
    pieces, refs = refs[:8], refs[8:]
    (ahead_ref, far_up, far_down), refs = refs[:3], refs[3:]
    own_refs, (acc, behind, drives, tiles_ref, tile_sems, piece_sems) = refs[:6], refs[6:]

    def tile_copy(index):
        span = pl.ds(index * 4, 4)
        return pltpu.make_async_copy(tiles_hbm.at[span], tiles_ref.at[span], tile_sems.at[index])

    arriving = [
        pltpu.make_async_copy(pieces[index], drives.at[index], piece_sems.at[index]) for index in range(8)
    ]
    for copy in arriving:
        copy.start()
    for index in range(8):
        tile_copy(index).start()
    acc[...] = jnp.zeros_like(acc)
    behind[...] = jnp.zeros_like(behind)
    for copy in arriving:
        copy.wait()
    count = count_ref[0]
    my_z = lax.axis_index("z")
    my_half = lax.axis_index("xhi")
    group = 4

    def step(index, carry):
        tile_copy(index).wait()
        results = []
        for part in range(group):
            slot = index * group + part
            row = rows_ref[slot]
            col = cols_ref[slot]
            owner = col // 2
            hops = lax.rem(my_z - lax.rem(owner, 8) + 8, 8)
            side = lax.rem(owner // 8 + my_half, 2)
            tile = tiles_ref[slot]
            fwd = dot_last(drives[hops, side, lax.rem(col, 2)], tile)
            bwd = dot(low_ref[row], tile)
            results.append((slot < count, row, col, fwd, bwd))
        for live, row, col, fwd, bwd in results:
            acc[row] += jnp.where(live, fwd, 0.0)
            behind[col] += jnp.where(live, bwd, 0.0)
        return carry

    groups = (count + group - 1) // group
    lax.fori_loop(0, groups, step, 0)

    def drain(index, carry):
        tile_copy(index).wait()
        return carry

    lax.fori_loop(groups, 8, drain, 0)
    for part in range(2):
        ahead_ref[:, part * 256 : part * 256 + 256] = acc[part]
    for ref, offset in zip((far_up, far_down, *own_refs), (4, -3, 3, -2, 2, -1, 1, 0)):
        owner_z = lax.rem(my_z + offset + 8, 8)
        for half in range(2):
            for part in range(4):
                value = behind[half * 16 + 2 * owner_z + part // 2, :, part % 2 * 128 : part % 2 * 128 + 128]
                rows = slice(half * 256 + part * 64, half * 256 + part * 64 + 64)
                ref[rows, :] = value.astype(ref.dtype)


def add_two(up_ref, own_up_ref, down_ref, own_down_ref, up_out, down_out):
    up_out[...] = (up_ref[...].astype(f32) + own_up_ref[...]).astype(bf16)
    down_out[...] = (down_ref[...].astype(f32) + own_down_ref[...]).astype(bf16)


def add_last(up_ref, own_up_ref, down_ref, own_ref, up_out, sum_out):
    up_out[...] = (up_ref[...].astype(f32) + own_up_ref[...]).astype(bf16)
    sum_out[...] = down_ref[...].astype(f32) + own_ref[...]


def close_ring(up_ref, sum_ref, keep_ref, send_ref):
    mine = pl.multiple_of(lax.axis_index("xhi") * 256, 256)
    mates = 256 - mine
    keep_ref[...] = up_ref[pl.ds(mine, 256), :].astype(f32) + sum_ref[pl.ds(mine, 256), :]
    send_ref[...] = up_ref[pl.ds(mates, 256), :].astype(f32) + sum_ref[pl.ds(mates, 256), :]


def fold(msg_ref, out_ref):
    out_ref[...] = jnp.sum(msg_ref[...].astype(f32), axis=0)


def last_message(mine_ref, mate_ref, pot_ref, mate_pot_ref, out_ref):
    adjoint = (mine_ref[...] + mate_ref[...]).astype(bf16)
    upper = lax.axis_index("xhi") == 1
    pot = pot_ref[...].astype(f32)
    mate_pot = mate_pot_ref[...].astype(f32)
    first = jnp.where(upper, mate_pot, pot).astype(bf16)
    second = jnp.where(upper, pot, mate_pot).astype(bf16)
    for piece in range(8):
        out_ref[piece, 0:64, :] = adjoint
        out_ref[piece, 64:96, :] = first
        out_ref[piece, 96:128, :] = second


def finish(msg_ref, ahead_ref, keep_ref, mate_ref, skin_hbm, skout_hbm, resp_ref, sens_ref, skin_ref, skout_ref, sems):
    first = pltpu.make_async_copy(skin_hbm, skin_ref, sems.at[0])
    second = pltpu.make_async_copy(skout_hbm, skout_ref, sems.at[1])
    first.start()
    second.start()
    adjoint = jnp.concatenate(
        [
            jnp.concatenate([msg_ref[z, part * 8 : part * 8 + 8, :] for part in range(8)], axis=1)
            for z in range(8)
        ],
        axis=0,
    )
    packed = jnp.concatenate([msg_ref[r % 8, 64 + r // 8 * 32 : 96 + r // 8 * 32, :] for r in range(16)], axis=0)
    packed = packed.astype(f32).T.astype(bf16)
    near_sum = keep_ref[...] + mate_ref[...]
    first.wait()
    sens_ref[...] = dot(adjoint, skin_ref[...]) + jnp.concatenate(
        [near_sum[part * 64 : part * 64 + 64] for part in range(4)], axis=1
    )
    second.wait()
    upper = jnp.concatenate([skout_ref[r * 64 : r * 64 + 32, :] for r in range(16)], axis=0)
    lower = jnp.concatenate([skout_ref[r * 64 + 32 : r * 64 + 64, :] for r in range(16)], axis=0)
    resp_ref[...] = ahead_ref[...] + dot(packed[:64], upper) + dot(packed[64:], lower)


def swap(value, axis):
    return lax.ppermute(value, axis, [(0, 1), (1, 0)])


def exchange(value, axes):
    return lax.all_to_all(value, axes, 0, 0, tiled=True)


def in_hbm(value):
    return pltpu.with_memory_space_constraint(value, pltpu.HBM)


def shift(value, step):
    return lax.ppermute(value, "z", [(i, (i + step) % 8) for i in range(8)])


def tie(*values):
    return lax.optimization_barrier(values)


def on_device(exc, loads, tiles, tile_rows, tile_cols, tile_count, skin, skout, trans):
    drive, low, msg = call(
        prepare,
        [((2, 64, 256), bf16), ((2, 64, 256), bf16), ((16, 96, 128), bf16)],
        [in_hbm(exc), in_hbm(loads), in_hbm(skin), in_hbm(skout)],
        specs=[hbm()] * 4,
        scratch=[pltpu.VMEM((64, 512), f32)] * 2
        + [pltpu.VMEM((1024, 512), bf16)] * 2
        + [pltpu.SemaphoreType.DMA((4,))],
        name="prepare",
    )
    mate = swap(drive, "xhi")
    (parts,) = call(
        split_translation,
        [((15, 128, 1024), bf16)],
        [in_hbm(trans)],
        specs=[hbm()],
        scratch=[pltpu.VMEM((15, 64, 1024), f32), pltpu.SemaphoreType.DMA((15,))],
        name="split_translation",
    )
    parts = in_hbm(parts)
    here = jnp.stack([drive, mate])
    up1, down1 = shift(here, 1), shift(here, -1)
    msg, up1, down1, parts = tie(exchange(msg, ROWS), up1, down1, parts)
    copies, gradient = call(
        shares, [((16, 32, 128), bf16), ((128, 64), bf16)], [msg], name="shares"
    )
    blocks = [pltpu.VMEM((8, 128, 1024), bf16), pltpu.SemaphoreType.DMA((8,))]
    (send,) = call(
        other_terms,
        [((8, 64, 1024), f32)],
        [gradient, parts],
        specs=[vmem(), hbm()],
        scratch=blocks,
        name="other_terms",
    )
    (own,) = call(
        own_terms,
        [((8, 64, 1024), bf16)],
        [gradient, swap(send, "core"), parts],
        specs=[vmem(), vmem(), hbm()],
        scratch=blocks,
        name="own_terms",
    )
    up2, down2 = shift(up1, 1), shift(down1, -1)
    up3, down3 = shift(up2, 1), shift(down2, -1)
    up4 = shift(up3, 1)
    copies, up4, down3, own = tie(exchange(copies, ROWS), up4, down3, own)
    (both,) = call(pack, [((8, 2, 64, 1024), bf16)], [own, copies], name="pack")
    chunk = (512, 128)
    ahead, ring_up, ring_down, own3, own_2, own2, own_1, own1, own0 = call(
        near,
        [((64, 512), f32), (chunk, bf16), (chunk, bf16)] + [(chunk, f32)] * 6,
        [tile_count, tile_rows, tile_cols, low, in_hbm(tiles)]
        + [in_hbm(piece) for piece in (here, up1, up2, up3, up4, down3, down2, down1)],
        specs=[smem(), smem(), smem(), vmem()] + [hbm()] * 9,
        scratch=[
            pltpu.VMEM((2, 64, 256), f32),
            pltpu.VMEM((32, 64, 256), f32),
            pltpu.VMEM((8, 2, 2, 64, 256), bf16),
            pltpu.VMEM((32, 256, 256), bf16),
            pltpu.SemaphoreType.DMA((8,)),
            pltpu.SemaphoreType.DMA((8,)),
        ],
        name="near",
    )
    for own_up, own_down in ((own3, own_2), (own2, own_1)):
        ring_up, ring_down = call(
            add_two,
            [(chunk, bf16)] * 2,
            [shift(ring_up, 1), own_up, shift(ring_down, -1), own_down],
            name="add_two",
        )
    ring_up, near_sum = call(
        add_last,
        [(chunk, bf16), (chunk, f32)],
        [shift(ring_up, 1), own1, shift(ring_down, -1), own0],
        name="add_last",
    )
    ring_up = shift(ring_up, 1)
    both, ahead, ring_up, near_sum = tie(exchange(both, FACE), ahead, ring_up, near_sum)
    keep, send = call(close_ring, [((256, 128), f32)] * 2, [ring_up, near_sum], name="close_ring")
    mate_near = swap(send, "xhi")
    adjoint, charges = call(
        unpack,
        [((8, 64, 128), bf16), ((8, 64, 1024), bf16)],
        [both],
        name="unpack",
    )
    others = swap(charges, "core")
    (potential,) = call(
        forward,
        [((32, 128), bf16)],
        [others, both, parts],
        specs=[vmem(), vmem(), hbm()],
        scratch=[pltpu.VMEM((16, 128, 1024), bf16), pltpu.SemaphoreType.DMA((16,))],
        name="forward",
    )
    mate_pot = swap(potential, "xhi")
    adjoint, mate_pot, mate_near = tie(exchange(adjoint, "z"), mate_pot, mate_near)
    (mine,) = call(fold, [((64, 128), f32)], [adjoint], name="fold")
    (last,) = call(
        last_message,
        [((8, 128, 128), bf16)],
        [mine, swap(mine, "xhi"), potential, mate_pot],
        name="last_message",
    )
    return tuple(
        call(
            finish,
            [((64, 512), f32), ((64, 512), f32)],
            [exchange(last, "z"), ahead, keep, mate_near, in_hbm(skin), in_hbm(skout)],
            specs=[vmem()] * 4 + [hbm()] * 2,
            scratch=[pltpu.VMEM((1024, 512), bf16)] * 2 + [pltpu.SemaphoreType.DMA((2,))],
            name="finish",
        )
    )


def solution(mesh):
    fine = Mesh(mesh.devices.reshape(2, 4, 2, 2, 8), BLK + ROWS)
    every = BLK + ROWS
    return jax.shard_map(
        on_device,
        mesh=fine,
        in_specs=(
            P(None, every),
            P(None, every),
            P(every, None, None),
            P(every),
            P(every),
            P(every),
            P(None, every),
            P(None, every),
            P(BLK, None, ROWS, None),
        ),
        out_specs=(P(None, every), P(None, every)),
        check_vma=False,
    )
```

```python
import jax
import jax.numpy as jnp
from jax import lax
from jax.experimental import pallas as pl
from jax.experimental.pallas import tpu as pltpu
from jax.sharding import Mesh
from jax.sharding import PartitionSpec as P

BLK = ("xlo", "y", "core")
ROWS = ("xhi", "z")
FACE = ("xlo", "y")
bf16 = jnp.bfloat16
f32 = jnp.float32
LAST = (((1,), (1,)), ((), ()))


def vmem():
    return pl.BlockSpec(memory_space=pltpu.VMEM)


def smem():
    return pl.BlockSpec(memory_space=pltpu.SMEM)


def hbm():
    return pl.BlockSpec(memory_space=pltpu.HBM)


def call(kernel, outs, args, specs=None, out_specs=None, scratch=(), alias=None, name=None):
    return pl.pallas_call(
        kernel,
        out_shape=[jax.ShapeDtypeStruct(s, d) for s, d in outs],
        in_specs=specs or [vmem()] * len(args),
        out_specs=out_specs or [vmem()] * len(outs),
        scratch_shapes=list(scratch),
        compiler_params=pltpu.CompilerParams(vmem_limit_bytes=20 * 2**20),
        cost_estimate=pl.CostEstimate(flops=1000, bytes_accessed=1000, transcendentals=0),
        name=name,
        input_output_aliases=alias or {},
    )(*args)


def split(value):
    high = value.astype(bf16)
    return high, (value - high.astype(f32)).astype(bf16)


def dot(a, b):
    return jnp.dot(a, b, preferred_element_type=f32)


def dot_last(a, b):
    return lax.dot_general(a, b, LAST, preferred_element_type=f32)


def join_pieces(ref, first):
    rows = []
    for band in range(8):
        blocks = [
            ref[band * 2 + half, first + part * 8 : first + part * 8 + 8, :]
            for half in range(2)
            for part in range(4)
        ]
        rows.append(jnp.concatenate(blocks, axis=1))
    return jnp.concatenate(rows, axis=0)


def prepare(exc_hbm, loads_hbm, skin_hbm, skout_hbm, drive_ref, low_ref, msg_ref, exc, loads, skin, skout, sems):
    pairs = ((exc_hbm, exc), (skin_hbm, skin), (loads_hbm, loads), (skout_hbm, skout))
    copies = [pltpu.make_async_copy(src, dst, sems.at[i]) for i, (src, dst) in enumerate(pairs)]
    for copy in copies:
        copy.start()
    copies[0].wait()
    drive = exc[...].astype(bf16)
    for part in range(2):
        drive_ref[part] = drive[:, part * 256 : part * 256 + 256]
    copies[1].wait()
    charges = dot_last(drive, skin[...])
    for piece in range(16):
        row = piece // 2 * 8
        for part in range(4):
            col = piece % 2 * 512 + part * 128
            msg_ref[piece, part * 8 : part * 8 + 8, :] = charges[row : row + 8, col : col + 128].astype(bf16)
    copies[2].wait()
    low = loads[...].astype(bf16)
    for part in range(2):
        low_ref[part] = low[:, part * 256 : part * 256 + 256]
    twice = jnp.concatenate([low, low], axis=0)
    copies[3].wait()
    gradient = dot_last(skout[...], twice)
    left = lax.broadcasted_iota(jnp.int32, (32, 128), 1) < 64
    for piece in range(16):
        k = piece * 64
        high, rest = split(jnp.where(left, gradient[k : k + 32], gradient[k + 32 : k + 64]))
        msg_ref[piece, 32:64, :] = high
        msg_ref[piece, 64:96, :] = rest


def split_translation(trans_hbm, out_ref, blocks, sems):
    copies = [pltpu.make_async_copy(trans_hbm.at[0, d], blocks.at[d], sems.at[d]) for d in range(15)]
    for copy in copies:
        copy.start()
    for d in range(15):
        copies[d].wait()
        high, low = split(blocks[d])
        out_ref[d, :64] = high
        out_ref[d, 64:] = low


def lags(parity):
    cluster = lax.axis_index(BLK)
    return [lax.rem(cluster - (2 * q + parity) + 16, 16) for q in range(8)]


def fetch(parts_hbm, blocks, sems, lag):
    copies = []
    for index, behind in enumerate(lag):
        source = parts_hbm.at[jnp.maximum(behind - 1, 0)]
        copies.append(pltpu.make_async_copy(source, blocks.at[index], sems.at[index]))
        copies[index].start()
    return copies


def term(both, block):
    pair = dot(both, block[:64])
    return pair[:64] + pair[64:] + dot(both[:64], block[64:])


def shares(msg_ref, copies_ref, grad_ref):
    share = jnp.sum(msg_ref[:, 0:32, :].astype(f32), axis=0).astype(bf16)
    for piece in range(16):
        copies_ref[piece] = share
    packed = jnp.sum(msg_ref[:, 32:64, :].astype(f32) + msg_ref[:, 64:96, :].astype(f32), axis=0)
    gradient = jnp.concatenate([packed, pltpu.roll(packed, 64, 1)], axis=0)
    high, low = split(gradient.T[:64])
    grad_ref[:64] = high
    grad_ref[64:] = low


def other_terms(grad_ref, parts_hbm, send_ref, blocks, sems):
    fetched = fetch(parts_hbm, blocks, sems, lags(1 - lax.axis_index("core")))
    both = grad_ref[...]
    for index in range(8):
        fetched[index].wait()
        send_ref[index] = term(both, blocks[index])


def own_terms(grad_ref, came_ref, parts_hbm, out_ref, blocks, sems):
    lag = lags(lax.axis_index("core"))
    fetched = fetch(parts_hbm, blocks, sems, lag)
    both = grad_ref[...]
    for index in range(8):
        fetched[index].wait()
        value = jnp.where(lag[index] == 0, 0.0, term(both, blocks[index]))
        out_ref[index] = (value + came_ref[index]).astype(bf16)


def pack(own_ref, pieces_ref, out_ref):
    charges = join_pieces(pieces_ref, 0)
    for q in range(8):
        out_ref[q, 0] = own_ref[q]
        out_ref[q, 1] = charges


def unpack(came_ref, near_hbm, msg_hbm, charges_ref, rows, sem):
    del near_hbm
    total = came_ref[0, 0].astype(f32)
    for q in range(1, 8):
        total = total + came_ref[q, 0].astype(f32)
    for piece in range(8):
        for part in range(8):
            rows[piece, part * 8 : part * 8 + 8, :] = total[
                piece * 8 : piece * 8 + 8, part * 128 : part * 128 + 128
            ].astype(bf16)
    copy = pltpu.make_async_copy(rows, msg_hbm.at[:, pl.ds(512, 64), :], sem)
    copy.start()
    for q in range(8):
        charges_ref[q] = came_ref[q, 1]
    copy.wait()


def forward(other_ref, came_ref, parts_hbm, pot_ref, blocks, sems):
    core = lax.axis_index("core")
    lag = lags(1 - core) + lags(core)
    fetched = fetch(parts_hbm, blocks, sems, lag)
    total = jnp.zeros((64, 64), f32)
    for index in range(16):
        charges = other_ref[index] if index < 8 else came_ref[index - 8, 1]
        fetched[index].wait()
        pair = dot_last(blocks[index], charges)
        total = total + jnp.where(lag[index] == 0, 0.0, pair[:64] + pair[64:])
    pot_ref[...] = jnp.concatenate([total[:32], total[32:]], axis=1).astype(bf16)


def near(count_ref, rows_ref, cols_ref, low_ref, tiles_hbm, *refs):
    pieces, refs = refs[:8], refs[8:]
    ahead_ref, msg_ref, acc, behind, drives, tiles_ref, tile_sems, piece_sems = refs

    def tile_copy(index):
        span = pl.ds(index * 4, 4)
        return pltpu.make_async_copy(tiles_hbm.at[span], tiles_ref.at[span], tile_sems.at[index])

    arriving = [
        pltpu.make_async_copy(pieces[index], drives.at[index], piece_sems.at[index]) for index in range(8)
    ]
    for copy in arriving:
        copy.start()
    for index in range(8):
        tile_copy(index).start()
    acc[...] = jnp.zeros_like(acc)
    behind[...] = jnp.zeros_like(behind)
    for copy in arriving:
        copy.wait()
    count = count_ref[0]
    my_z = lax.axis_index("z")
    my_half = lax.axis_index("xhi")
    group = 4

    def step(index, carry):
        tile_copy(index).wait()
        results = []
        for part in range(group):
            slot = index * group + part
            row = rows_ref[slot]
            col = cols_ref[slot]
            owner = col // 2
            hops = lax.rem(my_z - lax.rem(owner, 8) + 8, 8)
            side = lax.rem(owner // 8 + my_half, 2)
            tile = tiles_ref[slot]
            fwd = dot_last(drives[hops, side, lax.rem(col, 2)], tile)
            bwd = dot(low_ref[row], tile)
            results.append((slot < count, row, col, fwd, bwd))
        for live, row, col, fwd, bwd in results:
            acc[row] += jnp.where(live, fwd, 0.0)
            behind[col] += jnp.where(live, bwd, 0.0)
        return carry

    groups = (count + group - 1) // group
    lax.fori_loop(0, groups, step, 0)

    def drain(index, carry):
        tile_copy(index).wait()
        return carry

    lax.fori_loop(groups, 8, drain, 0)
    for part in range(2):
        ahead_ref[:, part * 256 : part * 256 + 256] = acc[part]
    for z in range(8):
        for half in range(2):
            for part in range(4):
                rows = slice(half * 256 + part * 64, half * 256 + part * 64 + 64)
                value = behind[half * 16 + 2 * z + part // 2, :, part % 2 * 128 : part % 2 * 128 + 128]
                msg_ref[z, rows, :] = value.astype(bf16)


def fold(msg_ref, out_ref):
    out_ref[...] = jnp.sum(msg_ref[:, 512:576, :].astype(f32), axis=0)


def fold_near(msg_ref, keep_ref, send_ref):
    mine = pl.multiple_of(lax.axis_index("xhi") * 256, 256)
    for ref, first in ((keep_ref, mine), (send_ref, 256 - mine)):
        value = msg_ref[0, pl.ds(first, 256), :].astype(f32)
        for source in range(1, 8):
            value = value + msg_ref[source, pl.ds(first, 256), :].astype(f32)
        ref[...] = value


def stage(skin_hbm, skout_hbm, skin_ref, skout_ref, sems):
    first = pltpu.make_async_copy(skin_hbm, skin_ref, sems.at[0])
    second = pltpu.make_async_copy(skout_hbm, skout_ref, sems.at[1])
    first.start()
    second.start()
    first.wait()
    second.wait()


def last_message(mine_ref, mate_ref, pot_ref, mate_pot_ref, out_ref):
    adjoint = (mine_ref[...] + mate_ref[...]).astype(bf16)
    upper = lax.axis_index("xhi") == 1
    pot = pot_ref[...].astype(f32)
    mate_pot = mate_pot_ref[...].astype(f32)
    first = jnp.where(upper, mate_pot, pot).astype(bf16)
    second = jnp.where(upper, pot, mate_pot).astype(bf16)
    for piece in range(8):
        out_ref[piece, 0:64, :] = adjoint
        out_ref[piece, 64:96, :] = first
        out_ref[piece, 96:128, :] = second


def finish(msg_ref, ahead_ref, keep_ref, mate_ref, skin_ref, skout_ref, resp_ref, sens_ref):
    adjoint = jnp.concatenate(
        [
            jnp.concatenate([msg_ref[z, part * 8 : part * 8 + 8, :] for part in range(8)], axis=1)
            for z in range(8)
        ],
        axis=0,
    )
    packed = jnp.concatenate([msg_ref[r % 8, 64 + r // 8 * 32 : 96 + r // 8 * 32, :] for r in range(16)], axis=0)
    packed = packed.astype(f32).T.astype(bf16)
    near_sum = keep_ref[...] + mate_ref[...]
    sens_ref[...] = dot(adjoint, skin_ref[...]) + jnp.concatenate(
        [near_sum[part * 64 : part * 64 + 64] for part in range(4)], axis=1
    )
    upper = jnp.concatenate([skout_ref[r * 64 : r * 64 + 32, :] for r in range(16)], axis=0)
    lower = jnp.concatenate([skout_ref[r * 64 + 32 : r * 64 + 64, :] for r in range(16)], axis=0)
    resp_ref[...] = ahead_ref[...] + dot(packed[:64], upper) + dot(packed[64:], lower)


def swap(value, axis):
    return lax.ppermute(value, axis, [(0, 1), (1, 0)])


def exchange(value, axes):
    return lax.all_to_all(value, axes, 0, 0, tiled=True)


def in_hbm(value):
    return pltpu.with_memory_space_constraint(value, pltpu.HBM)


def shift(value, step):
    return lax.ppermute(value, "z", [(i, (i + step) % 8) for i in range(8)])


def tie(*values):
    return lax.optimization_barrier(values)


def on_device(exc, loads, tiles, tile_rows, tile_cols, tile_count, skin, skout, trans):
    drive, low, msg = call(
        prepare,
        [((2, 64, 256), bf16), ((2, 64, 256), bf16), ((16, 96, 128), bf16)],
        [in_hbm(exc), in_hbm(loads), in_hbm(skin), in_hbm(skout)],
        specs=[hbm()] * 4,
        scratch=[pltpu.VMEM((64, 512), f32)] * 2
        + [pltpu.VMEM((1024, 512), bf16)] * 2
        + [pltpu.SemaphoreType.DMA((4,))],
        name="prepare",
    )
    mate = swap(drive, "xhi")
    (parts,) = call(
        split_translation,
        [((15, 128, 1024), bf16)],
        [in_hbm(trans)],
        specs=[hbm()],
        scratch=[pltpu.VMEM((15, 64, 1024), f32), pltpu.SemaphoreType.DMA((15,))],
        name="split_translation",
    )
    parts = in_hbm(parts)
    here = jnp.stack([drive, mate])
    up1, down1 = shift(here, 1), shift(here, -1)
    msg, up1, down1, parts = tie(exchange(msg, ROWS), up1, down1, parts)
    copies, gradient = call(
        shares, [((16, 32, 128), bf16), ((128, 64), bf16)], [msg], name="shares"
    )
    blocks = [pltpu.VMEM((8, 128, 1024), bf16), pltpu.SemaphoreType.DMA((8,))]
    (send,) = call(
        other_terms,
        [((8, 64, 1024), f32)],
        [gradient, parts],
        specs=[vmem(), hbm()],
        scratch=blocks,
        name="other_terms",
    )
    (own,) = call(
        own_terms,
        [((8, 64, 1024), bf16)],
        [gradient, swap(send, "core"), parts],
        specs=[vmem(), vmem(), hbm()],
        scratch=blocks,
        name="own_terms",
    )
    copies, own = tie(exchange(copies, ROWS), own)
    (both,) = call(pack, [((8, 2, 64, 1024), bf16)], [own, copies], name="pack")
    up2, down2 = shift(up1, 1), shift(down1, -1)
    up3, down3 = shift(up2, 1), shift(down2, -1)
    up4 = shift(up3, 1)
    ahead, behind = call(
        near,
        [((64, 512), f32), ((8, 576, 128), bf16)],
        [tile_count, tile_rows, tile_cols, low, in_hbm(tiles)]
        + [in_hbm(piece) for piece in (here, up1, up2, up3, up4, down3, down2, down1)],
        specs=[smem(), smem(), smem(), vmem()] + [hbm()] * 9,
        scratch=[
            pltpu.VMEM((2, 64, 256), f32),
            pltpu.VMEM((32, 64, 256), f32),
            pltpu.VMEM((8, 2, 2, 64, 256), bf16),
            pltpu.VMEM((32, 256, 256), bf16),
            pltpu.SemaphoreType.DMA((8,)),
            pltpu.SemaphoreType.DMA((8,)),
        ],
        name="near",
    )
    behind = in_hbm(behind)
    both, ahead, behind = tie(exchange(both, FACE), ahead, behind)
    behind, charges = call(
        unpack,
        [((8, 576, 128), bf16), ((8, 64, 1024), bf16)],
        [both, behind],
        specs=[vmem(), hbm()],
        out_specs=[hbm(), vmem()],
        scratch=[pltpu.VMEM((8, 64, 128), bf16), pltpu.SemaphoreType.DMA],
        alias={1: 0},
        name="unpack",
    )
    others = swap(charges, "core")
    (potential,) = call(
        forward,
        [((32, 128), bf16)],
        [others, both, parts],
        specs=[vmem(), vmem(), hbm()],
        scratch=[pltpu.VMEM((16, 128, 1024), bf16), pltpu.SemaphoreType.DMA((16,))],
        name="forward",
    )
    mate_pot = swap(potential, "xhi")
    behind, mate_pot = tie(exchange(behind, "z"), mate_pot)
    (mine,) = call(fold, [((64, 128), f32)], [behind], name="fold")
    (last,) = call(
        last_message,
        [((8, 128, 128), bf16)],
        [mine, swap(mine, "xhi"), potential, mate_pot],
        name="last_message",
    )
    keep, send = call(fold_near, [((256, 128), f32)] * 2, [behind], name="fold_near")
    mate_near = swap(send, "xhi")
    staged = call(
        stage,
        [((1024, 512), bf16)] * 2,
        [in_hbm(skin), in_hbm(skout)],
        specs=[hbm()] * 2,
        scratch=[pltpu.SemaphoreType.DMA((2,))],
        name="stage",
    )
    last, mate_near, *staged = tie(exchange(last, "z"), mate_near, *staged)
    return tuple(
        call(
            finish,
            [((64, 512), f32), ((64, 512), f32)],
            [last, ahead, keep, mate_near, *staged],
            name="finish",
        )
    )


def solution(mesh):
    fine = Mesh(mesh.devices.reshape(2, 4, 2, 2, 8), BLK + ROWS)
    every = BLK + ROWS
    return jax.shard_map(
        on_device,
        mesh=fine,
        in_specs=(
            P(None, every),
            P(None, every),
            P(every, None, None),
            P(every),
            P(every),
            P(every),
            P(None, every),
            P(None, every),
            P(BLK, None, ROWS, None),
        ),
        out_specs=(P(None, every), P(None, every)),
        check_vma=False,
    )
```

```python
import jax
import jax.numpy as jnp
from jax import lax
from jax.experimental import pallas as pl
from jax.experimental.pallas import tpu as pltpu
from jax.sharding import Mesh
from jax.sharding import PartitionSpec as P

BLK = ("xlo", "y", "core")
ROWS = ("xhi", "z")
FACE = ("xlo", "y")
bf16 = jnp.bfloat16
f32 = jnp.float32
LAST = (((1,), (1,)), ((), ()))


def vmem():
    return pl.BlockSpec(memory_space=pltpu.VMEM)


def smem():
    return pl.BlockSpec(memory_space=pltpu.SMEM)


def hbm():
    return pl.BlockSpec(memory_space=pltpu.HBM)


def call(kernel, outs, args, specs=None, scratch=(), name=None):
    return pl.pallas_call(
        kernel,
        out_shape=[jax.ShapeDtypeStruct(s, d) for s, d in outs],
        in_specs=specs or [vmem()] * len(args),
        out_specs=[vmem()] * len(outs),
        scratch_shapes=list(scratch),
        compiler_params=pltpu.CompilerParams(vmem_limit_bytes=20 * 2**20),
        cost_estimate=pl.CostEstimate(flops=1000, bytes_accessed=1000, transcendentals=0),
        name=name,
    )(*args)


def split(value):
    high = value.astype(bf16)
    return high, (value - high.astype(f32)).astype(bf16)


def dot(a, b):
    return jnp.dot(a, b, preferred_element_type=f32)


def dot_last(a, b):
    return lax.dot_general(a, b, LAST, preferred_element_type=f32)


def join_pieces(ref, first):
    rows = []
    for band in range(8):
        blocks = [
            ref[band * 2 + half, first + part * 8 : first + part * 8 + 8, :]
            for half in range(2)
            for part in range(4)
        ]
        rows.append(jnp.concatenate(blocks, axis=1))
    return jnp.concatenate(rows, axis=0)


def prepare(exc_hbm, loads_hbm, skin_hbm, skout_hbm, drive_ref, low_ref, msg_ref, exc, loads, skin, skout, sems):
    pairs = ((exc_hbm, exc), (skin_hbm, skin), (loads_hbm, loads), (skout_hbm, skout))
    copies = [pltpu.make_async_copy(src, dst, sems.at[i]) for i, (src, dst) in enumerate(pairs)]
    for copy in copies:
        copy.start()
    copies[0].wait()
    drive = exc[...].astype(bf16)
    for part in range(2):
        drive_ref[part] = drive[:, part * 256 : part * 256 + 256]
    copies[1].wait()
    charges = dot_last(drive, skin[...])
    for piece in range(16):
        row = piece // 2 * 8
        for part in range(4):
            col = piece % 2 * 512 + part * 128
            msg_ref[piece, part * 8 : part * 8 + 8, :] = charges[row : row + 8, col : col + 128].astype(bf16)
    copies[2].wait()
    low = loads[...].astype(bf16)
    for part in range(2):
        low_ref[part] = low[:, part * 256 : part * 256 + 256]
    twice = jnp.concatenate([low, low], axis=0)
    copies[3].wait()
    gradient = dot_last(skout[...], twice)
    left = lax.broadcasted_iota(jnp.int32, (32, 128), 1) < 64
    for piece in range(16):
        k = piece * 64
        high, rest = split(jnp.where(left, gradient[k : k + 32], gradient[k + 32 : k + 64]))
        msg_ref[piece, 32:64, :] = high
        msg_ref[piece, 64:96, :] = rest


def split_translation(trans_hbm, out_ref, blocks, sems):
    copies = [pltpu.make_async_copy(trans_hbm.at[0, d], blocks.at[d], sems.at[d]) for d in range(15)]
    for copy in copies:
        copy.start()
    for d in range(15):
        copies[d].wait()
        high, low = split(blocks[d])
        out_ref[d, :64] = high
        out_ref[d, 64:] = low


def lags(parity):
    cluster = lax.axis_index(BLK)
    return [lax.rem(cluster - (2 * q + parity) + 16, 16) for q in range(8)]


def fetch(parts_hbm, blocks, sems, lag):
    copies = []
    for index, behind in enumerate(lag):
        source = parts_hbm.at[jnp.maximum(behind - 1, 0)]
        copies.append(pltpu.make_async_copy(source, blocks.at[index], sems.at[index]))
        copies[index].start()
    return copies


def term(both, block):
    pair = dot(both, block[:64])
    return pair[:64] + pair[64:] + dot(both[:64], block[64:])


def other_terms(msg_ref, parts_hbm, copies_ref, grad_ref, send_ref, blocks, sems):
    fetched = fetch(parts_hbm, blocks, sems, lags(1 - lax.axis_index("core")))
    share = jnp.sum(msg_ref[:, 0:32, :].astype(f32), axis=0).astype(bf16)
    for piece in range(16):
        copies_ref[piece] = share
    packed = jnp.sum(msg_ref[:, 32:64, :].astype(f32) + msg_ref[:, 64:96, :].astype(f32), axis=0)
    gradient = jnp.concatenate([packed, pltpu.roll(packed, 64, 1)], axis=0)
    high, low = split(gradient.T[:64])
    both = jnp.concatenate([high, low], axis=0)
    grad_ref[...] = both
    for index in range(8):
        fetched[index].wait()
        send_ref[index] = term(both, blocks[index])


def own_terms(grad_ref, came_ref, parts_hbm, out_ref, blocks, sems):
    lag = lags(lax.axis_index("core"))
    fetched = fetch(parts_hbm, blocks, sems, lag)
    both = grad_ref[...]
    for index in range(8):
        fetched[index].wait()
        value = jnp.where(lag[index] == 0, 0.0, term(both, blocks[index]))
        out_ref[index] = (value + came_ref[index]).astype(bf16)


def pack(own_ref, pieces_ref, out_ref):
    charges = join_pieces(pieces_ref, 0)
    for q in range(8):
        out_ref[q, 0] = own_ref[q]
        out_ref[q, 1] = charges


def unpack(came_ref, msg_ref, charges_ref):
    total = came_ref[0, 0].astype(f32)
    charges_ref[0] = came_ref[0, 1]
    for q in range(1, 8):
        total = total + came_ref[q, 0].astype(f32)
        charges_ref[q] = came_ref[q, 1]
    for piece in range(16):
        row = piece // 2 * 8
        for part in range(4):
            col = piece % 2 * 512 + part * 128
            msg_ref[piece, part * 8 : part * 8 + 8, :] = total[row : row + 8, col : col + 128].astype(bf16)


def forward(other_ref, came_ref, parts_hbm, pot_ref, blocks, sems):
    core = lax.axis_index("core")
    lag = lags(1 - core) + lags(core)
    fetched = fetch(parts_hbm, blocks, sems, lag)
    total = jnp.zeros((64, 64), f32)
    for index in range(16):
        charges = other_ref[index] if index < 8 else came_ref[index - 8, 1]
        fetched[index].wait()
        pair = dot_last(blocks[index], charges)
        total = total + jnp.where(lag[index] == 0, 0.0, pair[:64] + pair[64:])
    pot_ref[...] = jnp.concatenate([total[:32], total[32:]], axis=1).astype(bf16)


def near(count_ref, rows_ref, cols_ref, low_ref, tiles_hbm, *refs):
    pieces, refs = refs[:8], refs[8:]
    ahead_ref, send_ref, keep_ref, acc, behind, drives, tiles_ref, tile_sems, piece_sems = refs

    def tile_copy(index):
        span = pl.ds(index * 4, 4)
        return pltpu.make_async_copy(tiles_hbm.at[span], tiles_ref.at[span], tile_sems.at[index])

    arriving = [
        pltpu.make_async_copy(pieces[index], drives.at[index], piece_sems.at[index]) for index in range(8)
    ]
    for copy in arriving:
        copy.start()
    for index in range(8):
        tile_copy(index).start()
    acc[...] = jnp.zeros_like(acc)
    behind[...] = jnp.zeros_like(behind)
    for copy in arriving:
        copy.wait()
    count = count_ref[0]
    my_z = lax.axis_index("z")
    my_half = lax.axis_index("xhi")
    group = 4

    def step(index, carry):
        tile_copy(index).wait()
        results = []
        for part in range(group):
            slot = index * group + part
            row = rows_ref[slot]
            col = cols_ref[slot]
            owner = col // 2
            hops = lax.rem(my_z - lax.rem(owner, 8) + 8, 8)
            side = lax.rem(owner // 8 + my_half, 2)
            tile = tiles_ref[slot]
            fwd = dot_last(drives[hops, side, lax.rem(col, 2)], tile)
            bwd = dot(low_ref[row], tile)
            results.append((slot < count, row, col, fwd, bwd))
        for live, row, col, fwd, bwd in results:
            acc[row] += jnp.where(live, fwd, 0.0)
            behind[col] += jnp.where(live, bwd, 0.0)
        return carry

    groups = (count + group - 1) // group
    lax.fori_loop(0, groups, step, 0)

    def drain(index, carry):
        tile_copy(index).wait()
        return carry

    lax.fori_loop(groups, 8, drain, 0)
    for part in range(2):
        ahead_ref[:, part * 256 : part * 256 + 256] = acc[part]
    for target in range(16):
        for part in range(2):
            rows = slice(part * 64, part * 64 + 64)
            cols = slice(part * 128, part * 128 + 128)
            send_ref[target, rows, :] = behind[2 * target + 1 - my_half, :, cols].astype(bf16)
            keep_ref[target, rows, :] = behind[2 * target + my_half, :, cols]


def last_message(adj_ref, pot_ref, keep_ref, mate_ref, out_ref):
    adjoint = jnp.sum(adj_ref[...].astype(f32), axis=0).astype(bf16)
    for piece in range(16):
        out_ref[piece, 0:32, :] = adjoint
        out_ref[piece, 32:64, :] = pot_ref[...]
        out_ref[piece, 64:192, :] = (keep_ref[piece] + mate_ref[piece].astype(f32)).astype(bf16)


def stage(*refs):
    sources, targets, sems = refs[:3], refs[3:6], refs[6]
    copies = [pltpu.make_async_copy(sources[i], targets[i], sems.at[i]) for i in range(3)]
    for copy in copies:
        copy.start()
    for copy in copies:
        copy.wait()


def finish(msg_ref, skin_ref, skout_ref, ahead_ref, resp_ref, sens_ref):
    adjoint = join_pieces(msg_ref, 0)
    packed = jnp.concatenate([msg_ref[r, 32:64, :] for r in range(16)], axis=0)
    packed = packed.astype(f32).T.astype(bf16)
    near_sums = []
    for block in range(2):
        value = msg_ref[block * 8, 64:192, :].astype(f32)
        for z in range(1, 8):
            value = value + msg_ref[block * 8 + z, 64:192, :].astype(f32)
        near_sums += [value[:64], value[64:]]
    sens_ref[...] = dot(adjoint, skin_ref[...]) + jnp.concatenate(near_sums, axis=1)
    upper = jnp.concatenate([skout_ref[r * 64 : r * 64 + 32, :] for r in range(16)], axis=0)
    lower = jnp.concatenate([skout_ref[r * 64 + 32 : r * 64 + 64, :] for r in range(16)], axis=0)
    resp_ref[...] = ahead_ref[...] + dot(packed[:64], upper) + dot(packed[64:], lower)


def swap(value, axis):
    return lax.ppermute(value, axis, [(0, 1), (1, 0)])


def exchange(value, axes):
    return lax.all_to_all(value, axes, 0, 0, tiled=True)


def in_hbm(value):
    return pltpu.with_memory_space_constraint(value, pltpu.HBM)


def shift(value, step):
    return lax.ppermute(value, "z", [(i, (i + step) % 8) for i in range(8)])


def tie(*values):
    return lax.optimization_barrier(values)


def on_device(exc, loads, tiles, tile_rows, tile_cols, tile_count, skin, skout, trans):
    drive, low, msg = call(
        prepare,
        [((2, 64, 256), bf16), ((2, 64, 256), bf16), ((16, 96, 128), bf16)],
        [in_hbm(exc), in_hbm(loads), in_hbm(skin), in_hbm(skout)],
        specs=[hbm()] * 4,
        scratch=[pltpu.VMEM((64, 512), f32)] * 2
        + [pltpu.VMEM((1024, 512), bf16)] * 2
        + [pltpu.SemaphoreType.DMA((4,))],
        name="prepare",
    )
    mate = swap(drive, "xhi")
    (parts,) = call(
        split_translation,
        [((15, 128, 1024), bf16)],
        [in_hbm(trans)],
        specs=[hbm()],
        scratch=[pltpu.VMEM((15, 64, 1024), f32), pltpu.SemaphoreType.DMA((15,))],
        name="split_translation",
    )
    parts = in_hbm(parts)
    msg, mate, parts = tie(exchange(msg, ROWS), mate, parts)
    blocks = [pltpu.VMEM((8, 128, 1024), bf16), pltpu.SemaphoreType.DMA((8,))]
    copies, gradient, send = call(
        other_terms,
        [((16, 32, 128), bf16), ((128, 64), bf16), ((8, 64, 1024), f32)],
        [msg, parts],
        specs=[vmem(), hbm()],
        scratch=blocks,
        name="other_terms",
    )
    here = jnp.stack([drive, mate])
    up1, down1 = shift(here, 1), shift(here, -1)
    (own,) = call(
        own_terms,
        [((8, 64, 1024), bf16)],
        [gradient, swap(send, "core"), parts],
        specs=[vmem(), vmem(), hbm()],
        scratch=blocks,
        name="own_terms",
    )
    copies, up1, down1, own = tie(exchange(copies, ROWS), up1, down1, own)
    (both,) = call(pack, [((8, 2, 64, 1024), bf16)], [own, copies], name="pack")
    up2, down2 = shift(up1, 1), shift(down1, -1)
    up3, down3 = shift(up2, 1), shift(down2, -1)
    up4 = shift(up3, 1)
    ahead, send, keep = call(
        near,
        [((64, 512), f32), ((16, 128, 128), bf16), ((16, 128, 128), f32)],
        [tile_count, tile_rows, tile_cols, low, in_hbm(tiles)]
        + [in_hbm(piece) for piece in (here, up1, up2, up3, up4, down3, down2, down1)],
        specs=[smem(), smem(), smem(), vmem()] + [hbm()] * 9,
        scratch=[
            pltpu.VMEM((2, 64, 256), f32),
            pltpu.VMEM((32, 64, 256), f32),
            pltpu.VMEM((8, 2, 2, 64, 256), bf16),
            pltpu.VMEM((32, 256, 256), bf16),
            pltpu.SemaphoreType.DMA((8,)),
            pltpu.SemaphoreType.DMA((8,)),
        ],
        name="near",
    )
    both, ahead, send, keep = tie(exchange(both, FACE), ahead, send, keep)
    mate_near = swap(send, "xhi")
    adjoint, charges = call(
        unpack,
        [((16, 32, 128), bf16), ((8, 64, 1024), bf16)],
        [both],
        name="unpack",
    )
    others = swap(charges, "core")
    (potential,) = call(
        forward,
        [((32, 128), bf16)],
        [others, both, parts],
        specs=[vmem(), vmem(), hbm()],
        scratch=[pltpu.VMEM((16, 128, 1024), bf16), pltpu.SemaphoreType.DMA((16,))],
        name="forward",
    )
    adjoint, potential, mate_near = tie(exchange(adjoint, ROWS), potential, mate_near)
    (last,) = call(
        last_message,
        [((16, 192, 128), bf16)],
        [adjoint, potential, keep, mate_near],
        name="last_message",
    )
    staged = call(
        stage,
        [((1024, 512), bf16), ((1024, 512), bf16), ((64, 512), f32)],
        [in_hbm(skin), in_hbm(skout), in_hbm(ahead)],
        specs=[hbm()] * 3,
        scratch=[pltpu.SemaphoreType.DMA((3,))],
        name="stage",
    )
    last, *staged = tie(exchange(last, ROWS), *staged)
    return tuple(call(finish, [((64, 512), f32), ((64, 512), f32)], [last, *staged], name="finish"))


def solution(mesh):
    fine = Mesh(mesh.devices.reshape(2, 4, 2, 2, 8), BLK + ROWS)
    every = BLK + ROWS
    return jax.shard_map(
        on_device,
        mesh=fine,
        in_specs=(
            P(None, every),
            P(None, every),
            P(every, None, None),
            P(every),
            P(every),
            P(every),
            P(None, every),
            P(None, every),
            P(BLK, None, ROWS, None),
        ),
        out_specs=(P(None, every), P(None, every)),
        check_vma=False,
    )
```

```python
import jax
import jax.numpy as jnp
from jax import lax
from jax.experimental import pallas as pl
from jax.experimental.pallas import tpu as pltpu
from jax.sharding import Mesh
from jax.sharding import PartitionSpec as P

BLK = ("xlo", "y", "core")
ROWS = ("xhi", "z")
FACE = ("xlo", "y")
bf16 = jnp.bfloat16
f32 = jnp.float32
LAST = (((1,), (1,)), ((), ()))


def vmem():
    return pl.BlockSpec(memory_space=pltpu.VMEM)


def smem():
    return pl.BlockSpec(memory_space=pltpu.SMEM)


def hbm():
    return pl.BlockSpec(memory_space=pltpu.HBM)


def call(kernel, outs, args, specs=None, scratch=(), name=None):
    return pl.pallas_call(
        kernel,
        out_shape=[jax.ShapeDtypeStruct(s, d) for s, d in outs],
        in_specs=specs or [vmem()] * len(args),
        out_specs=[vmem()] * len(outs),
        scratch_shapes=list(scratch),
        compiler_params=pltpu.CompilerParams(vmem_limit_bytes=20 * 2**20),
        cost_estimate=pl.CostEstimate(flops=1000, bytes_accessed=1000, transcendentals=0),
        name=name,
    )(*args)


def split(value):
    high = value.astype(bf16)
    return high, (value - high.astype(f32)).astype(bf16)


def dot(a, b):
    return jnp.dot(a, b, preferred_element_type=f32)


def dot_last(a, b):
    return lax.dot_general(a, b, LAST, preferred_element_type=f32)


def join_pieces(ref, first):
    rows = []
    for band in range(8):
        blocks = [
            ref[band * 2 + half, first + part * 8 : first + part * 8 + 8, :]
            for half in range(2)
            for part in range(4)
        ]
        rows.append(jnp.concatenate(blocks, axis=1))
    return jnp.concatenate(rows, axis=0)


def prepare(exc_hbm, loads_hbm, skin_hbm, skout_hbm, drive_ref, low_ref, msg_ref, exc, loads, skin, skout, sems):
    pairs = ((exc_hbm, exc), (skin_hbm, skin), (loads_hbm, loads), (skout_hbm, skout))
    copies = [pltpu.make_async_copy(src, dst, sems.at[i]) for i, (src, dst) in enumerate(pairs)]
    for copy in copies:
        copy.start()
    copies[0].wait()
    drive = exc[...].astype(bf16)
    for part in range(2):
        drive_ref[part] = drive[:, part * 256 : part * 256 + 256]
    copies[1].wait()
    charges = dot_last(drive, skin[...])
    for piece in range(16):
        row = piece // 2 * 8
        for part in range(4):
            col = piece % 2 * 512 + part * 128
            msg_ref[piece, part * 8 : part * 8 + 8, :] = charges[row : row + 8, col : col + 128].astype(bf16)
    copies[2].wait()
    low = loads[...].astype(bf16)
    for part in range(2):
        low_ref[part] = low[:, part * 256 : part * 256 + 256]
    twice = jnp.concatenate([low, low], axis=0)
    copies[3].wait()
    gradient = dot_last(skout[...], twice)
    left = lax.broadcasted_iota(jnp.int32, (32, 128), 1) < 64
    for piece in range(16):
        k = piece * 64
        high, rest = split(jnp.where(left, gradient[k : k + 32], gradient[k + 32 : k + 64]))
        msg_ref[piece, 32:64, :] = high
        msg_ref[piece, 64:96, :] = rest


def split_translation(trans_hbm, out_ref, blocks, sems):
    copies = [pltpu.make_async_copy(trans_hbm.at[0, d], blocks.at[d], sems.at[d]) for d in range(15)]
    for copy in copies:
        copy.start()
    for d in range(15):
        copies[d].wait()
        high, low = split(blocks[d])
        out_ref[d, :64] = high
        out_ref[d, 64:] = low


def lags(parity):
    cluster = lax.axis_index(BLK)
    return [lax.rem(cluster - (2 * q + parity) + 16, 16) for q in range(8)]


def fetch(parts_hbm, blocks, sems, lag):
    copies = []
    for index, behind in enumerate(lag):
        source = parts_hbm.at[jnp.maximum(behind - 1, 0)]
        copies.append(pltpu.make_async_copy(source, blocks.at[index], sems.at[index]))
        copies[index].start()
    return copies


def term(both, block):
    pair = dot(both, block[:64])
    return pair[:64] + pair[64:] + dot(both[:64], block[64:])


def other_terms(msg_ref, parts_hbm, copies_ref, grad_ref, send_ref, blocks, sems):
    fetched = fetch(parts_hbm, blocks, sems, lags(1 - lax.axis_index("core")))
    share = jnp.sum(msg_ref[:, 0:32, :].astype(f32), axis=0).astype(bf16)
    for piece in range(16):
        copies_ref[piece] = share
    packed = jnp.sum(msg_ref[:, 32:64, :].astype(f32) + msg_ref[:, 64:96, :].astype(f32), axis=0)
    gradient = jnp.concatenate([packed, pltpu.roll(packed, 64, 1)], axis=0)
    high, low = split(gradient.T[:64])
    both = jnp.concatenate([high, low], axis=0)
    grad_ref[...] = both
    for index in range(8):
        fetched[index].wait()
        send_ref[index] = term(both, blocks[index])


def own_terms(grad_ref, came_ref, parts_hbm, out_ref, blocks, sems):
    lag = lags(lax.axis_index("core"))
    fetched = fetch(parts_hbm, blocks, sems, lag)
    both = grad_ref[...]
    for index in range(8):
        fetched[index].wait()
        value = jnp.where(lag[index] == 0, 0.0, term(both, blocks[index]))
        out_ref[index] = (value + came_ref[index]).astype(bf16)


def pack(own_ref, pieces_ref, out_ref):
    charges = join_pieces(pieces_ref, 0)
    for q in range(8):
        out_ref[q, 0] = own_ref[q]
        out_ref[q, 1] = charges


def unpack(came_ref, msg_ref, charges_ref):
    total = came_ref[0, 0].astype(f32)
    charges_ref[0] = came_ref[0, 1]
    for q in range(1, 8):
        total = total + came_ref[q, 0].astype(f32)
        charges_ref[q] = came_ref[q, 1]
    for piece in range(16):
        row = piece // 2 * 8
        for part in range(4):
            col = piece % 2 * 512 + part * 128
            msg_ref[piece, part * 8 : part * 8 + 8, :] = total[row : row + 8, col : col + 128].astype(bf16)


def forward(other_ref, came_ref, parts_hbm, pot_ref, blocks, sems):
    core = lax.axis_index("core")
    lag = lags(1 - core) + lags(core)
    fetched = fetch(parts_hbm, blocks, sems, lag)
    total = jnp.zeros((64, 64), f32)
    for index in range(16):
        charges = other_ref[index] if index < 8 else came_ref[index - 8, 1]
        fetched[index].wait()
        pair = dot_last(blocks[index], charges)
        total = total + jnp.where(lag[index] == 0, 0.0, pair[:64] + pair[64:])
    pot_ref[...] = jnp.concatenate([total[:32], total[32:]], axis=1).astype(bf16)


def near(count_ref, rows_ref, cols_ref, low_ref, tiles_hbm, *refs):
    pieces, refs = refs[:8], refs[8:]
    ahead_ref, keep_ref, across_ref, beside_ref, both_ref, acc, behind, drives, tiles_ref, tile_sems, piece_sems = refs

    def tile_copy(index):
        span = pl.ds(index * 4, 4)
        return pltpu.make_async_copy(tiles_hbm.at[span], tiles_ref.at[span], tile_sems.at[index])

    arriving = [
        pltpu.make_async_copy(pieces[index], drives.at[index], piece_sems.at[index]) for index in range(8)
    ]
    for copy in arriving:
        copy.start()
    for index in range(8):
        tile_copy(index).start()
    acc[...] = jnp.zeros_like(acc)
    behind[...] = jnp.zeros_like(behind)
    for copy in arriving:
        copy.wait()
    count = count_ref[0]
    my_z = lax.axis_index("z")
    my_half = lax.axis_index("xhi")
    group = 4

    def step(index, carry):
        tile_copy(index).wait()
        results = []
        for part in range(group):
            slot = index * group + part
            row = rows_ref[slot]
            col = cols_ref[slot]
            owner = col // 2
            hops = lax.rem(my_z - lax.rem(owner, 8) + 8, 8)
            side = lax.rem(owner // 8 + my_half, 2)
            tile = tiles_ref[slot]
            fwd = dot_last(drives[hops, side, lax.rem(col, 2)], tile)
            bwd = dot(low_ref[row], tile)
            results.append((slot < count, row, col, fwd, bwd))
        for live, row, col, fwd, bwd in results:
            acc[row] += jnp.where(live, fwd, 0.0)
            behind[col] += jnp.where(live, bwd, 0.0)
        return carry

    groups = (count + group - 1) // group
    lax.fori_loop(0, groups, step, 0)

    def drain(index, carry):
        tile_copy(index).wait()
        return carry

    lax.fori_loop(groups, 8, drain, 0)
    for part in range(2):
        ahead_ref[:, part * 256 : part * 256 + 256] = acc[part]
    parity = lax.rem(my_z, 2)
    mine = pl.ds(pl.multiple_of(parity * 128, 128), 128)
    theirs = pl.ds(pl.multiple_of((1 - parity) * 128, 128), 128)
    for target in range(16):
        keep_ref[target] = behind[2 * target + my_half, :, mine]
        across_ref[target] = behind[2 * target + 1 - my_half, :, mine].astype(bf16)
        beside_ref[target] = behind[2 * target + my_half, :, theirs].astype(bf16)
        both_ref[target] = behind[2 * target + 1 - my_half, :, theirs].astype(bf16)


def last_message(adj_ref, pot_ref, keep_ref, across_ref, beside_ref, both_ref, out_ref):
    adjoint = jnp.sum(adj_ref[...].astype(f32), axis=0).astype(bf16)
    for piece in range(16):
        out_ref[piece, 0:32, :] = adjoint
        out_ref[piece, 32:64, :] = pot_ref[...]
        near_sum = keep_ref[piece] + across_ref[piece].astype(f32)
        near_sum = near_sum + beside_ref[piece].astype(f32) + both_ref[piece].astype(f32)
        out_ref[piece, 64:128, :] = near_sum.astype(bf16)


def stage(*refs):
    sources, targets, sems = refs[:3], refs[3:6], refs[6]
    copies = [pltpu.make_async_copy(sources[i], targets[i], sems.at[i]) for i in range(3)]
    for copy in copies:
        copy.start()
    for copy in copies:
        copy.wait()


def finish(msg_ref, skin_ref, skout_ref, ahead_ref, resp_ref, sens_ref):
    adjoint = join_pieces(msg_ref, 0)
    packed = jnp.concatenate([msg_ref[r, 32:64, :] for r in range(16)], axis=0)
    packed = packed.astype(f32).T.astype(bf16)
    near_sums = []
    for block in range(2):
        for parity in range(2):
            value = msg_ref[block * 8 + parity, 64:128, :].astype(f32)
            for z in range(parity + 2, 8, 2):
                value = value + msg_ref[block * 8 + z, 64:128, :].astype(f32)
            near_sums.append(value)
    sens_ref[...] = dot(adjoint, skin_ref[...]) + jnp.concatenate(near_sums, axis=1)
    upper = jnp.concatenate([skout_ref[r * 64 : r * 64 + 32, :] for r in range(16)], axis=0)
    lower = jnp.concatenate([skout_ref[r * 64 + 32 : r * 64 + 64, :] for r in range(16)], axis=0)
    resp_ref[...] = ahead_ref[...] + dot(packed[:64], upper) + dot(packed[64:], lower)


def swap(value, axis):
    return lax.ppermute(value, axis, [(0, 1), (1, 0)])


def exchange(value, axes):
    return lax.all_to_all(value, axes, 0, 0, tiled=True)


def in_hbm(value):
    return pltpu.with_memory_space_constraint(value, pltpu.HBM)


def shift(value, step):
    return lax.ppermute(value, "z", [(i, (i + step) % 8) for i in range(8)])


def tie(*values):
    return lax.optimization_barrier(values)


def on_device(exc, loads, tiles, tile_rows, tile_cols, tile_count, skin, skout, trans):
    drive, low, msg = call(
        prepare,
        [((2, 64, 256), bf16), ((2, 64, 256), bf16), ((16, 96, 128), bf16)],
        [in_hbm(exc), in_hbm(loads), in_hbm(skin), in_hbm(skout)],
        specs=[hbm()] * 4,
        scratch=[pltpu.VMEM((64, 512), f32)] * 2
        + [pltpu.VMEM((1024, 512), bf16)] * 2
        + [pltpu.SemaphoreType.DMA((4,))],
        name="prepare",
    )
    mate = swap(drive, "xhi")
    (parts,) = call(
        split_translation,
        [((15, 128, 1024), bf16)],
        [in_hbm(trans)],
        specs=[hbm()],
        scratch=[pltpu.VMEM((15, 64, 1024), f32), pltpu.SemaphoreType.DMA((15,))],
        name="split_translation",
    )
    parts = in_hbm(parts)
    msg, mate, parts = tie(exchange(msg, ROWS), mate, parts)
    blocks = [pltpu.VMEM((8, 128, 1024), bf16), pltpu.SemaphoreType.DMA((8,))]
    copies, gradient, send = call(
        other_terms,
        [((16, 32, 128), bf16), ((128, 64), bf16), ((8, 64, 1024), f32)],
        [msg, parts],
        specs=[vmem(), hbm()],
        scratch=blocks,
        name="other_terms",
    )
    here = jnp.stack([drive, mate])
    up1, down1 = shift(here, 1), shift(here, -1)
    (own,) = call(
        own_terms,
        [((8, 64, 1024), bf16)],
        [gradient, swap(send, "core"), parts],
        specs=[vmem(), vmem(), hbm()],
        scratch=blocks,
        name="own_terms",
    )
    copies, up1, down1, own = tie(exchange(copies, ROWS), up1, down1, own)
    (both,) = call(pack, [((8, 2, 64, 1024), bf16)], [own, copies], name="pack")
    up2, down2 = shift(up1, 1), shift(down1, -1)
    up3, down3 = shift(up2, 1), shift(down2, -1)
    up4 = shift(up3, 1)
    ahead, keep, *quarters = call(
        near,
        [((64, 512), f32), ((16, 64, 128), f32)] + [((16, 64, 128), bf16)] * 3,
        [tile_count, tile_rows, tile_cols, low, in_hbm(tiles)]
        + [in_hbm(piece) for piece in (here, up1, up2, up3, up4, down3, down2, down1)],
        specs=[smem(), smem(), smem(), vmem()] + [hbm()] * 9,
        scratch=[
            pltpu.VMEM((2, 64, 256), f32),
            pltpu.VMEM((32, 64, 256), f32),
            pltpu.VMEM((8, 2, 2, 64, 256), bf16),
            pltpu.VMEM((32, 256, 256), bf16),
            pltpu.SemaphoreType.DMA((8,)),
            pltpu.SemaphoreType.DMA((8,)),
        ],
        name="near",
    )
    both, ahead = tie(exchange(both, FACE), ahead)
    quarters = [
        lax.ppermute(value, ROWS, [(i, i ^ mask) for i in range(16)])
        for value, mask in zip(quarters, (8, 1, 9))
    ]
    adjoint, charges = call(
        unpack,
        [((16, 32, 128), bf16), ((8, 64, 1024), bf16)],
        [both],
        name="unpack",
    )
    others = swap(charges, "core")
    (potential,) = call(
        forward,
        [((32, 128), bf16)],
        [others, both, parts],
        specs=[vmem(), vmem(), hbm()],
        scratch=[pltpu.VMEM((16, 128, 1024), bf16), pltpu.SemaphoreType.DMA((16,))],
        name="forward",
    )
    adjoint, potential, *quarters = tie(exchange(adjoint, ROWS), potential, *quarters)
    (last,) = call(
        last_message,
        [((16, 128, 128), bf16)],
        [adjoint, potential, keep, *quarters],
        name="last_message",
    )
    staged = call(
        stage,
        [((1024, 512), bf16), ((1024, 512), bf16), ((64, 512), f32)],
        [in_hbm(skin), in_hbm(skout), in_hbm(ahead)],
        specs=[hbm()] * 3,
        scratch=[pltpu.SemaphoreType.DMA((3,))],
        name="stage",
    )
    last, *staged = tie(exchange(last, ROWS), *staged)
    return tuple(call(finish, [((64, 512), f32), ((64, 512), f32)], [last, *staged], name="finish"))


def solution(mesh):
    fine = Mesh(mesh.devices.reshape(2, 4, 2, 2, 8), BLK + ROWS)
    every = BLK + ROWS
    return jax.shard_map(
        on_device,
        mesh=fine,
        in_specs=(
            P(None, every),
            P(None, every),
            P(every, None, None),
            P(every),
            P(every),
            P(every),
            P(None, every),
            P(None, every),
            P(BLK, None, ROWS, None),
        ),
        out_specs=(P(None, every), P(None, every)),
        check_vma=False,
    )
```

```python
import jax
import jax.numpy as jnp
from jax import lax
from jax.experimental import pallas as pl
from jax.experimental.pallas import tpu as pltpu
from jax.sharding import Mesh
from jax.sharding import PartitionSpec as P

BLK = ("xlo", "y", "core")
ROWS = ("xhi", "z")
FACE = ("xlo", "y")
bf16 = jnp.bfloat16
f32 = jnp.float32
LAST = (((1,), (1,)), ((), ()))


def vmem():
    return pl.BlockSpec(memory_space=pltpu.VMEM)


def smem():
    return pl.BlockSpec(memory_space=pltpu.SMEM)


def hbm():
    return pl.BlockSpec(memory_space=pltpu.HBM)


def call(kernel, outs, args, specs=None, scratch=(), name=None):
    return pl.pallas_call(
        kernel,
        out_shape=[jax.ShapeDtypeStruct(s, d) for s, d in outs],
        in_specs=specs or [vmem()] * len(args),
        out_specs=[vmem()] * len(outs),
        scratch_shapes=list(scratch),
        compiler_params=pltpu.CompilerParams(vmem_limit_bytes=20 * 2**20),
        cost_estimate=pl.CostEstimate(flops=1000, bytes_accessed=1000, transcendentals=0),
        name=name,
    )(*args)


def split(value):
    high = value.astype(bf16)
    return high, (value - high.astype(f32)).astype(bf16)


def dot(a, b):
    return jnp.dot(a, b, preferred_element_type=f32)


def dot_last(a, b):
    return lax.dot_general(a, b, LAST, preferred_element_type=f32)


def join_pieces(ref, first):
    rows = []
    for band in range(8):
        blocks = [
            ref[band * 2 + half, first + part * 8 : first + part * 8 + 8, :]
            for half in range(2)
            for part in range(4)
        ]
        rows.append(jnp.concatenate(blocks, axis=1))
    return jnp.concatenate(rows, axis=0)


def prepare(exc_hbm, loads_hbm, skin_hbm, skout_hbm, drive_ref, low_ref, msg_ref, exc, loads, skin, skout, sems):
    pairs = ((exc_hbm, exc), (skin_hbm, skin), (loads_hbm, loads), (skout_hbm, skout))
    copies = [pltpu.make_async_copy(src, dst, sems.at[i]) for i, (src, dst) in enumerate(pairs)]
    for copy in copies:
        copy.start()
    copies[0].wait()
    drive = exc[...].astype(bf16)
    for part in range(2):
        drive_ref[part] = drive[:, part * 256 : part * 256 + 256]
    copies[1].wait()
    charges = dot_last(drive, skin[...])
    for piece in range(16):
        row = piece // 2 * 8
        for part in range(4):
            col = piece % 2 * 512 + part * 128
            msg_ref[piece, part * 8 : part * 8 + 8, :] = charges[row : row + 8, col : col + 128].astype(bf16)
    copies[2].wait()
    low = loads[...].astype(bf16)
    for part in range(2):
        low_ref[part] = low[:, part * 256 : part * 256 + 256]
    twice = jnp.concatenate([low, low], axis=0)
    copies[3].wait()
    gradient = dot_last(skout[...], twice)
    left = lax.broadcasted_iota(jnp.int32, (32, 128), 1) < 64
    for piece in range(16):
        k = piece * 64
        high, rest = split(jnp.where(left, gradient[k : k + 32], gradient[k + 32 : k + 64]))
        msg_ref[piece, 32:64, :] = high
        msg_ref[piece, 64:96, :] = rest


def split_translation(trans_hbm, out_ref, blocks, sems):
    copies = [pltpu.make_async_copy(trans_hbm.at[0, d], blocks.at[d], sems.at[d]) for d in range(15)]
    for copy in copies:
        copy.start()
    for d in range(15):
        copies[d].wait()
        high, low = split(blocks[d])
        out_ref[d, :64] = high
        out_ref[d, 64:] = low


def lags(parity):
    cluster = lax.axis_index(BLK)
    return [lax.rem(cluster - (2 * q + parity) + 16, 16) for q in range(8)]


def fetch(parts_hbm, blocks, sems, lag):
    copies = []
    for index, behind in enumerate(lag):
        source = parts_hbm.at[jnp.maximum(behind - 1, 0)]
        copies.append(pltpu.make_async_copy(source, blocks.at[index], sems.at[index]))
        copies[index].start()
    return copies


def term(both, block):
    pair = dot(both, block[:64])
    return pair[:64] + pair[64:] + dot(both[:64], block[64:])


def other_terms(msg_ref, parts_hbm, copies_ref, grad_ref, send_ref, blocks, sems):
    fetched = fetch(parts_hbm, blocks, sems, lags(1 - lax.axis_index("core")))
    share = jnp.sum(msg_ref[:, 0:32, :].astype(f32), axis=0).astype(bf16)
    for piece in range(16):
        copies_ref[piece] = share
    packed = jnp.sum(msg_ref[:, 32:64, :].astype(f32) + msg_ref[:, 64:96, :].astype(f32), axis=0)
    gradient = jnp.concatenate([packed, pltpu.roll(packed, 64, 1)], axis=0)
    high, low = split(gradient.T[:64])
    both = jnp.concatenate([high, low], axis=0)
    grad_ref[...] = both
    for index in range(8):
        fetched[index].wait()
        send_ref[index] = term(both, blocks[index])


def own_terms(grad_ref, came_ref, parts_hbm, out_ref, blocks, sems):
    lag = lags(lax.axis_index("core"))
    fetched = fetch(parts_hbm, blocks, sems, lag)
    both = grad_ref[...]
    for index in range(8):
        fetched[index].wait()
        value = jnp.where(lag[index] == 0, 0.0, term(both, blocks[index]))
        out_ref[index] = (value + came_ref[index]).astype(bf16)


def pack(own_ref, pieces_ref, out_ref):
    charges = join_pieces(pieces_ref, 0)
    for q in range(8):
        out_ref[q, 0] = own_ref[q]
        out_ref[q, 1] = charges


def unpack(came_ref, msg_ref):
    total = came_ref[0, 0].astype(f32)
    for q in range(1, 8):
        total = total + came_ref[q, 0].astype(f32)
    for piece in range(16):
        row = piece // 2 * 8
        for part in range(4):
            col = piece % 2 * 512 + part * 128
            msg_ref[piece, part * 8 : part * 8 + 8, :] = total[row : row + 8, col : col + 128].astype(bf16)


def forward(other_ref, came_ref, parts_hbm, pot_ref, blocks, sems):
    core = lax.axis_index("core")
    lag = lags(1 - core) + lags(core)
    fetched = fetch(parts_hbm, blocks, sems, lag)
    total = jnp.zeros((64, 64), f32)
    for index in range(16):
        charges = other_ref[index, 1] if index < 8 else came_ref[index - 8, 1]
        fetched[index].wait()
        pair = dot_last(blocks[index], charges)
        total = total + jnp.where(lag[index] == 0, 0.0, pair[:64] + pair[64:])
    pot_ref[...] = jnp.concatenate([total[:32], total[32:]], axis=1).astype(bf16)


def near(count_ref, rows_ref, cols_ref, low_ref, tiles_hbm, *refs):
    pieces, refs = refs[:8], refs[8:]
    ahead_ref, keep_ref, across_ref, beside_ref, both_ref, acc, behind, drives, tiles_ref, tile_sems, piece_sems = refs

    def tile_copy(index):
        span = pl.ds(index * 4, 4)
        return pltpu.make_async_copy(tiles_hbm.at[span], tiles_ref.at[span], tile_sems.at[index])

    arriving = [
        pltpu.make_async_copy(pieces[index], drives.at[index], piece_sems.at[index]) for index in range(8)
    ]
    for copy in arriving:
        copy.start()
    for index in range(8):
        tile_copy(index).start()
    acc[...] = jnp.zeros_like(acc)
    behind[...] = jnp.zeros_like(behind)
    for copy in arriving:
        copy.wait()
    count = count_ref[0]
    my_z = lax.axis_index("z")
    my_half = lax.axis_index("xhi")
    group = 4

    def step(index, carry):
        tile_copy(index).wait()
        results = []
        for part in range(group):
            slot = index * group + part
            row = rows_ref[slot]
            col = cols_ref[slot]
            owner = col // 2
            hops = lax.rem(my_z - lax.rem(owner, 8) + 8, 8)
            side = lax.rem(owner // 8 + my_half, 2)
            tile = tiles_ref[slot]
            fwd = dot_last(drives[hops, side, lax.rem(col, 2)], tile)
            bwd = dot(low_ref[row], tile)
            results.append((slot < count, row, col, fwd, bwd))
        for live, row, col, fwd, bwd in results:
            acc[row] += jnp.where(live, fwd, 0.0)
            behind[col] += jnp.where(live, bwd, 0.0)
        return carry

    groups = (count + group - 1) // group
    lax.fori_loop(0, groups, step, 0)

    def drain(index, carry):
        tile_copy(index).wait()
        return carry

    lax.fori_loop(groups, 8, drain, 0)
    for part in range(2):
        ahead_ref[:, part * 256 : part * 256 + 256] = acc[part]
    parity = lax.rem(my_z, 2)
    mine = pl.ds(pl.multiple_of(parity * 128, 128), 128)
    theirs = pl.ds(pl.multiple_of((1 - parity) * 128, 128), 128)
    for target in range(16):
        keep_ref[target] = behind[2 * target + my_half, :, mine].astype(bf16)
        across_ref[target] = behind[2 * target + 1 - my_half, :, mine].astype(bf16)
        beside_ref[target] = behind[2 * target + my_half, :, theirs].astype(bf16)
        both_ref[target] = behind[2 * target + 1 - my_half, :, theirs].astype(bf16)


def last_message(adj_ref, pot_ref, keep_hbm, across_ref, beside_ref, both_ref, out_ref, keep_ref, sem):
    copy = pltpu.make_async_copy(keep_hbm, keep_ref, sem)
    copy.start()
    adjoint = jnp.sum(adj_ref[...].astype(f32), axis=0).astype(bf16)
    for piece in range(16):
        out_ref[piece, 0:32, :] = adjoint
        out_ref[piece, 32:64, :] = pot_ref[...]
    copy.wait()
    for piece in range(16):
        near_sum = keep_ref[piece].astype(f32) + across_ref[piece].astype(f32)
        near_sum = near_sum + beside_ref[piece].astype(f32) + both_ref[piece].astype(f32)
        out_ref[piece, 64:128, :] = near_sum.astype(bf16)


def stage(*refs):
    sources, targets, sems = refs[:3], refs[3:6], refs[6]
    copies = [pltpu.make_async_copy(sources[i], targets[i], sems.at[i]) for i in range(3)]
    for copy in copies:
        copy.start()
    for copy in copies:
        copy.wait()


def finish(msg_ref, skin_ref, skout_ref, ahead_ref, resp_ref, sens_ref):
    adjoint = join_pieces(msg_ref, 0)
    packed = jnp.concatenate([msg_ref[r, 32:64, :] for r in range(16)], axis=0)
    packed = packed.astype(f32).T.astype(bf16)
    near_sums = []
    for block in range(2):
        for parity in range(2):
            value = msg_ref[block * 8 + parity, 64:128, :].astype(f32)
            for z in range(parity + 2, 8, 2):
                value = value + msg_ref[block * 8 + z, 64:128, :].astype(f32)
            near_sums.append(value)
    sens_ref[...] = dot(adjoint, skin_ref[...]) + jnp.concatenate(near_sums, axis=1)
    upper = jnp.concatenate([skout_ref[r * 64 : r * 64 + 32, :] for r in range(16)], axis=0)
    lower = jnp.concatenate([skout_ref[r * 64 + 32 : r * 64 + 64, :] for r in range(16)], axis=0)
    resp_ref[...] = ahead_ref[...] + dot(packed[:64], upper) + dot(packed[64:], lower)


def swap(value, axis):
    return lax.ppermute(value, axis, [(0, 1), (1, 0)])


def exchange(value, axes):
    return lax.all_to_all(value, axes, 0, 0, tiled=True)


def in_hbm(value):
    return pltpu.with_memory_space_constraint(value, pltpu.HBM)


def shift(value, step):
    return lax.ppermute(value, "z", [(i, (i + step) % 8) for i in range(8)])


def tie(*values):
    return lax.optimization_barrier(values)


def on_device(exc, loads, tiles, tile_rows, tile_cols, tile_count, skin, skout, trans):
    drive, low, msg = call(
        prepare,
        [((2, 64, 256), bf16), ((2, 64, 256), bf16), ((16, 96, 128), bf16)],
        [in_hbm(exc), in_hbm(loads), in_hbm(skin), in_hbm(skout)],
        specs=[hbm()] * 4,
        scratch=[pltpu.VMEM((64, 512), f32)] * 2
        + [pltpu.VMEM((1024, 512), bf16)] * 2
        + [pltpu.SemaphoreType.DMA((4,))],
        name="prepare",
    )
    mate = swap(drive, "xhi")
    (parts,) = call(
        split_translation,
        [((15, 128, 1024), bf16)],
        [in_hbm(trans)],
        specs=[hbm()],
        scratch=[pltpu.VMEM((15, 64, 1024), f32), pltpu.SemaphoreType.DMA((15,))],
        name="split_translation",
    )
    parts = in_hbm(parts)
    msg, mate, parts = tie(exchange(msg, ROWS), mate, parts)
    blocks = [pltpu.VMEM((8, 128, 1024), bf16), pltpu.SemaphoreType.DMA((8,))]
    copies, gradient, send = call(
        other_terms,
        [((16, 32, 128), bf16), ((128, 64), bf16), ((8, 64, 1024), f32)],
        [msg, parts],
        specs=[vmem(), hbm()],
        scratch=blocks,
        name="other_terms",
    )
    here = jnp.stack([drive, mate])
    up1, down1 = shift(here, 1), shift(here, -1)
    (own,) = call(
        own_terms,
        [((8, 64, 1024), bf16)],
        [gradient, swap(send, "core"), parts],
        specs=[vmem(), vmem(), hbm()],
        scratch=blocks,
        name="own_terms",
    )
    copies, up1, down1, own = tie(exchange(copies, ROWS), up1, down1, own)
    (both,) = call(pack, [((8, 2, 64, 1024), bf16)], [own, copies], name="pack")
    up2, down2 = shift(up1, 1), shift(down1, -1)
    up3, down3 = shift(up2, 1), shift(down2, -1)
    up4 = shift(up3, 1)
    ahead, keep, *quarters = call(
        near,
        [((64, 512), f32)] + [((16, 64, 128), bf16)] * 4,
        [tile_count, tile_rows, tile_cols, low, in_hbm(tiles)]
        + [in_hbm(piece) for piece in (here, up1, up2, up3, up4, down3, down2, down1)],
        specs=[smem(), smem(), smem(), vmem()] + [hbm()] * 9,
        scratch=[
            pltpu.VMEM((2, 64, 256), f32),
            pltpu.VMEM((32, 64, 256), f32),
            pltpu.VMEM((8, 2, 2, 64, 256), bf16),
            pltpu.VMEM((32, 256, 256), bf16),
            pltpu.SemaphoreType.DMA((8,)),
            pltpu.SemaphoreType.DMA((8,)),
        ],
        name="near",
    )
    both, ahead = tie(exchange(both, FACE), ahead)
    quarters = [
        lax.ppermute(value, ROWS, [(i, i ^ mask) for i in range(16)])
        for value, mask in zip(quarters, (8, 1, 9))
    ]
    (adjoint,) = call(unpack, [((16, 32, 128), bf16)], [both], name="unpack")
    others = swap(both, "core")
    (potential,) = call(
        forward,
        [((32, 128), bf16)],
        [others, both, parts],
        specs=[vmem(), vmem(), hbm()],
        scratch=[pltpu.VMEM((16, 128, 1024), bf16), pltpu.SemaphoreType.DMA((16,))],
        name="forward",
    )
    adjoint, potential, *quarters = tie(exchange(adjoint, ROWS), potential, *quarters)
    (last,) = call(
        last_message,
        [((16, 128, 128), bf16)],
        [adjoint, potential, in_hbm(keep), *quarters],
        specs=[vmem()] * 2 + [hbm()] + [vmem()] * 3,
        scratch=[pltpu.VMEM((16, 64, 128), bf16), pltpu.SemaphoreType.DMA],
        name="last_message",
    )
    staged = call(
        stage,
        [((1024, 512), bf16), ((1024, 512), bf16), ((64, 512), f32)],
        [in_hbm(skin), in_hbm(skout), in_hbm(ahead)],
        specs=[hbm()] * 3,
        scratch=[pltpu.SemaphoreType.DMA((3,))],
        name="stage",
    )
    last, *staged = tie(exchange(last, ROWS), *staged)
    return tuple(call(finish, [((64, 512), f32), ((64, 512), f32)], [last, *staged], name="finish"))


def solution(mesh):
    fine = Mesh(mesh.devices.reshape(2, 4, 2, 2, 8), BLK + ROWS)
    every = BLK + ROWS
    return jax.shard_map(
        on_device,
        mesh=fine,
        in_specs=(
            P(None, every),
            P(None, every),
            P(every, None, None),
            P(every),
            P(every),
            P(every),
            P(None, every),
            P(None, every),
            P(BLK, None, ROWS, None),
        ),
        out_specs=(P(None, every), P(None, every)),
        check_vma=False,
    )
```

```python
import jax
import jax.numpy as jnp
from jax import lax
from jax.experimental import pallas as pl
from jax.experimental.pallas import tpu as pltpu
from jax.sharding import Mesh
from jax.sharding import PartitionSpec as P

BLK = ("xlo", "y", "core")
ROWS = ("xhi", "z")
FACE = ("xlo", "y")
bf16 = jnp.bfloat16
f32 = jnp.float32
LAST = (((1,), (1,)), ((), ()))


def vmem():
    return pl.BlockSpec(memory_space=pltpu.VMEM)


def smem():
    return pl.BlockSpec(memory_space=pltpu.SMEM)


def hbm():
    return pl.BlockSpec(memory_space=pltpu.HBM)


def call(kernel, outs, args, specs=None, scratch=(), name=None):
    return pl.pallas_call(
        kernel,
        out_shape=[jax.ShapeDtypeStruct(s, d) for s, d in outs],
        in_specs=specs or [vmem()] * len(args),
        out_specs=[vmem()] * len(outs),
        scratch_shapes=list(scratch),
        compiler_params=pltpu.CompilerParams(vmem_limit_bytes=20 * 2**20),
        cost_estimate=pl.CostEstimate(flops=1000, bytes_accessed=1000, transcendentals=0),
        name=name,
    )(*args)


def split(value):
    high = value.astype(bf16)
    return high, (value - high.astype(f32)).astype(bf16)


def dot(a, b):
    return jnp.dot(a, b, preferred_element_type=f32)


def dot_last(a, b):
    return lax.dot_general(a, b, LAST, preferred_element_type=f32)


def join_pieces(ref, first):
    rows = []
    for band in range(8):
        blocks = [
            ref[band * 2 + half, first + part * 8 : first + part * 8 + 8, :]
            for half in range(2)
            for part in range(4)
        ]
        rows.append(jnp.concatenate(blocks, axis=1))
    return jnp.concatenate(rows, axis=0)


def prepare(exc_hbm, loads_hbm, skin_hbm, skout_hbm, drive_ref, low_ref, msg_ref, exc, loads, skin, skout, sems):
    pairs = ((exc_hbm, exc), (skin_hbm, skin), (loads_hbm, loads), (skout_hbm, skout))
    copies = [pltpu.make_async_copy(src, dst, sems.at[i]) for i, (src, dst) in enumerate(pairs)]
    for copy in copies:
        copy.start()
    copies[0].wait()
    drive = exc[...].astype(bf16)
    for part in range(2):
        drive_ref[part] = drive[:, part * 256 : part * 256 + 256]
    copies[1].wait()
    charges = dot_last(drive, skin[...])
    for piece in range(16):
        row = piece // 2 * 8
        for part in range(4):
            col = piece % 2 * 512 + part * 128
            msg_ref[piece, part * 8 : part * 8 + 8, :] = charges[row : row + 8, col : col + 128].astype(bf16)
    copies[2].wait()
    low = loads[...].astype(bf16)
    for part in range(2):
        low_ref[part] = low[:, part * 256 : part * 256 + 256]
    twice = jnp.concatenate([low, low], axis=0)
    copies[3].wait()
    gradient = dot_last(skout[...], twice)
    left = lax.broadcasted_iota(jnp.int32, (32, 128), 1) < 64
    for piece in range(16):
        k = piece * 64
        high, rest = split(jnp.where(left, gradient[k : k + 32], gradient[k + 32 : k + 64]))
        msg_ref[piece, 32:64, :] = high
        msg_ref[piece, 64:96, :] = rest


def split_translation(trans_hbm, out_ref, blocks, sems):
    copies = [pltpu.make_async_copy(trans_hbm.at[0, d], blocks.at[d], sems.at[d]) for d in range(15)]
    for copy in copies:
        copy.start()
    for d in range(15):
        copies[d].wait()
        high, low = split(blocks[d])
        out_ref[d, :64] = high
        out_ref[d, 64:] = low


def lags(parity):
    cluster = lax.axis_index(BLK)
    return [lax.rem(cluster - (2 * q + parity) + 16, 16) for q in range(8)]


def fetch(parts_hbm, blocks, sems, lag):
    copies = []
    for index, behind in enumerate(lag):
        source = parts_hbm.at[jnp.maximum(behind - 1, 0)]
        copies.append(pltpu.make_async_copy(source, blocks.at[index], sems.at[index]))
        copies[index].start()
    return copies


def term(both, block):
    pair = dot(both, block[:64])
    return pair[:64] + pair[64:] + dot(both[:64], block[64:])


def other_terms(msg_ref, parts_hbm, copies_ref, grad_ref, send_ref, blocks, sems):
    fetched = fetch(parts_hbm, blocks, sems, lags(1 - lax.axis_index("core")))
    share = jnp.sum(msg_ref[:, 0:32, :].astype(f32), axis=0).astype(bf16)
    for piece in range(16):
        copies_ref[piece] = share
    packed = jnp.sum(msg_ref[:, 32:64, :].astype(f32) + msg_ref[:, 64:96, :].astype(f32), axis=0)
    gradient = jnp.concatenate([packed, pltpu.roll(packed, 64, 1)], axis=0)
    high, low = split(gradient.T[:64])
    both = jnp.concatenate([high, low], axis=0)
    grad_ref[...] = both
    for index in range(8):
        fetched[index].wait()
        send_ref[index] = term(both, blocks[index])


def own_terms(grad_ref, came_ref, parts_hbm, out_ref, blocks, sems):
    lag = lags(lax.axis_index("core"))
    fetched = fetch(parts_hbm, blocks, sems, lag)
    both = grad_ref[...]
    for index in range(8):
        fetched[index].wait()
        value = jnp.where(lag[index] == 0, 0.0, term(both, blocks[index]))
        out_ref[index] = (value + came_ref[index]).astype(bf16)


def pack(own_ref, pieces_ref, out_ref):
    charges = join_pieces(pieces_ref, 0)
    for q in range(8):
        out_ref[q, 0] = own_ref[q]
        out_ref[q, 1] = charges


def unpack(came_ref, msg_ref):
    total = came_ref[0, 0].astype(f32)
    for q in range(1, 8):
        total = total + came_ref[q, 0].astype(f32)
    for piece in range(16):
        row = piece // 2 * 8
        for part in range(4):
            col = piece % 2 * 512 + part * 128
            msg_ref[piece, part * 8 : part * 8 + 8, :] = total[row : row + 8, col : col + 128].astype(bf16)


def forward(other_ref, came_ref, parts_ref, pot_ref):
    core = lax.axis_index("core")
    lag = lags(1 - core) + lags(core)
    total = jnp.zeros((64, 64), f32)
    for index in range(16):
        charges = other_ref[index, 1] if index < 8 else came_ref[index - 8, 1]
        pair = dot_last(parts_ref[jnp.maximum(lag[index] - 1, 0)], charges)
        total = total + jnp.where(lag[index] == 0, 0.0, pair[:64] + pair[64:])
    pot_ref[...] = jnp.concatenate([total[:32], total[32:]], axis=1).astype(bf16)


def near(count_ref, rows_ref, cols_ref, low_ref, tiles_hbm, *refs):
    pieces, refs = refs[:8], refs[8:]
    ahead_ref, keep_ref, across_ref, beside_ref, both_ref, acc, behind, drives, tiles_ref, tile_sems, piece_sems = refs

    def tile_copy(index):
        span = pl.ds(index * 4, 4)
        return pltpu.make_async_copy(tiles_hbm.at[span], tiles_ref.at[span], tile_sems.at[index])

    arriving = [
        pltpu.make_async_copy(pieces[index], drives.at[index], piece_sems.at[index]) for index in range(8)
    ]
    for copy in arriving:
        copy.start()
    for index in range(8):
        tile_copy(index).start()
    acc[...] = jnp.zeros_like(acc)
    behind[...] = jnp.zeros_like(behind)
    for copy in arriving:
        copy.wait()
    count = count_ref[0]
    my_z = lax.axis_index("z")
    my_half = lax.axis_index("xhi")
    group = 4

    def step(index, carry):
        tile_copy(index).wait()
        results = []
        for part in range(group):
            slot = index * group + part
            row = rows_ref[slot]
            col = cols_ref[slot]
            owner = col // 2
            hops = lax.rem(my_z - lax.rem(owner, 8) + 8, 8)
            side = lax.rem(owner // 8 + my_half, 2)
            tile = tiles_ref[slot]
            fwd = dot_last(drives[hops, side, lax.rem(col, 2)], tile)
            bwd = dot(low_ref[row], tile)
            results.append((slot < count, row, col, fwd, bwd))
        for live, row, col, fwd, bwd in results:
            acc[row] += jnp.where(live, fwd, 0.0)
            behind[col] += jnp.where(live, bwd, 0.0)
        return carry

    groups = (count + group - 1) // group
    lax.fori_loop(0, groups, step, 0)

    def drain(index, carry):
        tile_copy(index).wait()
        return carry

    lax.fori_loop(groups, 8, drain, 0)
    for part in range(2):
        ahead_ref[:, part * 256 : part * 256 + 256] = acc[part]
    parity = lax.rem(my_z, 2)
    mine = pl.ds(pl.multiple_of(parity * 128, 128), 128)
    theirs = pl.ds(pl.multiple_of((1 - parity) * 128, 128), 128)
    for target in range(16):
        keep_ref[target] = behind[2 * target + my_half, :, mine].astype(bf16)
        across_ref[target] = behind[2 * target + 1 - my_half, :, mine].astype(bf16)
        beside_ref[target] = behind[2 * target + my_half, :, theirs].astype(bf16)
        both_ref[target] = behind[2 * target + 1 - my_half, :, theirs].astype(bf16)


def last_message(adj_ref, pot_ref, keep_hbm, across_ref, beside_ref, both_ref, out_ref, keep_ref, sem):
    copy = pltpu.make_async_copy(keep_hbm, keep_ref, sem)
    copy.start()
    adjoint = jnp.sum(adj_ref[...].astype(f32), axis=0).astype(bf16)
    for piece in range(16):
        out_ref[piece, 0:32, :] = adjoint
        out_ref[piece, 32:64, :] = pot_ref[...]
    copy.wait()
    for piece in range(16):
        near_sum = keep_ref[piece].astype(f32) + across_ref[piece].astype(f32)
        near_sum = near_sum + beside_ref[piece].astype(f32) + both_ref[piece].astype(f32)
        out_ref[piece, 64:128, :] = near_sum.astype(bf16)


def stage(*refs):
    sources, targets, sems = refs[:3], refs[3:6], refs[6]
    copies = [pltpu.make_async_copy(sources[i], targets[i], sems.at[i]) for i in range(3)]
    for copy in copies:
        copy.start()
    for copy in copies:
        copy.wait()


def finish(msg_ref, skin_ref, skout_ref, ahead_ref, resp_ref, sens_ref):
    adjoint = join_pieces(msg_ref, 0)
    packed = jnp.concatenate([msg_ref[r, 32:64, :] for r in range(16)], axis=0)
    packed = packed.astype(f32).T.astype(bf16)
    near_sums = []
    for block in range(2):
        for parity in range(2):
            value = msg_ref[block * 8 + parity, 64:128, :].astype(f32)
            for z in range(parity + 2, 8, 2):
                value = value + msg_ref[block * 8 + z, 64:128, :].astype(f32)
            near_sums.append(value)
    sens_ref[...] = dot(adjoint, skin_ref[...]) + jnp.concatenate(near_sums, axis=1)
    upper = jnp.concatenate([skout_ref[r * 64 : r * 64 + 32, :] for r in range(16)], axis=0)
    lower = jnp.concatenate([skout_ref[r * 64 + 32 : r * 64 + 64, :] for r in range(16)], axis=0)
    resp_ref[...] = ahead_ref[...] + dot(packed[:64], upper) + dot(packed[64:], lower)


def swap(value, axis):
    return lax.ppermute(value, axis, [(0, 1), (1, 0)])


def exchange(value, axes):
    return lax.all_to_all(value, axes, 0, 0, tiled=True)


def in_hbm(value):
    return pltpu.with_memory_space_constraint(value, pltpu.HBM)


def shift(value, step):
    return lax.ppermute(value, "z", [(i, (i + step) % 8) for i in range(8)])


def tie(*values):
    return lax.optimization_barrier(values)


def on_device(exc, loads, tiles, tile_rows, tile_cols, tile_count, skin, skout, trans):
    drive, low, msg = call(
        prepare,
        [((2, 64, 256), bf16), ((2, 64, 256), bf16), ((16, 96, 128), bf16)],
        [in_hbm(exc), in_hbm(loads), in_hbm(skin), in_hbm(skout)],
        specs=[hbm()] * 4,
        scratch=[pltpu.VMEM((64, 512), f32)] * 2
        + [pltpu.VMEM((1024, 512), bf16)] * 2
        + [pltpu.SemaphoreType.DMA((4,))],
        name="prepare",
    )
    mate = swap(drive, "xhi")
    (parts,) = call(
        split_translation,
        [((15, 128, 1024), bf16)],
        [in_hbm(trans)],
        specs=[hbm()],
        scratch=[pltpu.VMEM((15, 64, 1024), f32), pltpu.SemaphoreType.DMA((15,))],
        name="split_translation",
    )
    msg, mate, parts = tie(exchange(msg, ROWS), mate, parts)
    blocks = [pltpu.VMEM((8, 128, 1024), bf16), pltpu.SemaphoreType.DMA((8,))]
    copies, gradient, send = call(
        other_terms,
        [((16, 32, 128), bf16), ((128, 64), bf16), ((8, 64, 1024), f32)],
        [msg, in_hbm(parts)],
        specs=[vmem(), hbm()],
        scratch=blocks,
        name="other_terms",
    )
    here = jnp.stack([drive, mate])
    up1, down1 = shift(here, 1), shift(here, -1)
    (own,) = call(
        own_terms,
        [((8, 64, 1024), bf16)],
        [gradient, swap(send, "core"), in_hbm(parts)],
        specs=[vmem(), vmem(), hbm()],
        scratch=blocks,
        name="own_terms",
    )
    copies, up1, down1, own = tie(exchange(copies, ROWS), up1, down1, own)
    (both,) = call(pack, [((8, 2, 64, 1024), bf16)], [own, copies], name="pack")
    up2, down2 = shift(up1, 1), shift(down1, -1)
    up3, down3 = shift(up2, 1), shift(down2, -1)
    up4 = shift(up3, 1)
    ahead, keep, *quarters = call(
        near,
        [((64, 512), f32)] + [((16, 64, 128), bf16)] * 4,
        [tile_count, tile_rows, tile_cols, low, in_hbm(tiles)]
        + [in_hbm(piece) for piece in (here, up1, up2, up3, up4, down3, down2, down1)],
        specs=[smem(), smem(), smem(), vmem()] + [hbm()] * 9,
        scratch=[
            pltpu.VMEM((2, 64, 256), f32),
            pltpu.VMEM((32, 64, 256), f32),
            pltpu.VMEM((8, 2, 2, 64, 256), bf16),
            pltpu.VMEM((32, 256, 256), bf16),
            pltpu.SemaphoreType.DMA((8,)),
            pltpu.SemaphoreType.DMA((8,)),
        ],
        name="near",
    )
    both, ahead = tie(exchange(both, FACE), ahead)
    quarters = [
        lax.ppermute(value, ROWS, [(i, i ^ mask) for i in range(16)])
        for value, mask in zip(quarters, (8, 1, 9))
    ]
    (adjoint,) = call(unpack, [((16, 32, 128), bf16)], [both], name="unpack")
    others = swap(both, "core")
    (potential,) = call(
        forward,
        [((32, 128), bf16)],
        [others, both, parts],
        name="forward",
    )
    adjoint, potential, *quarters = tie(exchange(adjoint, ROWS), potential, *quarters)
    (last,) = call(
        last_message,
        [((16, 128, 128), bf16)],
        [adjoint, potential, in_hbm(keep), *quarters],
        specs=[vmem()] * 2 + [hbm()] + [vmem()] * 3,
        scratch=[pltpu.VMEM((16, 64, 128), bf16), pltpu.SemaphoreType.DMA],
        name="last_message",
    )
    staged = call(
        stage,
        [((1024, 512), bf16), ((1024, 512), bf16), ((64, 512), f32)],
        [in_hbm(skin), in_hbm(skout), in_hbm(ahead)],
        specs=[hbm()] * 3,
        scratch=[pltpu.SemaphoreType.DMA((3,))],
        name="stage",
    )
    last, *staged = tie(exchange(last, ROWS), *staged)
    return tuple(call(finish, [((64, 512), f32), ((64, 512), f32)], [last, *staged], name="finish"))


def solution(mesh):
    fine = Mesh(mesh.devices.reshape(2, 4, 2, 2, 8), BLK + ROWS)
    every = BLK + ROWS
    return jax.shard_map(
        on_device,
        mesh=fine,
        in_specs=(
            P(None, every),
            P(None, every),
            P(every, None, None),
            P(every),
            P(every),
            P(every),
            P(None, every),
            P(None, every),
            P(BLK, None, ROWS, None),
        ),
        out_specs=(P(None, every), P(None, every)),
        check_vma=False,
    )
```

```python
import jax
import jax.numpy as jnp
from jax import lax
from jax.experimental import pallas as pl
from jax.experimental.pallas import tpu as pltpu
from jax.sharding import Mesh
from jax.sharding import PartitionSpec as P

BLK = ("xlo", "y", "core")
ROWS = ("xhi", "z")
FACE = ("xlo", "y")
bf16 = jnp.bfloat16
f32 = jnp.float32
LAST = (((1,), (1,)), ((), ()))


def vmem():
    return pl.BlockSpec(memory_space=pltpu.VMEM)


def smem():
    return pl.BlockSpec(memory_space=pltpu.SMEM)


def hbm():
    return pl.BlockSpec(memory_space=pltpu.HBM)


def call(kernel, outs, args, specs=None, scratch=(), name=None):
    return pl.pallas_call(
        kernel,
        out_shape=[jax.ShapeDtypeStruct(s, d) for s, d in outs],
        in_specs=specs or [vmem()] * len(args),
        out_specs=[vmem()] * len(outs),
        scratch_shapes=list(scratch),
        compiler_params=pltpu.CompilerParams(vmem_limit_bytes=20 * 2**20),
        cost_estimate=pl.CostEstimate(flops=1000, bytes_accessed=1000, transcendentals=0),
        name=name,
    )(*args)


def split(value):
    high = value.astype(bf16)
    return high, (value - high.astype(f32)).astype(bf16)


def dot(a, b):
    return jnp.dot(a, b, preferred_element_type=f32)


def dot_last(a, b):
    return lax.dot_general(a, b, LAST, preferred_element_type=f32)


def join_pieces(ref, first):
    rows = []
    for band in range(8):
        blocks = [
            ref[band * 2 + half, first + part * 8 : first + part * 8 + 8, :]
            for half in range(2)
            for part in range(4)
        ]
        rows.append(jnp.concatenate(blocks, axis=1))
    return jnp.concatenate(rows, axis=0)


def prepare(exc_hbm, loads_hbm, skin_hbm, skout_hbm, drive_ref, low_ref, msg_ref, exc, loads, skin, skout, sems):
    pairs = ((exc_hbm, exc), (skin_hbm, skin), (loads_hbm, loads), (skout_hbm, skout))
    copies = [pltpu.make_async_copy(src, dst, sems.at[i]) for i, (src, dst) in enumerate(pairs)]
    for copy in copies:
        copy.start()
    copies[0].wait()
    drive = exc[...].astype(bf16)
    for part in range(2):
        drive_ref[part] = drive[:, part * 256 : part * 256 + 256]
    copies[1].wait()
    charges = dot_last(drive, skin[...])
    for piece in range(16):
        row = piece // 2 * 8
        for part in range(4):
            col = piece % 2 * 512 + part * 128
            msg_ref[piece, part * 8 : part * 8 + 8, :] = charges[row : row + 8, col : col + 128].astype(bf16)
    copies[2].wait()
    low = loads[...].astype(bf16)
    for part in range(2):
        low_ref[part] = low[:, part * 256 : part * 256 + 256]
    twice = jnp.concatenate([low, low], axis=0)
    copies[3].wait()
    gradient = dot_last(skout[...], twice)
    left = lax.broadcasted_iota(jnp.int32, (32, 128), 1) < 64
    for piece in range(16):
        k = piece * 64
        high, rest = split(jnp.where(left, gradient[k : k + 32], gradient[k + 32 : k + 64]))
        msg_ref[piece, 32:64, :] = high
        msg_ref[piece, 64:96, :] = rest


def split_translation(trans_hbm, out_ref, blocks, sems):
    copies = [pltpu.make_async_copy(trans_hbm.at[0, d], blocks.at[d], sems.at[d]) for d in range(15)]
    for copy in copies:
        copy.start()
    for d in range(15):
        copies[d].wait()
        high, low = split(blocks[d])
        out_ref[d, :64] = high
        out_ref[d, 64:] = low


def lags(parity):
    cluster = lax.axis_index(BLK)
    return [lax.rem(cluster - (2 * q + parity) + 16, 16) for q in range(8)]


def fetch(parts_hbm, blocks, sems, lag):
    copies = []
    for index, behind in enumerate(lag):
        source = parts_hbm.at[jnp.maximum(behind - 1, 0)]
        copies.append(pltpu.make_async_copy(source, blocks.at[index], sems.at[index]))
        copies[index].start()
    return copies


def term(both, block):
    pair = dot(both, block[:64])
    return pair[:64] + pair[64:] + dot(both[:64], block[64:])


def other_terms(msg_ref, parts_hbm, copies_ref, grad_ref, send_ref, blocks, sems):
    fetched = fetch(parts_hbm, blocks, sems, lags(1 - lax.axis_index("core")))
    share = jnp.sum(msg_ref[:, 0:32, :].astype(f32), axis=0).astype(bf16)
    for piece in range(16):
        copies_ref[piece] = share
    packed = jnp.sum(msg_ref[:, 32:64, :].astype(f32) + msg_ref[:, 64:96, :].astype(f32), axis=0)
    gradient = jnp.concatenate([packed, pltpu.roll(packed, 64, 1)], axis=0)
    high, low = split(gradient.T[:64])
    both = jnp.concatenate([high, low], axis=0)
    grad_ref[...] = both
    for index in range(8):
        fetched[index].wait()
        send_ref[index] = term(both, blocks[index])


def own_terms(grad_ref, came_ref, parts_hbm, out_ref, blocks, sems):
    lag = lags(lax.axis_index("core"))
    fetched = fetch(parts_hbm, blocks, sems, lag)
    both = grad_ref[...]
    for index in range(8):
        fetched[index].wait()
        value = jnp.where(lag[index] == 0, 0.0, term(both, blocks[index]))
        out_ref[index] = (value + came_ref[index]).astype(bf16)


def pack(own_ref, pieces_ref, out_ref):
    charges = join_pieces(pieces_ref, 0)
    for q in range(8):
        out_ref[q, 0] = own_ref[q]
        out_ref[q, 1] = charges


def unpack(came_ref, msg_ref):
    total = came_ref[0, 0].astype(f32)
    for q in range(1, 8):
        total = total + came_ref[q, 0].astype(f32)
    for piece in range(16):
        row = piece // 2 * 8
        for part in range(4):
            col = piece % 2 * 512 + part * 128
            msg_ref[piece, part * 8 : part * 8 + 8, :] = total[row : row + 8, col : col + 128].astype(bf16)


def forward(other_ref, came_ref, parts_ref, pot_ref):
    core = lax.axis_index("core")
    lag = lags(1 - core) + lags(core)
    total = jnp.zeros((64, 64), f32)
    for index in range(16):
        charges = other_ref[index, 1] if index < 8 else came_ref[index - 8, 1]
        pair = dot_last(parts_ref[jnp.maximum(lag[index] - 1, 0)], charges)
        total = total + jnp.where(lag[index] == 0, 0.0, pair[:64] + pair[64:])
    pot_ref[...] = jnp.concatenate([total[:32], total[32:]], axis=1).astype(bf16)


def near(count_ref, rows_ref, cols_ref, low_ref, tiles_ref, *refs):
    pieces, refs = refs[:8], refs[8:]
    ahead_ref, keep_ref, across_ref, beside_ref, both_ref, acc, behind, drives, piece_sems = refs

    arriving = [
        pltpu.make_async_copy(pieces[index], drives.at[index], piece_sems.at[index]) for index in range(8)
    ]
    for copy in arriving:
        copy.start()
    acc[...] = jnp.zeros_like(acc)
    behind[...] = jnp.zeros_like(behind)
    for copy in arriving:
        copy.wait()
    count = count_ref[0]
    my_z = lax.axis_index("z")
    my_half = lax.axis_index("xhi")
    group = 4

    def step(index, carry):
        results = []
        for part in range(group):
            slot = index * group + part
            row = rows_ref[slot]
            col = cols_ref[slot]
            owner = col // 2
            hops = lax.rem(my_z - lax.rem(owner, 8) + 8, 8)
            side = lax.rem(owner // 8 + my_half, 2)
            tile = tiles_ref[slot]
            fwd = dot_last(drives[hops, side, lax.rem(col, 2)], tile)
            bwd = dot(low_ref[row], tile)
            results.append((slot < count, row, col, fwd, bwd))
        for live, row, col, fwd, bwd in results:
            acc[row] += jnp.where(live, fwd, 0.0)
            behind[col] += jnp.where(live, bwd, 0.0)
        return carry

    lax.fori_loop(0, (count + group - 1) // group, step, 0)
    for part in range(2):
        ahead_ref[:, part * 256 : part * 256 + 256] = acc[part]
    parity = lax.rem(my_z, 2)
    mine = pl.ds(pl.multiple_of(parity * 128, 128), 128)
    theirs = pl.ds(pl.multiple_of((1 - parity) * 128, 128), 128)
    for target in range(16):
        keep_ref[target] = behind[2 * target + my_half, :, mine].astype(bf16)
        across_ref[target] = behind[2 * target + 1 - my_half, :, mine].astype(bf16)
        beside_ref[target] = behind[2 * target + my_half, :, theirs].astype(bf16)
        both_ref[target] = behind[2 * target + 1 - my_half, :, theirs].astype(bf16)


def last_message(adj_ref, pot_ref, keep_hbm, across_ref, beside_ref, both_ref, out_ref, keep_ref, sem):
    copy = pltpu.make_async_copy(keep_hbm, keep_ref, sem)
    copy.start()
    adjoint = jnp.sum(adj_ref[...].astype(f32), axis=0).astype(bf16)
    for piece in range(16):
        out_ref[piece, 0:32, :] = adjoint
        out_ref[piece, 32:64, :] = pot_ref[...]
    copy.wait()
    for piece in range(16):
        near_sum = keep_ref[piece].astype(f32) + across_ref[piece].astype(f32)
        near_sum = near_sum + beside_ref[piece].astype(f32) + both_ref[piece].astype(f32)
        out_ref[piece, 64:128, :] = near_sum.astype(bf16)


def stage(*refs):
    sources, targets, sems = refs[:3], refs[3:6], refs[6]
    copies = [pltpu.make_async_copy(sources[i], targets[i], sems.at[i]) for i in range(3)]
    for copy in copies:
        copy.start()
    for copy in copies:
        copy.wait()


def finish(msg_ref, skin_ref, skout_ref, ahead_ref, resp_ref, sens_ref):
    adjoint = join_pieces(msg_ref, 0)
    packed = jnp.concatenate([msg_ref[r, 32:64, :] for r in range(16)], axis=0)
    packed = packed.astype(f32).T.astype(bf16)
    near_sums = []
    for block in range(2):
        for parity in range(2):
            value = msg_ref[block * 8 + parity, 64:128, :].astype(f32)
            for z in range(parity + 2, 8, 2):
                value = value + msg_ref[block * 8 + z, 64:128, :].astype(f32)
            near_sums.append(value)
    sens_ref[...] = dot(adjoint, skin_ref[...]) + jnp.concatenate(near_sums, axis=1)
    upper = jnp.concatenate([skout_ref[r * 64 : r * 64 + 32, :] for r in range(16)], axis=0)
    lower = jnp.concatenate([skout_ref[r * 64 + 32 : r * 64 + 64, :] for r in range(16)], axis=0)
    resp_ref[...] = ahead_ref[...] + dot(packed[:64], upper) + dot(packed[64:], lower)


def swap(value, axis):
    return lax.ppermute(value, axis, [(0, 1), (1, 0)])


def exchange(value, axes):
    return lax.all_to_all(value, axes, 0, 0, tiled=True)


def in_hbm(value):
    return pltpu.with_memory_space_constraint(value, pltpu.HBM)


def shift(value, step):
    return lax.ppermute(value, "z", [(i, (i + step) % 8) for i in range(8)])


def tie(*values):
    return lax.optimization_barrier(values)


def on_device(exc, loads, tiles, tile_rows, tile_cols, tile_count, skin, skout, trans):
    drive, low, msg = call(
        prepare,
        [((2, 64, 256), bf16), ((2, 64, 256), bf16), ((16, 96, 128), bf16)],
        [in_hbm(exc), in_hbm(loads), in_hbm(skin), in_hbm(skout)],
        specs=[hbm()] * 4,
        scratch=[pltpu.VMEM((64, 512), f32)] * 2
        + [pltpu.VMEM((1024, 512), bf16)] * 2
        + [pltpu.SemaphoreType.DMA((4,))],
        name="prepare",
    )
    mate = swap(drive, "xhi")
    (parts,) = call(
        split_translation,
        [((15, 128, 1024), bf16)],
        [in_hbm(trans)],
        specs=[hbm()],
        scratch=[pltpu.VMEM((15, 64, 1024), f32), pltpu.SemaphoreType.DMA((15,))],
        name="split_translation",
    )
    msg, mate, parts = tie(exchange(msg, ROWS), mate, parts)
    blocks = [pltpu.VMEM((8, 128, 1024), bf16), pltpu.SemaphoreType.DMA((8,))]
    copies, gradient, send = call(
        other_terms,
        [((16, 32, 128), bf16), ((128, 64), bf16), ((8, 64, 1024), f32)],
        [msg, in_hbm(parts)],
        specs=[vmem(), hbm()],
        scratch=blocks,
        name="other_terms",
    )
    here = jnp.stack([drive, mate])
    up1, down1 = shift(here, 1), shift(here, -1)
    (own,) = call(
        own_terms,
        [((8, 64, 1024), bf16)],
        [gradient, swap(send, "core"), in_hbm(parts)],
        specs=[vmem(), vmem(), hbm()],
        scratch=blocks,
        name="own_terms",
    )
    copies, up1, down1, own = tie(exchange(copies, ROWS), up1, down1, own)
    (both,) = call(pack, [((8, 2, 64, 1024), bf16)], [own, copies], name="pack")
    up2, down2 = shift(up1, 1), shift(down1, -1)
    up3, down3 = shift(up2, 1), shift(down2, -1)
    up4 = shift(up3, 1)
    ahead, keep, *quarters = call(
        near,
        [((64, 512), f32)] + [((16, 64, 128), bf16)] * 4,
        [tile_count, tile_rows, tile_cols, low, tiles]
        + [in_hbm(piece) for piece in (here, up1, up2, up3, up4, down3, down2, down1)],
        specs=[smem(), smem(), smem(), vmem(), vmem()] + [hbm()] * 8,
        scratch=[
            pltpu.VMEM((2, 64, 256), f32),
            pltpu.VMEM((32, 64, 256), f32),
            pltpu.VMEM((8, 2, 2, 64, 256), bf16),
            pltpu.SemaphoreType.DMA((8,)),
        ],
        name="near",
    )
    both, ahead = tie(exchange(both, FACE), ahead)
    quarters = [
        lax.ppermute(value, ROWS, [(i, i ^ mask) for i in range(16)])
        for value, mask in zip(quarters, (8, 1, 9))
    ]
    (adjoint,) = call(unpack, [((16, 32, 128), bf16)], [both], name="unpack")
    others = swap(both, "core")
    (potential,) = call(
        forward,
        [((32, 128), bf16)],
        [others, both, parts],
        name="forward",
    )
    adjoint, potential, *quarters = tie(exchange(adjoint, ROWS), potential, *quarters)
    (last,) = call(
        last_message,
        [((16, 128, 128), bf16)],
        [adjoint, potential, in_hbm(keep), *quarters],
        specs=[vmem()] * 2 + [hbm()] + [vmem()] * 3,
        scratch=[pltpu.VMEM((16, 64, 128), bf16), pltpu.SemaphoreType.DMA],
        name="last_message",
    )
    staged = call(
        stage,
        [((1024, 512), bf16), ((1024, 512), bf16), ((64, 512), f32)],
        [in_hbm(skin), in_hbm(skout), in_hbm(ahead)],
        specs=[hbm()] * 3,
        scratch=[pltpu.SemaphoreType.DMA((3,))],
        name="stage",
    )
    last, *staged = tie(exchange(last, ROWS), *staged)
    return tuple(call(finish, [((64, 512), f32), ((64, 512), f32)], [last, *staged], name="finish"))


def solution(mesh):
    fine = Mesh(mesh.devices.reshape(2, 4, 2, 2, 8), BLK + ROWS)
    every = BLK + ROWS
    return jax.shard_map(
        on_device,
        mesh=fine,
        in_specs=(
            P(None, every),
            P(None, every),
            P(every, None, None),
            P(every),
            P(every),
            P(every),
            P(None, every),
            P(None, every),
            P(BLK, None, ROWS, None),
        ),
        out_specs=(P(None, every), P(None, every)),
        check_vma=False,
    )
```

```python
import jax
import jax.numpy as jnp
from jax import lax
from jax.experimental import pallas as pl
from jax.experimental.pallas import tpu as pltpu
from jax.sharding import Mesh
from jax.sharding import PartitionSpec as P

BLK = ("xlo", "y", "core")
ROWS = ("xhi", "z")
FACE = ("xlo", "y")
bf16 = jnp.bfloat16
f32 = jnp.float32
LAST = (((1,), (1,)), ((), ()))


def vmem():
    return pl.BlockSpec(memory_space=pltpu.VMEM)


def smem():
    return pl.BlockSpec(memory_space=pltpu.SMEM)


def hbm():
    return pl.BlockSpec(memory_space=pltpu.HBM)


def call(kernel, outs, args, specs=None, scratch=(), name=None):
    return pl.pallas_call(
        kernel,
        out_shape=[jax.ShapeDtypeStruct(s, d) for s, d in outs],
        in_specs=specs or [vmem()] * len(args),
        out_specs=[vmem()] * len(outs),
        scratch_shapes=list(scratch),
        compiler_params=pltpu.CompilerParams(vmem_limit_bytes=20 * 2**20),
        cost_estimate=pl.CostEstimate(flops=1000, bytes_accessed=1000, transcendentals=0),
        name=name,
    )(*args)


def split(value):
    high = value.astype(bf16)
    return high, (value - high.astype(f32)).astype(bf16)


def dot(a, b):
    return jnp.dot(a, b, preferred_element_type=f32)


def dot_last(a, b):
    return lax.dot_general(a, b, LAST, preferred_element_type=f32)


def join_pieces(ref, first):
    rows = []
    for band in range(8):
        blocks = [
            ref[band * 2 + half, first + part * 8 : first + part * 8 + 8, :]
            for half in range(2)
            for part in range(4)
        ]
        rows.append(jnp.concatenate(blocks, axis=1))
    return jnp.concatenate(rows, axis=0)


def prepare(exc_hbm, loads_hbm, skin_hbm, skout_hbm, drive_ref, low_ref, msg_ref, exc, loads, skin, skout, sems):
    pairs = ((exc_hbm, exc), (skin_hbm, skin), (loads_hbm, loads), (skout_hbm, skout))
    copies = [pltpu.make_async_copy(src, dst, sems.at[i]) for i, (src, dst) in enumerate(pairs)]
    for copy in copies:
        copy.start()
    copies[0].wait()
    drive = exc[...].astype(bf16)
    for part in range(2):
        drive_ref[part] = drive[:, part * 256 : part * 256 + 256]
    copies[1].wait()
    charges = dot_last(drive, skin[...])
    for piece in range(16):
        row = piece // 2 * 8
        for part in range(4):
            col = piece % 2 * 512 + part * 128
            msg_ref[piece, part * 8 : part * 8 + 8, :] = charges[row : row + 8, col : col + 128].astype(bf16)
    copies[2].wait()
    low = loads[...].astype(bf16)
    for part in range(2):
        low_ref[part] = low[:, part * 256 : part * 256 + 256]
    twice = jnp.concatenate([low, low], axis=0)
    copies[3].wait()
    gradient = dot_last(skout[...], twice)
    left = lax.broadcasted_iota(jnp.int32, (32, 128), 1) < 64
    for piece in range(16):
        k = piece * 64
        high, rest = split(jnp.where(left, gradient[k : k + 32], gradient[k + 32 : k + 64]))
        msg_ref[piece, 32:64, :] = high
        msg_ref[piece, 64:96, :] = rest


def split_translation(trans_hbm, out_ref, blocks, sems):
    copies = [pltpu.make_async_copy(trans_hbm.at[0, d], blocks.at[d], sems.at[d]) for d in range(15)]
    for copy in copies:
        copy.start()
    for d in range(15):
        copies[d].wait()
        high, low = split(blocks[d])
        out_ref[d, :64] = high
        out_ref[d, 64:] = low


def lags(parity):
    cluster = lax.axis_index(BLK)
    return [lax.rem(cluster - (2 * q + parity) + 16, 16) for q in range(8)]


def fetch(parts_hbm, blocks, sems, lag):
    copies = []
    for index, behind in enumerate(lag):
        source = parts_hbm.at[jnp.maximum(behind - 1, 0)]
        copies.append(pltpu.make_async_copy(source, blocks.at[index], sems.at[index]))
        copies[index].start()
    return copies


def term(both, block):
    pair = dot(both, block[:64])
    return pair[:64] + pair[64:] + dot(both[:64], block[64:])


def other_terms(msg_ref, parts_hbm, copies_ref, grad_ref, send_ref, blocks, sems):
    fetched = fetch(parts_hbm, blocks, sems, lags(1 - lax.axis_index("core")))
    share = jnp.sum(msg_ref[:, 0:32, :].astype(f32), axis=0).astype(bf16)
    for piece in range(16):
        copies_ref[piece] = share
    packed = jnp.sum(msg_ref[:, 32:64, :].astype(f32) + msg_ref[:, 64:96, :].astype(f32), axis=0)
    gradient = jnp.concatenate([packed, pltpu.roll(packed, 64, 1)], axis=0)
    high, low = split(gradient.T[:64])
    both = jnp.concatenate([high, low], axis=0)
    grad_ref[...] = both
    for index in range(8):
        fetched[index].wait()
        send_ref[index] = term(both, blocks[index])


def own_terms(grad_ref, came_ref, parts_hbm, out_ref, blocks, sems):
    lag = lags(lax.axis_index("core"))
    fetched = fetch(parts_hbm, blocks, sems, lag)
    both = grad_ref[...]
    for index in range(8):
        fetched[index].wait()
        value = jnp.where(lag[index] == 0, 0.0, term(both, blocks[index]))
        out_ref[index] = (value + came_ref[index]).astype(bf16)


def pack(own_ref, pieces_ref, out_ref):
    charges = join_pieces(pieces_ref, 0)
    for q in range(8):
        out_ref[q, 0] = own_ref[q]
        out_ref[q, 1] = charges


def unpack(came_ref, msg_ref):
    total = came_ref[0, 0].astype(f32)
    for q in range(1, 8):
        total = total + came_ref[q, 0].astype(f32)
    for piece in range(16):
        row = piece // 2 * 8
        for part in range(4):
            col = piece % 2 * 512 + part * 128
            msg_ref[piece, part * 8 : part * 8 + 8, :] = total[row : row + 8, col : col + 128].astype(bf16)


def forward(other_ref, came_ref, parts_ref, pot_ref):
    core = lax.axis_index("core")
    lag = lags(1 - core) + lags(core)
    total = jnp.zeros((64, 64), f32)
    for index in range(16):
        charges = other_ref[index, 1] if index < 8 else came_ref[index - 8, 1]
        pair = dot_last(parts_ref[jnp.maximum(lag[index] - 1, 0)], charges)
        total = total + jnp.where(lag[index] == 0, 0.0, pair[:64] + pair[64:])
    pot_ref[...] = jnp.concatenate([total[:32], total[32:]], axis=1).astype(bf16)


def near(count_ref, rows_ref, cols_ref, low_ref, tiles_hbm, *refs):
    pieces, refs = refs[:8], refs[8:]
    ahead_ref, keep_ref, across_ref, beside_ref, both_ref, acc, behind, drives, tiles_ref, tile_sems, piece_sems = refs

    def tile_copy(index):
        span = pl.ds(index * 4, 4)
        return pltpu.make_async_copy(tiles_hbm.at[span], tiles_ref.at[span], tile_sems.at[index])

    arriving = [
        pltpu.make_async_copy(pieces[index], drives.at[index], piece_sems.at[index])
        for index in (0, 1, 2, 3, 6, 7)
    ]
    for copy in arriving:
        copy.start()
    for index in range(8):
        tile_copy(index).start()
    for index in (4, 5):
        drives[index] = pieces[index][...]
    acc[...] = jnp.zeros_like(acc)
    behind[...] = jnp.zeros_like(behind)
    for copy in arriving:
        copy.wait()
    count = count_ref[0]
    my_z = lax.axis_index("z")
    my_half = lax.axis_index("xhi")
    group = 4

    def step(index, carry):
        tile_copy(index).wait()
        results = []
        for part in range(group):
            slot = index * group + part
            row = rows_ref[slot]
            col = cols_ref[slot]
            owner = col // 2
            hops = lax.rem(my_z - lax.rem(owner, 8) + 8, 8)
            side = lax.rem(owner // 8 + my_half, 2)
            tile = tiles_ref[slot]
            fwd = dot_last(drives[hops, side, lax.rem(col, 2)], tile)
            bwd = dot(low_ref[row], tile)
            results.append((slot < count, row, col, fwd, bwd))
        for live, row, col, fwd, bwd in results:
            acc[row] += jnp.where(live, fwd, 0.0)
            behind[col] += jnp.where(live, bwd, 0.0)
        return carry

    groups = (count + group - 1) // group
    lax.fori_loop(0, groups, step, 0)

    def drain(index, carry):
        tile_copy(index).wait()
        return carry

    lax.fori_loop(groups, 8, drain, 0)
    for part in range(2):
        ahead_ref[:, part * 256 : part * 256 + 256] = acc[part]
    parity = lax.rem(my_z, 2)
    mine = pl.ds(pl.multiple_of(parity * 128, 128), 128)
    theirs = pl.ds(pl.multiple_of((1 - parity) * 128, 128), 128)
    for target in range(16):
        keep_ref[target] = behind[2 * target + my_half, :, mine].astype(bf16)
        across_ref[target] = behind[2 * target + 1 - my_half, :, mine].astype(bf16)
        beside_ref[target] = behind[2 * target + my_half, :, theirs].astype(bf16)
        both_ref[target] = behind[2 * target + 1 - my_half, :, theirs].astype(bf16)


def last_message(adj_ref, pot_ref, keep_hbm, across_ref, beside_ref, both_ref, out_ref, keep_ref, sem):
    copy = pltpu.make_async_copy(keep_hbm, keep_ref, sem)
    copy.start()
    adjoint = jnp.sum(adj_ref[...].astype(f32), axis=0).astype(bf16)
    for piece in range(16):
        out_ref[piece, 0:32, :] = adjoint
        out_ref[piece, 32:64, :] = pot_ref[...]
    copy.wait()
    for piece in range(16):
        near_sum = keep_ref[piece].astype(f32) + across_ref[piece].astype(f32)
        near_sum = near_sum + beside_ref[piece].astype(f32) + both_ref[piece].astype(f32)
        out_ref[piece, 64:128, :] = near_sum.astype(bf16)


def stage(*refs):
    sources, targets, sems = refs[:3], refs[3:6], refs[6]
    copies = [pltpu.make_async_copy(sources[i], targets[i], sems.at[i]) for i in range(3)]
    for copy in copies:
        copy.start()
    for copy in copies:
        copy.wait()


def finish(msg_ref, skin_ref, skout_ref, ahead_ref, resp_ref, sens_ref):
    adjoint = join_pieces(msg_ref, 0)
    packed = jnp.concatenate([msg_ref[r, 32:64, :] for r in range(16)], axis=0)
    packed = packed.astype(f32).T.astype(bf16)
    near_sums = []
    for block in range(2):
        for parity in range(2):
            value = msg_ref[block * 8 + parity, 64:128, :].astype(f32)
            for z in range(parity + 2, 8, 2):
                value = value + msg_ref[block * 8 + z, 64:128, :].astype(f32)
            near_sums.append(value)
    sens_ref[...] = dot(adjoint, skin_ref[...]) + jnp.concatenate(near_sums, axis=1)
    upper = jnp.concatenate([skout_ref[r * 64 : r * 64 + 32, :] for r in range(16)], axis=0)
    lower = jnp.concatenate([skout_ref[r * 64 + 32 : r * 64 + 64, :] for r in range(16)], axis=0)
    resp_ref[...] = ahead_ref[...] + dot(packed[:64], upper) + dot(packed[64:], lower)


def swap(value, axis):
    return lax.ppermute(value, axis, [(0, 1), (1, 0)])


def exchange(value, axes):
    return lax.all_to_all(value, axes, 0, 0, tiled=True)


def in_hbm(value):
    return pltpu.with_memory_space_constraint(value, pltpu.HBM)


def shift(value, step):
    return lax.ppermute(value, "z", [(i, (i + step) % 8) for i in range(8)])


def tie(*values):
    return lax.optimization_barrier(values)


def on_device(exc, loads, tiles, tile_rows, tile_cols, tile_count, skin, skout, trans):
    drive, low, msg = call(
        prepare,
        [((2, 64, 256), bf16), ((2, 64, 256), bf16), ((16, 96, 128), bf16)],
        [in_hbm(exc), in_hbm(loads), in_hbm(skin), in_hbm(skout)],
        specs=[hbm()] * 4,
        scratch=[pltpu.VMEM((64, 512), f32)] * 2
        + [pltpu.VMEM((1024, 512), bf16)] * 2
        + [pltpu.SemaphoreType.DMA((4,))],
        name="prepare",
    )
    mate = swap(drive, "xhi")
    (parts,) = call(
        split_translation,
        [((15, 128, 1024), bf16)],
        [in_hbm(trans)],
        specs=[hbm()],
        scratch=[pltpu.VMEM((15, 64, 1024), f32), pltpu.SemaphoreType.DMA((15,))],
        name="split_translation",
    )
    msg, mate, parts = tie(exchange(msg, ROWS), mate, parts)
    blocks = [pltpu.VMEM((8, 128, 1024), bf16), pltpu.SemaphoreType.DMA((8,))]
    copies, gradient, send = call(
        other_terms,
        [((16, 32, 128), bf16), ((128, 64), bf16), ((8, 64, 1024), f32)],
        [msg, in_hbm(parts)],
        specs=[vmem(), hbm()],
        scratch=blocks,
        name="other_terms",
    )
    here = jnp.stack([drive, mate])
    up1, down1 = shift(here, 1), shift(here, -1)
    (own,) = call(
        own_terms,
        [((8, 64, 1024), bf16)],
        [gradient, swap(send, "core"), in_hbm(parts)],
        specs=[vmem(), vmem(), hbm()],
        scratch=blocks,
        name="own_terms",
    )
    copies, up1, down1, own = tie(exchange(copies, ROWS), up1, down1, own)
    (both,) = call(pack, [((8, 2, 64, 1024), bf16)], [own, copies], name="pack")
    up2, down2 = shift(up1, 1), shift(down1, -1)
    up3, down3 = shift(up2, 1), shift(down2, -1)
    up4 = shift(up3, 1)
    ahead, keep, *quarters = call(
        near,
        [((64, 512), f32)] + [((16, 64, 128), bf16)] * 4,
        [tile_count, tile_rows, tile_cols, low, in_hbm(tiles)]
        + [in_hbm(piece) for piece in (here, up1, up2, up3)]
        + [up4, down3]
        + [in_hbm(piece) for piece in (down2, down1)],
        specs=[smem(), smem(), smem(), vmem()] + [hbm()] * 5 + [vmem()] * 2 + [hbm()] * 2,
        scratch=[
            pltpu.VMEM((2, 64, 256), f32),
            pltpu.VMEM((32, 64, 256), f32),
            pltpu.VMEM((8, 2, 2, 64, 256), bf16),
            pltpu.VMEM((32, 256, 256), bf16),
            pltpu.SemaphoreType.DMA((8,)),
            pltpu.SemaphoreType.DMA((8,)),
        ],
        name="near",
    )
    both, ahead = tie(exchange(both, FACE), ahead)
    quarters = [
        lax.ppermute(value, ROWS, [(i, i ^ mask) for i in range(16)])
        for value, mask in zip(quarters, (8, 1, 9))
    ]
    (adjoint,) = call(unpack, [((16, 32, 128), bf16)], [both], name="unpack")
    others = swap(both, "core")
    (potential,) = call(
        forward,
        [((32, 128), bf16)],
        [others, both, parts],
        name="forward",
    )
    adjoint, potential, *quarters = tie(exchange(adjoint, ROWS), potential, *quarters)
    (last,) = call(
        last_message,
        [((16, 128, 128), bf16)],
        [adjoint, potential, in_hbm(keep), *quarters],
        specs=[vmem()] * 2 + [hbm()] + [vmem()] * 3,
        scratch=[pltpu.VMEM((16, 64, 128), bf16), pltpu.SemaphoreType.DMA],
        name="last_message",
    )
    staged = call(
        stage,
        [((1024, 512), bf16), ((1024, 512), bf16), ((64, 512), f32)],
        [in_hbm(skin), in_hbm(skout), in_hbm(ahead)],
        specs=[hbm()] * 3,
        scratch=[pltpu.SemaphoreType.DMA((3,))],
        name="stage",
    )
    last, *staged = tie(exchange(last, ROWS), *staged)
    return tuple(call(finish, [((64, 512), f32), ((64, 512), f32)], [last, *staged], name="finish"))


def solution(mesh):
    fine = Mesh(mesh.devices.reshape(2, 4, 2, 2, 8), BLK + ROWS)
    every = BLK + ROWS
    return jax.shard_map(
        on_device,
        mesh=fine,
        in_specs=(
            P(None, every),
            P(None, every),
            P(every, None, None),
            P(every),
            P(every),
            P(every),
            P(None, every),
            P(None, every),
            P(BLK, None, ROWS, None),
        ),
        out_specs=(P(None, every), P(None, every)),
        check_vma=False,
    )
```
